32 devices in a mesh: ctx: 8 (over z, x), fsdp: 4 (over y, core).
Axes of the slice: x: 2, y: 2, z: 4, core: 2. Of those that a mesh axis runs over, the one named last changes fastest.
Arguments:
- tokens: bfloat16 [4, 2048, 768], P('fsdp', 'ctx'), may hold values from -6 to 6
- lengths: int32 [4, 4], P('fsdp'), may hold values from 1 to 1024, 2048 in all within a row
- span_order: int32 [4, 16], P('fsdp'), may hold values from 0 to 15, each once within a row
- w_query: bfloat16 [768, 768], P('fsdp'), may hold values from -0.109375 to 0.109375
- w_key: bfloat16 [768, 768], P('fsdp'), may hold values from -0.109375 to 0.109375
- w_value: bfloat16 [768, 768], P('fsdp'), may hold values from -0.21875 to 0.21875
- w_out: bfloat16 [768, 768], P('fsdp'), may hold values from -1.25 to 1.25
- w_in: bfloat16 [768, 3072], P('fsdp'), may hold values from -0.21875 to 0.21875
- w_ffn_out: bfloat16 [3072, 768], P('fsdp'), may hold values from -0.109375 to 0.109375
- gain_attn: bfloat16 [768], P('fsdp'), may hold values from 0.099609375 to 1.8984375
- gain_ffn: bfloat16 [768], P('fsdp'), may hold values from 0.099609375 to 1.8984375
- rel_table: bfloat16 [32, 12], P('fsdp'), may hold values from -4 to 4
- cotangent: bfloat16 [4, 2048, 768], P('fsdp', 'ctx'), may hold values from -6 to 6
Outputs:
- output: bfloat16 [4, 2048, 768], P('fsdp', 'ctx')
- grad_tokens: bfloat16 [4, 2048, 768], P('fsdp', 'ctx')
- grad_query: float32 [768, 768], P('fsdp')
- grad_key: float32 [768, 768], P('fsdp')
- grad_value: float32 [768, 768], P('fsdp')
- grad_out: float32 [768, 768], P('fsdp')
- grad_in: float32 [768, 3072], P('fsdp')
- grad_ffn_out: float32 [3072, 768], P('fsdp')
- grad_gain_attn: float32 [768], P('fsdp')
- grad_gain_ffn: float32 [768], P('fsdp')
- grad_table: float32 [32, 12], P('fsdp')
The draws below stay inside these ranges and needn't reach their ends.
Inputs may be any that keep to these rules, and one draw needn't show every extreme that they name: Each group's 4 lengths sum to 2048, and the longest is exactly 1024. `span_order`: each row is a permutation of the group's span numbers; slot s lies on ctx device s // 2.
All inputs are finite; a program needn't handle non-finite values.
Results may differ from the reference program's by a relative error of at most 0.02.
Values may be sent and summed in bfloat16 or wider, within the bound.
No kernel may reach another device: no remote copies, remote signals or barrier semaphores. Data moves between devices by JAX's collectives and lax.ppermute only.
A program may use at most 192 MiB of HBM per device.

```python
import math
import jax
import jax.numpy as jnp
import numpy as np
from jax import lax

D = 768
H = 12
DH = 64
FF = 3072
NB = 32
SPAN = 128
SEQS = 4
GROUPS = 4
GROUP_TOK = 2048
SPANS_GRP = 16


def block_levels(own_key, dims, cuts, least, high):
    factor_of, own = 1.0, jax.random.fold_in(own_key, 6)
    for position, blocks in cuts:
        steps = jnp.exp(jax.random.uniform(jax.random.fold_in(own, position), (blocks,), jnp.float32, least / len(cuts), high / len(cuts)))
        factor_of = factor_of * jnp.repeat(steps, dims[position] // blocks).reshape([-1 if axis == position else 1 for axis in range(len(dims))])
    return factor_of


def length_profile(amount, total, limit, lean):
    loads = [(1 << 20) // math.isqrt(rank ** lean) + 1 for rank in range(2, amount + 1)]
    surplus, holding = total - limit - (amount - 1), [1] * (amount - 1)
    while surplus > 0:
        free = [i for i in range(amount - 1) if holding[i] < limit]
        pool, budget = sum([loads[i] for i in free]), surplus
        for i in free:
            more = min(limit - holding[i], max(1, budget * loads[i] // pool), surplus)
            holding[i] = holding[i] + more
            surplus = surplus - more
    return np.array([limit] + holding)


def uneven(own_key, amount, total, reach, skew):
    if amount == 2:
        one = jax.random.randint(own_key, (), max(1, total - reach), min(reach, total - 1) + 1)
        return jnp.stack([one, total - one])
    sizes = jnp.asarray(length_profile(amount, total, reach, skew), jnp.int32)
    twos = (amount - 1) // 2
    source_of, sink = sizes[1:1 + 2 * twos:2], sizes[2:2 + 2 * twos:2]
    margin = jnp.minimum(source_of - 1, reach - sink)
    passed = jax.random.randint(jax.random.fold_in(own_key, 1), (twos,), 0, 1 << 20) % (margin + 1)
    sizes = sizes.at[1:1 + 2 * twos:2].set(source_of - passed).at[2:2 + 2 * twos:2].set(sink + passed)
    return sizes[jax.random.permutation(jax.random.fold_in(own_key, 2), amount)]


def scatter_about(own_key, dims, scale, limit, cuts=(), held_as=jnp.bfloat16):
    level = block_levels(own_key, dims, cuts, -0.22, 0.18) if cuts else 1.0
    array = jax.random.normal(own_key, dims, jnp.float32) * scale * level
    return jnp.minimum(jnp.maximum(array, -limit), limit).astype(held_as)


def setup_inputs(seed: int = 0) -> dict:
    streams_of = jax.random.split(jax.random.key(seed), 14)
    tokens = scatter_about(streams_of[0], (GROUPS, GROUP_TOK, D), 1.0, 6.0, ((0, 4), (1, 8)))
    lengths = jax.vmap(lambda own: uneven(own, SEQS, GROUP_TOK, GROUP_TOK // 2, 2))(jax.random.split(streams_of[1], GROUPS)).reshape((GROUPS, SEQS)).astype(jnp.int32)
    span_order = jax.vmap(lambda own: jax.random.permutation(own, SPANS_GRP))(jax.random.split(streams_of[2], GROUPS)).reshape((GROUPS, SPANS_GRP)).astype(jnp.int32)
    w_query = scatter_about(streams_of[3], (D, D), (4 * D) ** -0.5, 0.109375, ((0, 4),))
    w_key = scatter_about(streams_of[4], (D, D), (4 * D) ** -0.5, 0.109375, ((0, 4),))
    w_value = scatter_about(streams_of[5], (D, D), D ** -0.5, 0.21875, ((0, 4),))
    w_out = scatter_about(streams_of[6], (D, D), (D // 32) ** -0.5, 1.25, ((0, 4),))
    w_in = scatter_about(streams_of[7], (D, FF), D ** -0.5, 0.21875, ((0, 4),))
    w_ffn_out = scatter_about(streams_of[8], (FF, D), FF ** -0.5, 0.109375, ((0, 4),))
    gain_attn = jnp.clip(1.0 + 0.18 * jax.random.normal(streams_of[9], (D,), jnp.float32), 0.099609375, 1.8984375).astype(jnp.bfloat16)
    gain_ffn = jnp.clip(1.0 + 0.18 * jax.random.normal(streams_of[10], (D,), jnp.float32), 0.099609375, 1.8984375).astype(jnp.bfloat16)
    rel_table = scatter_about(streams_of[11], (NB, H), 1.0, 4.0, ((0, 4),))
    cotangent = scatter_about(streams_of[12], (GROUPS, GROUP_TOK, D), 1.0, 6.0, ((0, 4), (1, 8)))
    return {"tokens": tokens, "lengths": lengths, "span_order": span_order, "w_query": w_query, "w_key": w_key, "w_value": w_value, "w_out": w_out, "w_in": w_in, "w_ffn_out": w_ffn_out, "gain_attn": gain_attn, "gain_ffn": gain_ffn, "rel_table": rel_table, "cotangent": cotangent}


@jax.custom_vjp
def low(v):
    return lax.optimization_barrier(v.astype(jnp.bfloat16)).astype(jnp.float32)

@jax.custom_vjp
def low_back(v):
    return v

def low_keep(v):
    return (low(v), None)

def low_pass(kept, grad):
    return (grad,)

def back_keep(v):
    return (v, None)

def back_low(kept, grad):
    return (low(grad),)
low.defvjp(low_keep, low_pass)
low_back.defvjp(back_keep, back_low)
norm_eps = 1e-06
masked_score = -1e+30
highest = lax.Precision.HIGHEST

def matmul(left_op, right_op):
    return jnp.dot(left_op, right_op, precision=highest, preferred_element_type=jnp.float32)

def rms_norm(values, gain_vec):
    inv_rms = lax.rsqrt(lax.optimization_barrier(jnp.mean(values * values, axis=-1, keepdims=True)) + norm_eps)
    return values * inv_rms * gain_vec

def gelu_tanh(values):
    return 0.5 * values * (1.0 + jnp.tanh(0.7978845608028654 * (values + 0.044715 * values * values * values)))

def bucket_of(relative):
    distance = jnp.abs(relative).astype(jnp.int32)
    far_steps = jnp.zeros_like(distance)
    for exponent in range(1, 8):
        far_steps = far_steps + (distance * distance >= 64 * 2 ** exponent).astype(jnp.int32)
    magnitude = jnp.where(distance < 8, distance, 8 + far_steps).astype(jnp.int32)
    return magnitude + jnp.where(relative > 0, 16, 0).astype(jnp.int32)

def token_places(span_order, lengths):
    row_index = jnp.arange(GROUP_TOK, dtype=jnp.int32)
    positions = (jnp.repeat(span_order, SPAN, axis=1) * SPAN + row_index % SPAN).astype(jnp.int32)
    bounds = jnp.cumsum(lengths, axis=1).astype(jnp.int32)
    segments = lax.optimization_barrier(jnp.sum((positions[:, :, None] >= bounds[:, None, :-1]).astype(jnp.int32), axis=2)).astype(jnp.int32)
    return (positions, segments)

def attend(query_rows, query_pos, query_segment_ids, key_rows, value_rows, key_pos, key_seg, bucket_bias_matrix):
    heads_q = query_rows.reshape(query_rows.shape[0], H, DH)
    heads_k = key_rows.reshape(key_rows.shape[0], H, DH)
    heads_v = value_rows.reshape(value_rows.shape[0], H, DH)
    raw_scores = jnp.einsum('qhd,khd->hqk', heads_q, heads_k, precision=highest)
    buckets = bucket_of(key_pos[None, :] - query_pos[:, None])
    position_bias_values = jnp.transpose(bucket_bias_matrix[buckets], (2, 0, 1))
    scores = low_back(raw_scores + position_bias_values)
    inside = (query_segment_ids[:, None] == key_seg[None, :])[None]
    scores = jnp.where(inside, scores, masked_score)
    row_max = lax.optimization_barrier(jnp.max(scores, axis=2, keepdims=True))
    log_total = row_max + jnp.log(lax.optimization_barrier(jnp.sum(jnp.exp(scores - row_max), axis=2, keepdims=True)))
    probabilities = jnp.exp(scores - log_total)
    attended = jnp.einsum('hqk,khd->qhd', low(probabilities), heads_v, precision=highest)
    return attended.reshape(query_rows.shape[0], D)

def group_layer(tokens_f, positions, segments, w_query, w_key, w_value, w_out, w_in, w_ffn_out, gain_attn, gain_ffn, bucket_bias_matrix):
    normed = low(rms_norm(tokens_f, gain_attn))
    query_rows = low(low_back(matmul(normed, w_query)))
    key_rows = low(low_back(matmul(normed, w_key)))
    value_rows = low(low_back(matmul(normed, w_value)))
    block_len = min(512, GROUP_TOK)
    block_count = GROUP_TOK // block_len

    def one_block(inputs):
        block_q, block_pos, block_seg = inputs
        return attend(block_q, block_pos, block_seg, key_rows, value_rows, positions, segments, bucket_bias_matrix)
    attended = lax.map(jax.checkpoint(one_block), (query_rows.reshape(block_count, block_len, D), positions.reshape(block_count, block_len), segments.reshape(block_count, block_len)))
    attn_rounded = low(low_back(attended.reshape(GROUP_TOK, D)))
    residual = tokens_f + low_back(matmul(attn_rounded, w_out))
    normed_ffn = low(rms_norm(residual, gain_ffn))
    up_rows = low_back(matmul(normed_ffn, w_in))
    activated = low(gelu_tanh(up_rows))
    return residual + low_back(matmul(activated, w_ffn_out))

def reference(tokens, lengths, span_order, w_query, w_key, w_value, w_out, w_in, w_ffn_out, gain_attn, gain_ffn, rel_table, cotangent):
    positions, segments = token_places(span_order, lengths)
    params = tuple((weight_arg.astype(jnp.float32) for weight_arg in (w_query, w_key, w_value, w_out, w_in, w_ffn_out, gain_attn, gain_ffn, rel_table)))

    def forward(tokens_f, *weights_f):

        def one_group(inputs):
            group_tokens, group_pos, group_seg = inputs
            return group_layer(group_tokens, group_pos, group_seg, *weights_f)
        return lax.map(jax.checkpoint(one_group), (tokens_f, positions, segments))
    outputs, pull_back = jax.vjp(forward, tokens.astype(jnp.float32), *params)
    gradients = pull_back(cotangent.astype(jnp.float32))
    return (outputs.astype(jnp.bfloat16), gradients[0].astype(jnp.bfloat16), gradients[1], gradients[2], gradients[3], gradients[4], gradients[5], gradients[6], gradients[7], gradients[8], gradients[9])
```

```python
import jax
import jax.numpy as jnp
from jax import lax
from jax.experimental import pallas as pl
from jax.experimental.pallas import tpu as pltpu
from jax.sharding import PartitionSpec as P

D = 768
H = 12
DH = 64
NB = 32
SPAN = 128
PAIRS = H // 2
BIG = 1e30
VMEM_LIMIT = 58 * 2**20
norm_eps = 1e-06


def bucket_of(relative):
    distance = jnp.abs(relative)
    far_steps = jnp.zeros_like(distance)
    for exponent in range(1, 8):
        far_steps = far_steps + (distance * distance >= 64 * 2**exponent).astype(jnp.int32)
    magnitude = jnp.where(distance < 8, distance, 8 + far_steps)
    return magnitude + jnp.where(relative > 0, 16, 0).astype(jnp.int32)


def dot(a, b, ca=1, cb=0):
    return lax.dot_general(a, b, (((ca,), (cb,)), ((), ())), preferred_element_type=jnp.float32)


def diagonal_onehot(offset):
    lane = lax.broadcasted_iota(jnp.int32, (128, 256), 1)
    row = lax.broadcasted_iota(jnp.int32, (128, 256), 0)
    return (bucket_of(offset * SPAN + 127 - lane) == row).astype(jnp.bfloat16)


def fill_inverse(order_ref, inv_ref, spans):
    def put(i, carry):
        inv_ref[order_ref[0, i]] = i
        return carry

    lax.fori_loop(0, spans, put, 0)


def fill_near_bias(table_t, near_ref):
    for index in range(3):
        rows = dot(table_t, diagonal_onehot(index - 1))
        for head in range(H):
            wide = jnp.broadcast_to(rows[head : head + 1, :], (128, 256))
            tile = pltpu.roll(wide, 129, 1, stride=1, stride_axis=0)[:, :128]
            near_ref[index, head // 2, :, (head % 2) * 128 : (head % 2) * 128 + 128] = tile
    near_ref[3] = jnp.zeros_like(near_ref[3])


def key_range(span, b1, b2, b3, total):
    first, last = span * SPAN, span * SPAN + SPAN - 1
    start = jnp.where(first >= b3, b3, jnp.where(first >= b2, b2, jnp.where(first >= b1, b1, 0)))
    end = jnp.where(last < b1, b1, jnp.where(last < b2, b2, jnp.where(last < b3, b3, total)))
    return start // 256, (end + 255) // 256


def key_features(chunk, span, b1, b2, b3):
    lane = lax.broadcasted_iota(jnp.int32, (256, 128), 1)
    pos = lax.broadcasted_iota(jnp.int32, (256, 128), 0) + chunk * 256
    seg = (pos >= b1).astype(jnp.int32) + (pos >= b2).astype(jnp.int32) + (pos >= b3).astype(jnp.int32)
    code = jnp.where(pos < (span - 1) * SPAN, 4, jnp.where(pos >= (span + 2) * SPAN, 5, seg))
    hot = (lane == seg) | (lane == code) | ((lane >= 6) & (lane < 9))
    return jnp.where(hot, 1.0, 0.0).astype(jnp.bfloat16)


def query_features(span, pair, tab_ref, b1, b2, b3, extra=None):
    row = lax.broadcasted_iota(jnp.int32, (128, 256), 0)
    lane = lax.broadcasted_iota(jnp.int32, (128, 256), 1)
    pos = (lane % SPAN) + span * SPAN
    seg = (pos >= b1).astype(jnp.int32) + (pos >= b2).astype(jnp.int32) + (pos >= b3).astype(jnp.int32)
    first = lane < 128
    below = jnp.where(first, tab_ref[NB // 2 - 1, 2 * pair], tab_ref[NB // 2 - 1, 2 * pair + 1])
    above = jnp.where(first, tab_ref[NB - 1, 2 * pair], tab_ref[NB - 1, 2 * pair + 1])
    feat = jnp.where((row < 4) & (row != seg), -BIG, 0.0)
    feat = jnp.where(row == 4, below, jnp.where(row == 5, above, feat))
    if extra is not None:
        high = extra.astype(jnp.bfloat16).astype(jnp.float32)
        rest = extra - high
        mid = rest.astype(jnp.bfloat16).astype(jnp.float32)
        low = rest - mid
        feat = jnp.where(row == 6, high, jnp.where(row == 7, mid, jnp.where(row == 8, low, feat)))
    return feat.astype(jnp.bfloat16)


def block_diagonal(x_t):
    row = lax.broadcasted_iota(jnp.int32, (128, 128), 0)
    zero = jnp.zeros_like(x_t)
    return jnp.concatenate([jnp.where(row < DH, x_t, zero), jnp.where(row >= DH, x_t, zero)], axis=1)


def stacked_heads(x):
    lane = lax.broadcasted_iota(jnp.int32, (128, 128), 1)
    zero = jnp.zeros_like(x)
    return jnp.concatenate([jnp.where(lane < DH, x, zero), jnp.where(lane >= DH, x, zero)], axis=0)


def near_index(delta):
    return jnp.where((delta >= -1) & (delta <= 1), delta + 1, 3)


def fwd_kernel(
    place_ref, order_ref, len_ref, tab_ref, table_t_ref, q_ref, k_ref, v_ref,
    o_ref, ot_ref, lse_ref,
    inv_ref, rhs_ref, near_ref, m_ref, l_ref, acc_ref,
):
    spans, own = k_ref.shape[0], q_ref.shape[0]
    b1 = len_ref[0, 0]
    b2 = b1 + len_ref[0, 1]
    b3 = b2 + len_ref[0, 2]
    fill_inverse(order_ref, inv_ref, spans)
    fill_near_bias(table_t_ref[...], near_ref)

    def one_span(i, carry):
        span = order_ref[0, place_ref[0] * own + i]
        low, high = key_range(span, b1, b2, b3, spans * SPAN)
        for p in range(PAIRS):
            q_t = q_ref[i, :, p * 128 : p * 128 + 128].T
            rhs_ref[p, 0:128, :] = block_diagonal(q_t)
            rhs_ref[p, 128:256, :] = query_features(span, p, tab_ref, b1, b2, b3)
        m_ref[...] = jnp.full_like(m_ref, -BIG)
        l_ref[...] = jnp.zeros_like(l_ref)
        acc_ref[...] = jnp.zeros_like(acc_ref)

        def chunk_body(t, near):
            s0, s1 = inv_ref[2 * t], inv_ref[2 * t + 1]
            feat = key_features(t, span, b1, b2, b3)
            for p in range(PAIRS):
                cols = slice(p * 128, p * 128 + 128)
                kp = jnp.concatenate([k_ref[s0, :, cols], k_ref[s1, :, cols]], axis=0)
                s = dot(jnp.concatenate([kp, feat], axis=1), rhs_ref[p])
                if near:
                    n0, n1 = near_index(2 * t - span), near_index(2 * t + 1 - span)
                    s = s + jnp.concatenate([near_ref[n0, p], near_ref[n1, p]], axis=0)
                old = m_ref[p]
                new = jnp.maximum(old, jnp.max(s, axis=0, keepdims=True))
                scale = jnp.exp(old - new)
                e = jnp.exp(s - new)
                m_ref[p] = new
                l_ref[p] = l_ref[p] * scale + jnp.sum(e, axis=0, keepdims=True)
                vp = jnp.concatenate([v_ref[s0, :, cols], v_ref[s1, :, cols]], axis=0)
                o = dot(vp, e.astype(jnp.bfloat16), 0, 0)
                acc_ref[p, 0:64, :] = acc_ref[p, 0:64, :] * scale[:, 0:128] + o[0:64, 0:128]
                acc_ref[p, 64:128, :] = acc_ref[p, 64:128, :] * scale[:, 128:256] + o[64:128, 128:256]

        def step(t, carry):
            near = (2 * t + 2 >= span) & (2 * t <= span + 1)
            pl.when(near)(lambda: chunk_body(t, True))
            pl.when(jnp.logical_not(near))(lambda: chunk_body(t, False))
            return carry

        lax.fori_loop(low, high, step, 0)
        for p in range(PAIRS):
            total = l_ref[p]
            lse_ref[i, p] = m_ref[p] + jnp.log(total)
            inv = 1.0 / total
            out = jnp.concatenate(
                [acc_ref[p, 0:64, :] * inv[:, 0:128], acc_ref[p, 64:128, :] * inv[:, 128:256]], axis=0
            )
            ot_ref[i, p] = out
            o_ref[i, :, p * 128 : p * 128 + 128] = out.T.astype(jnp.bfloat16)
        return carry

    lax.fori_loop(0, own, one_span, 0)


def bwd_kernel(
    place_ref, order_ref, len_ref, tab_ref, table_t_ref, q_ref, k_ref, v_ref, do_ref, ot_ref, lse_ref,
    dq_ref, dk_ref, dv_ref, dtab_ref,
    inv_ref, rhs_ref, dorhs_ref, qbd_ref, dobd_ref, near_ref, nacc_ref, acc_ref, far_ref,
):
    spans, own = k_ref.shape[0], q_ref.shape[0]
    b1 = len_ref[0, 0]
    b2 = b1 + len_ref[0, 1]
    b3 = b2 + len_ref[0, 2]
    fill_inverse(order_ref, inv_ref, spans)
    fill_near_bias(table_t_ref[...], near_ref)
    nacc_ref[...] = jnp.zeros_like(nacc_ref)
    far_ref[...] = jnp.zeros_like(far_ref)

    def clear(i, carry):
        dk_ref[i] = jnp.zeros_like(dk_ref[i])
        dv_ref[i] = jnp.zeros_like(dv_ref[i])
        return carry

    lax.fori_loop(0, spans, clear, 0)

    def one_span(i, carry):
        span = order_ref[0, place_ref[0] * own + i]
        low, high = key_range(span, b1, b2, b3, spans * SPAN)
        for p in range(PAIRS):
            cols = slice(p * 128, p * 128 + 128)
            qp, dop = q_ref[i, :, cols], do_ref[i, :, cols]
            do_t = dop.T
            prod = do_t.astype(jnp.float32) * ot_ref[i, p]
            delta = jnp.concatenate(
                [jnp.sum(prod[0:64], axis=0, keepdims=True), jnp.sum(prod[64:128], axis=0, keepdims=True)], axis=1
            )
            rhs_ref[p, 0:128, :] = block_diagonal(qp.T)
            rhs_ref[p, 128:256, :] = query_features(span, p, tab_ref, b1, b2, b3, -lse_ref[i, p])
            row = lax.broadcasted_iota(jnp.int32, (128, 256), 0)
            neg = -delta
            h1 = neg.astype(jnp.bfloat16).astype(jnp.float32)
            h2 = (neg - h1).astype(jnp.bfloat16).astype(jnp.float32)
            h3 = neg - h1 - h2
            dfeat = jnp.where(row == 6, h1, jnp.where(row == 7, h2, jnp.where(row == 8, h3, 0.0)))
            dorhs_ref[p, 0:128, :] = block_diagonal(do_t)
            dorhs_ref[p, 128:256, :] = dfeat.astype(jnp.bfloat16)
            qbd_ref[p] = stacked_heads(qp)
            dobd_ref[p] = stacked_heads(dop)
        acc_ref[...] = jnp.zeros_like(acc_ref)

        def chunk_body(t, near):
            s0, s1 = inv_ref[2 * t], inv_ref[2 * t + 1]
            feat = key_features(t, span, b1, b2, b3)
            far_sum = jnp.zeros((8, 256), jnp.float32)
            for p in range(PAIRS):
                cols = slice(p * 128, p * 128 + 128)
                kp = jnp.concatenate([k_ref[s0, :, cols], k_ref[s1, :, cols]], axis=0)
                vp = jnp.concatenate([v_ref[s0, :, cols], v_ref[s1, :, cols]], axis=0)
                kf = jnp.concatenate([kp, feat], axis=1)
                s = dot(kf, rhs_ref[p])
                if near:
                    n0, n1 = near_index(2 * t - span), near_index(2 * t + 1 - span)
                    s = s + jnp.concatenate([near_ref[n0, p], near_ref[n1, p]], axis=0)
                prob = jnp.exp(s)
                dp = dot(jnp.concatenate([vp, feat], axis=1), dorhs_ref[p])
                ds = prob * dp
                if near:
                    nacc_ref[n0, p] += ds[0:128]
                    nacc_ref[n1, p] += ds[128:256]
                dsb = ds.astype(jnp.bfloat16)
                dv = dot(prob.astype(jnp.bfloat16), dobd_ref[p])
                dk = dot(dsb, qbd_ref[p])
                dv_ref[s0, :, cols] += dv[0:128]
                dv_ref[s1, :, cols] += dv[128:256]
                dk_ref[s0, :, cols] += dk[0:128]
                dk_ref[s1, :, cols] += dk[128:256]
                dq = dot(kf, dsb, 0, 0)
                acc_ref[p, 0:64, :] += dq[0:64, 0:128]
                acc_ref[p, 64:128, :] += dq[64:128, 128:256]
                far_ref[p] += dq[128:136, :]

        def step(t, carry):
            near = (2 * t + 2 >= span) & (2 * t <= span + 1)
            pl.when(near)(lambda: chunk_body(t, True))
            pl.when(jnp.logical_not(near))(lambda: chunk_body(t, False))
            return carry

        lax.fori_loop(low, high, step, 0)
        for p in range(PAIRS):
            dq_ref[i, :, p * 128 : p * 128 + 128] = acc_ref[p].T.astype(jnp.bfloat16)
        return carry

    lax.fori_loop(0, own, one_span, 0)

    row16 = lax.broadcasted_iota(jnp.int32, (16, 128), 0)
    lane16 = lax.broadcasted_iota(jnp.int32, (16, 128), 1)
    grad = jnp.zeros((16, 128), jnp.float32)
    for head in range(H):
        half = slice((head % 2) * 128, (head % 2) * 128 + 128)
        sums = jnp.sum(far_ref[head // 2, 4:6, half], axis=1, keepdims=True)
        grad = grad + jnp.where((row16 == head) & (lane16 == NB // 2 - 1), sums[0:1], 0.0)
        grad = grad + jnp.where((row16 == head) & (lane16 == NB - 1), sums[1:2], 0.0)
    rowd = lax.broadcasted_iota(jnp.int32, (16, 256), 0)
    flip_row = lax.broadcasted_iota(jnp.int32, (128, 128), 0)
    flip_lane = lax.broadcasted_iota(jnp.int32, (128, 128), 1)
    flip = (flip_row + flip_lane == 127).astype(jnp.bfloat16)
    for index in range(3):
        sums = jnp.zeros((16, 256), jnp.float32)
        for p in range(PAIRS):
            both = nacc_ref[index, p]
            high = both.astype(jnp.bfloat16)
            rest = (both - high.astype(jnp.float32)).astype(jnp.bfloat16)
            turned = dot(flip, high) + dot(flip, rest)
            for side in range(2):
                tile = turned[:, side * 128 : side * 128 + 128]
                wide = jnp.concatenate([tile, jnp.zeros_like(tile)], axis=1)
                shifted = pltpu.roll(wide, 0, 1, stride=1, stride_axis=0)
                sums = sums + jnp.where(rowd == 2 * p + side, jnp.sum(shifted, axis=0, keepdims=True), 0.0)
        hot = diagonal_onehot(index - 1).astype(jnp.float32)
        grad = grad + lax.dot_general(
            sums, hot, (((1,), (1,)), ((), ())), preferred_element_type=jnp.float32, precision=lax.Precision.HIGHEST
        )
    dtab_ref[...] = grad


def smem():
    return pl.BlockSpec(memory_space=pltpu.SMEM)


def vmem():
    return pl.BlockSpec(memory_space=pltpu.VMEM)


def attend(place, order, lengths, table, table_t, q, k, v):
    own, spans = q.shape[0], k.shape[0]
    return pl.pallas_call(
        fwd_kernel,
        name="attend",
        out_shape=(
            jax.ShapeDtypeStruct((own, SPAN, D), jnp.bfloat16),
            jax.ShapeDtypeStruct((own, PAIRS, 128, 128), jnp.float32),
            jax.ShapeDtypeStruct((own, PAIRS, 1, 256), jnp.float32),
        ),
        in_specs=[smem()] * 4 + [vmem()] * 4,
        out_specs=(vmem(),) * 3,
        scratch_shapes=[
            pltpu.SMEM((spans,), jnp.int32),
            pltpu.VMEM((PAIRS, 256, 256), jnp.bfloat16),
            pltpu.VMEM((4, PAIRS, 128, 256), jnp.float32),
            pltpu.VMEM((PAIRS, 1, 256), jnp.float32),
            pltpu.VMEM((PAIRS, 1, 256), jnp.float32),
            pltpu.VMEM((PAIRS, 128, 128), jnp.float32),
        ],
        compiler_params=pltpu.CompilerParams(vmem_limit_bytes=VMEM_LIMIT),
    )(place, order, lengths, table, table_t, q, k, v)


def attend_back(place, order, lengths, table, table_t, q, k, v, d_out, out_t, lse):
    own, spans = q.shape[0], k.shape[0]
    return pl.pallas_call(
        bwd_kernel,
        name="attend_back",
        out_shape=(
            jax.ShapeDtypeStruct((own, SPAN, D), jnp.bfloat16),
            jax.ShapeDtypeStruct((spans, SPAN, D), jnp.float32),
            jax.ShapeDtypeStruct((spans, SPAN, D), jnp.float32),
            jax.ShapeDtypeStruct((16, 128), jnp.float32),
        ),
        in_specs=[smem()] * 4 + [vmem()] * 7,
        out_specs=(vmem(),) * 4,
        scratch_shapes=[
            pltpu.SMEM((spans,), jnp.int32),
            pltpu.VMEM((PAIRS, 256, 256), jnp.bfloat16),
            pltpu.VMEM((PAIRS, 256, 256), jnp.bfloat16),
            pltpu.VMEM((PAIRS, 256, 128), jnp.bfloat16),
            pltpu.VMEM((PAIRS, 256, 128), jnp.bfloat16),
            pltpu.VMEM((4, PAIRS, 128, 256), jnp.float32),
            pltpu.VMEM((4, PAIRS, 128, 256), jnp.float32),
            pltpu.VMEM((PAIRS, 128, 128), jnp.float32),
            pltpu.VMEM((PAIRS, 8, 256), jnp.float32),
        ],
        compiler_params=pltpu.CompilerParams(vmem_limit_bytes=VMEM_LIMIT),
    )(place, order, lengths, table, table_t, q, k, v, d_out, out_t, lse)


def rms_norm(values, gain_vec):
    inv_rms = lax.rsqrt(jnp.mean(values * values, axis=-1, keepdims=True) + norm_eps)
    return values * inv_rms * gain_vec


def gelu_tanh(values):
    return (
        0.5
        * values
        * (1.0 + jnp.tanh(0.7978845608028654 * (values + 0.044715 * values * values * values)))
    )


def on_device(
    tokens,
    lengths,
    span_order,
    w_query,
    w_key,
    w_value,
    w_out,
    w_in,
    w_ffn_out,
    gain_attn,
    gain_ffn,
    rel_table,
    cotangent,
):
    gathered = (
        lax.all_gather(w_query, "fsdp", axis=0, tiled=True),
        lax.all_gather(w_key, "fsdp", axis=0, tiled=True),
        lax.all_gather(w_value, "fsdp", axis=0, tiled=True),
        lax.all_gather(w_out, "fsdp", axis=0, tiled=True),
        lax.all_gather(w_in, "fsdp", axis=0, tiled=True),
        lax.all_gather(w_ffn_out, "fsdp", axis=0, tiled=True),
        lax.all_gather(gain_attn, "fsdp", axis=0, tiled=True),
        lax.all_gather(gain_ffn, "fsdp", axis=0, tiled=True),
        lax.all_gather(rel_table, "fsdp", axis=0, tiled=True),
    )
    query_w, key_w, value_w, out_w, in_w, ffn_w, attn_gain, ffn_gain, bucket_bias_matrix = gathered
    ctx_count = lax.axis_size("ctx")
    local_rows = tokens.shape[1]
    group_rows = local_rows * ctx_count
    own = local_rows // SPAN
    spans = group_rows // SPAN
    place = lax.axis_index("ctx").astype(jnp.int32).reshape(1)
    table = bucket_bias_matrix.astype(jnp.float32)
    table_t = jnp.pad(bucket_bias_matrix.T, ((0, 16 - H), (0, 128 - NB)))
    inputs_f = tokens[0].astype(jnp.float32)
    normed, norm_attn_back = jax.vjp(rms_norm, inputs_f, attn_gain.astype(jnp.float32))
    normed_b = normed.astype(jnp.bfloat16)
    query_b = jnp.dot(normed_b, query_w, preferred_element_type=jnp.float32).astype(jnp.bfloat16)
    key_b = jnp.dot(normed_b, key_w, preferred_element_type=jnp.float32).astype(jnp.bfloat16)
    value_b = jnp.dot(normed_b, value_w, preferred_element_type=jnp.float32).astype(jnp.bfloat16)
    all_keys, all_values = (
        lax.all_gather(key_b, "ctx", axis=0, tiled=True),
        lax.all_gather(value_b, "ctx", axis=0, tiled=True),
    )
    query_s = query_b.reshape(own, SPAN, D)
    keys_s = all_keys.reshape(spans, SPAN, D)
    values_s = all_values.reshape(spans, SPAN, D)
    attended_s, attended_t, lse = attend(
        place, span_order, lengths, table, table_t, query_s, keys_s, values_s
    )
    attended_b = attended_s.reshape(local_rows, D)
    residual = inputs_f + jnp.dot(attended_b, out_w, preferred_element_type=jnp.float32)
    normed_ffn, norm_ffn_back = jax.vjp(rms_norm, residual, ffn_gain.astype(jnp.float32))
    feedforward_normed_block = normed_ffn.astype(jnp.bfloat16)
    up_rows = jnp.dot(feedforward_normed_block, in_w, preferred_element_type=jnp.float32)
    activated, gelu_back = jax.vjp(gelu_tanh, up_rows)
    activated_b = activated.astype(jnp.bfloat16)
    result = residual + jnp.dot(activated_b, ffn_w, preferred_element_type=jnp.float32)
    grad_b = cotangent[0]
    grad_ffn = jnp.einsum("tf,td->fd", activated_b, grad_b, preferred_element_type=jnp.float32)
    grad_act = jnp.einsum("td,fd->tf", grad_b, ffn_w, preferred_element_type=jnp.float32)
    (grad_up,) = gelu_back(grad_act)
    grad_up_b = grad_up.astype(jnp.bfloat16)
    grad_inw = jnp.einsum(
        "td,tf->df", feedforward_normed_block, grad_up_b, preferred_element_type=jnp.float32
    )
    grad_normed_ffn = jnp.einsum("tf,df->td", grad_up_b, in_w, preferred_element_type=jnp.float32)
    grad_resid_norm, grad_ffn_gain = norm_ffn_back(grad_normed_ffn)
    grad_resid = grad_b.astype(jnp.float32) + grad_resid_norm
    grad_resid_b = grad_resid.astype(jnp.bfloat16)
    grad_outw = jnp.einsum(
        "tc,td->cd", attended_b, grad_resid_b, preferred_element_type=jnp.float32
    )
    grad_att_b = jnp.einsum(
        "td,cd->tc", grad_resid_b, out_w, preferred_element_type=jnp.float32
    ).astype(jnp.bfloat16)
    grad_query, grad_keys, grad_values, grad_table_t = attend_back(
        place,
        span_order,
        lengths,
        table,
        table_t,
        query_s,
        keys_s,
        values_s,
        grad_att_b.reshape(own, SPAN, D),
        attended_t,
        lse,
    )
    grad_table = grad_table_t[:H, :NB].T
    own_keys, own_values = (
        lax.psum_scatter(
            grad_keys.reshape(group_rows, D).astype(jnp.bfloat16),
            "ctx",
            scatter_dimension=0,
            tiled=True,
        ).astype(jnp.float32),
        lax.psum_scatter(
            grad_values.reshape(group_rows, D).astype(jnp.bfloat16),
            "ctx",
            scatter_dimension=0,
            tiled=True,
        ).astype(jnp.float32),
    )
    grad_q_b = grad_query.reshape(local_rows, D).astype(jnp.bfloat16)
    grad_k_b = own_keys.astype(jnp.bfloat16)
    grad_v_b = own_values.astype(jnp.bfloat16)
    query_weight_gradient = jnp.einsum(
        "tc,td->cd", normed_b, grad_q_b, preferred_element_type=jnp.float32
    )
    grad_kw = jnp.einsum("tc,td->cd", normed_b, grad_k_b, preferred_element_type=jnp.float32)
    grad_vw = jnp.einsum("tc,td->cd", normed_b, grad_v_b, preferred_element_type=jnp.float32)
    grad_normed = jnp.einsum("td,cd->tc", grad_q_b, query_w, preferred_element_type=jnp.float32)
    grad_normed = grad_normed + jnp.einsum(
        "td,cd->tc", grad_k_b, key_w, preferred_element_type=jnp.float32
    )
    grad_normed = grad_normed + jnp.einsum(
        "td,cd->tc", grad_v_b, value_w, preferred_element_type=jnp.float32
    )
    grad_input_norm, grad_attn_gain = norm_attn_back(grad_normed)
    grad_input = (grad_resid + grad_input_norm).astype(jnp.bfloat16)
    pieces = (
        lax.psum_scatter(
            query_weight_gradient.astype(jnp.bfloat16), "fsdp", scatter_dimension=0, tiled=True
        ).astype(jnp.float32),
        lax.psum_scatter(
            grad_kw.astype(jnp.bfloat16), "fsdp", scatter_dimension=0, tiled=True
        ).astype(jnp.float32),
        lax.psum_scatter(
            grad_vw.astype(jnp.bfloat16), "fsdp", scatter_dimension=0, tiled=True
        ).astype(jnp.float32),
        lax.psum_scatter(
            grad_outw.astype(jnp.bfloat16), "fsdp", scatter_dimension=0, tiled=True
        ).astype(jnp.float32),
        lax.psum_scatter(
            grad_inw.astype(jnp.bfloat16), "fsdp", scatter_dimension=0, tiled=True
        ).astype(jnp.float32),
        lax.psum_scatter(
            grad_ffn.astype(jnp.bfloat16), "fsdp", scatter_dimension=0, tiled=True
        ).astype(jnp.float32),
        lax.psum_scatter(
            grad_attn_gain.astype(jnp.bfloat16), "fsdp", scatter_dimension=0, tiled=True
        ).astype(jnp.float32),
        lax.psum_scatter(
            grad_ffn_gain.astype(jnp.bfloat16), "fsdp", scatter_dimension=0, tiled=True
        ).astype(jnp.float32),
        lax.psum_scatter(
            grad_table.astype(jnp.bfloat16), "fsdp", scatter_dimension=0, tiled=True
        ).astype(jnp.float32),
    )
    final_grads = (
        lax.psum(pieces[0].astype(jnp.bfloat16), "ctx").astype(jnp.float32),
        lax.psum(pieces[1].astype(jnp.bfloat16), "ctx").astype(jnp.float32),
        lax.psum(pieces[2].astype(jnp.bfloat16), "ctx").astype(jnp.float32),
        lax.psum(pieces[3].astype(jnp.bfloat16), "ctx").astype(jnp.float32),
        lax.psum(pieces[4].astype(jnp.bfloat16), "ctx").astype(jnp.float32),
        lax.psum(pieces[5].astype(jnp.bfloat16), "ctx").astype(jnp.float32),
        lax.psum(pieces[6].astype(jnp.bfloat16), "ctx").astype(jnp.float32),
        lax.psum(pieces[7].astype(jnp.bfloat16), "ctx").astype(jnp.float32),
        lax.psum(pieces[8].astype(jnp.bfloat16), "ctx").astype(jnp.float32),
    )
    return (
        result.astype(jnp.bfloat16)[None],
        grad_input[None],
        final_grads[0],
        final_grads[1],
        final_grads[2],
        final_grads[3],
        final_grads[4],
        final_grads[5],
        final_grads[6],
        final_grads[7],
        final_grads[8],
    )


def solution(mesh):
    in_specs = (
        P("fsdp", "ctx", None),
        P("fsdp", None),
        P("fsdp", None),
        P("fsdp", None),
        P("fsdp", None),
        P("fsdp", None),
        P("fsdp", None),
        P("fsdp", None),
        P("fsdp", None),
        P("fsdp"),
        P("fsdp"),
        P("fsdp", None),
        P("fsdp", "ctx", None),
    )
    out_specs = (
        P("fsdp", "ctx", None),
        P("fsdp", "ctx", None),
        P("fsdp", None),
        P("fsdp", None),
        P("fsdp", None),
        P("fsdp", None),
        P("fsdp", None),
        P("fsdp", None),
        P("fsdp"),
        P("fsdp"),
        P("fsdp", None),
    )
    return jax.shard_map(
        on_device, mesh=mesh, in_specs=in_specs, out_specs=out_specs, check_vma=False
    )
```

```python
import jax
import jax.numpy as jnp
from jax import lax
from jax.experimental import pallas as pl
from jax.experimental.pallas import tpu as pltpu
from jax.sharding import PartitionSpec as P

D = 768
H = 12
DH = 64
NB = 32
SPAN = 128
PAIRS = H // 2
BIG = 1e30
VMEM_LIMIT = 56 * 2**20
EPS = 1e-06
GELU_C = 0.7978845608028654
ANY = pl.ANY


def bucket_of(relative):
    distance = jnp.abs(relative)
    far_steps = jnp.zeros_like(distance)
    for exponent in range(1, 8):
        far_steps = far_steps + (distance * distance >= 64 * 2**exponent).astype(jnp.int32)
    magnitude = jnp.where(distance < 8, distance, 8 + far_steps)
    return magnitude + jnp.where(relative > 0, 16, 0).astype(jnp.int32)


def dot(a, b, ca=1, cb=0):
    return lax.dot_general(a, b, (((ca,), (cb,)), ((), ())), preferred_element_type=jnp.float32)


def diagonal_onehot(offset):
    lane = lax.broadcasted_iota(jnp.int32, (128, 256), 1)
    row = lax.broadcasted_iota(jnp.int32, (128, 256), 0)
    return (bucket_of(offset * SPAN + 127 - lane) == row).astype(jnp.bfloat16)


def fill_inverse(order_ref, inv_ref, spans):
    def put(i, carry):
        inv_ref[order_ref[0, i]] = i
        return carry

    lax.fori_loop(0, spans, put, 0)


def fill_near_bias(table_t, near_ref):
    for index in range(3):
        rows = dot(table_t, diagonal_onehot(index - 1))
        for head in range(H):
            wide = jnp.broadcast_to(rows[head : head + 1, :], (128, 256))
            tile = pltpu.roll(wide, 129, 1, stride=1, stride_axis=0)[:, :128]
            near_ref[index, head // 2, :, (head % 2) * 128 : (head % 2) * 128 + 128] = tile
    near_ref[3] = jnp.zeros_like(near_ref[3])


def key_range(span, b1, b2, b3, total):
    first, last = span * SPAN, span * SPAN + SPAN - 1
    start = jnp.where(first >= b3, b3, jnp.where(first >= b2, b2, jnp.where(first >= b1, b1, 0)))
    end = jnp.where(last < b1, b1, jnp.where(last < b2, b2, jnp.where(last < b3, b3, total)))
    return start // 256, (end + 255) // 256


def key_features(chunk, span, b1, b2, b3):
    lane = lax.broadcasted_iota(jnp.int32, (256, 128), 1)
    pos = lax.broadcasted_iota(jnp.int32, (256, 128), 0) + chunk * 256
    seg = (pos >= b1).astype(jnp.int32) + (pos >= b2).astype(jnp.int32) + (pos >= b3).astype(jnp.int32)
    code = jnp.where(pos < (span - 1) * SPAN, 4, jnp.where(pos >= (span + 2) * SPAN, 5, seg))
    hot = (lane == seg) | (lane == code) | ((lane >= 6) & (lane < 9))
    return jnp.where(hot, 1.0, 0.0).astype(jnp.bfloat16)


def query_features(span, pair, tab_ref, b1, b2, b3, extra=None):
    row = lax.broadcasted_iota(jnp.int32, (128, 256), 0)
    lane = lax.broadcasted_iota(jnp.int32, (128, 256), 1)
    pos = (lane % SPAN) + span * SPAN
    seg = (pos >= b1).astype(jnp.int32) + (pos >= b2).astype(jnp.int32) + (pos >= b3).astype(jnp.int32)
    first = lane < 128
    below = jnp.where(first, tab_ref[NB // 2 - 1, 2 * pair], tab_ref[NB // 2 - 1, 2 * pair + 1])
    above = jnp.where(first, tab_ref[NB - 1, 2 * pair], tab_ref[NB - 1, 2 * pair + 1])
    feat = jnp.where((row < 4) & (row != seg), -BIG, 0.0)
    feat = jnp.where(row == 4, below, jnp.where(row == 5, above, feat))
    if extra is not None:
        high = extra.astype(jnp.bfloat16).astype(jnp.float32)
        rest = extra - high
        mid = rest.astype(jnp.bfloat16).astype(jnp.float32)
        low = rest - mid
        feat = jnp.where(row == 6, high, jnp.where(row == 7, mid, jnp.where(row == 8, low, feat)))
    return feat.astype(jnp.bfloat16)


def block_diagonal(x_t):
    row = lax.broadcasted_iota(jnp.int32, (128, 128), 0)
    zero = jnp.zeros_like(x_t)
    return jnp.concatenate([jnp.where(row < DH, x_t, zero), jnp.where(row >= DH, x_t, zero)], axis=1)


def stacked_heads(x):
    lane = lax.broadcasted_iota(jnp.int32, (128, 128), 1)
    zero = jnp.zeros_like(x)
    return jnp.concatenate([jnp.where(lane < DH, x, zero), jnp.where(lane >= DH, x, zero)], axis=0)


def near_index(delta):
    return jnp.where((delta >= -1) & (delta <= 1), delta + 1, 3)


def smem():
    return pl.BlockSpec(memory_space=pltpu.SMEM)


def vmem():
    return pl.BlockSpec(memory_space=pltpu.VMEM)


def once():
    return pl.BlockSpec(memory_space=pltpu.VMEM, pipeline_mode=pl.Buffered(1))


def by_chunk():
    return pl.BlockSpec((256, D), lambda t: (t, 0))


def hbm():
    return pl.BlockSpec(memory_space=ANY)


def load_pieces(pieces, target_ref, flip, sem):
    copies = []
    rows = target_ref.shape[0] // len(pieces)
    for number, (ref, index, place) in enumerate(pieces):
        start = pl.multiple_of(lax.bitwise_xor(jnp.int32(place), flip) * rows, 16)
        source = ref.at[index, pl.ds(0, rows)]
        copies.append(pltpu.make_async_copy(source, target_ref.at[pl.ds(start, rows)], sem.at[number]))
    for copy in copies:
        copy.start()
    return copies


def expand(refs):
    out, place = [], 0
    for ref in refs:
        for index in range(ref.shape[0]):
            out.append((ref, index, place))
            place += 1
    return out


def forward_kernel(counts, *refs):
    n_x, n_w = counts
    ids_ref, order_ref, len_ref, tab_ref, table_t_ref, gain_ref = refs[:6]
    x_refs, w_refs = refs[6 : 6 + n_x], refs[6 + n_x : 6 + n_x + n_w]
    (
        nf_ref, res_ref, o_ref, ot_ref, lse_ref, q_ref, k_ref, v_ref, xn_ref,
        inv_ref, x_ref, w_ref, rhs_ref, near_ref, s_ref, m_ref, l_ref, acc_ref, sem_x, sem_w,
    ) = refs[6 + n_x + n_w :]
    spans, own = order_ref.shape[1], q_ref.shape[0] // SPAN
    b1 = len_ref[0, 0]
    b2 = b1 + len_ref[0, 1]
    b3 = b2 + len_ref[0, 2]
    copies = load_pieces(expand(x_refs), x_ref, jnp.int32(0), sem_x)
    copies += load_pieces(expand(w_refs), w_ref, ids_ref[2], sem_w)
    fill_inverse(order_ref, inv_ref, spans)
    fill_near_bias(table_t_ref[...], near_ref)
    for copy in copies:
        copy.wait()
    own_rows = own * SPAN
    gain = gain_ref[0:1, :]

    def normed(x):
        x = x.astype(jnp.float32)
        return (x * lax.rsqrt(jnp.mean(x * x, axis=1, keepdims=True) + EPS) * gain).astype(jnp.bfloat16)

    my_spans = [order_ref[0, ids_ref[0] * own + i] for i in range(own)]
    my_ranges = [key_range(span, b1, b2, b3, spans * SPAN) for span in my_spans]

    def project(t, carry):
        needed = jnp.bool_(False)
        for low, high in my_ranges:
            needed = needed | ((t >= low) & (t < high))
        rows = pl.ds(pl.multiple_of(t * 256, 256), 256)

        def fill():
            parts = []
            for half in range(2):
                slot = inv_ref[2 * t + half]
                piece = lax.bitwise_xor(slot // own, ids_ref[1])
                start = pl.multiple_of(piece * own_rows + (slot % own) * SPAN, SPAN)
                parts.append(x_ref[pl.ds(start, SPAN), :])
            xn = normed(jnp.concatenate(parts, axis=0))
            xn_ref[rows, :] = xn
            k_ref[rows, :] = dot(xn, w_ref[:, D : 2 * D]).astype(jnp.bfloat16)
            v_ref[rows, :] = dot(xn, w_ref[:, 2 * D : 3 * D]).astype(jnp.bfloat16)

        def skip():
            xn_ref[rows, :] = jnp.zeros((256, D), jnp.bfloat16)

        pl.when(needed)(fill)
        pl.when(jnp.logical_not(needed))(skip)
        return carry

    lax.fori_loop(0, spans // 2, project, 0)
    mine = pl.multiple_of(lax.bitwise_xor(ids_ref[0], ids_ref[1]) * own_rows, SPAN)
    x_own = x_ref[pl.ds(mine, own_rows), :]
    q_ref[...] = dot(normed(x_own), w_ref[:, 0:D]).astype(jnp.bfloat16)

    def one_span(i, carry):
        span = order_ref[0, ids_ref[0] * own + i]
        low, high = key_range(span, b1, b2, b3, spans * SPAN)
        my_rows = pl.ds(pl.multiple_of(i * SPAN, SPAN), SPAN)
        for p in range(PAIRS):
            q_t = q_ref[my_rows, p * 128 : p * 128 + 128].T
            rhs_ref[p, 0:128, :] = block_diagonal(q_t)
            rhs_ref[p, 128:256, :] = query_features(span, p, tab_ref, b1, b2, b3)
        m_ref[...] = jnp.full_like(m_ref, -BIG)
        l_ref[...] = jnp.zeros_like(l_ref)
        acc_ref[...] = jnp.zeros_like(acc_ref)

        def chunk_body(t, near):
            rows = pl.ds(pl.multiple_of(t * 256, 256), 256)
            feat = key_features(t, span, b1, b2, b3)
            scales, tops = [], []
            for p in range(PAIRS):
                kp = k_ref[rows, p * 128 : p * 128 + 128]
                s = dot(jnp.concatenate([kp, feat], axis=1), rhs_ref[p])
                if near:
                    n0, n1 = near_index(2 * t - span), near_index(2 * t + 1 - span)
                    s = s + jnp.concatenate([near_ref[n0, p], near_ref[n1, p]], axis=0)
                s_ref[p] = s
                old = m_ref[p]
                new = jnp.maximum(old, jnp.max(s, axis=0, keepdims=True))
                m_ref[p] = new
                scales.append(jnp.exp(old - new))
                tops.append(new)
            for p in range(PAIRS):
                scale = scales[p]
                e = jnp.exp(s_ref[p] - tops[p])
                l_ref[p] = l_ref[p] * scale + jnp.sum(e, axis=0, keepdims=True)
                vp = v_ref[rows, p * 128 : p * 128 + 128]
                o = dot(vp, e.astype(jnp.bfloat16), 0, 0)
                acc_ref[p, 0:64, :] = acc_ref[p, 0:64, :] * scale[:, 0:128] + o[0:64, 0:128]
                acc_ref[p, 64:128, :] = acc_ref[p, 64:128, :] * scale[:, 128:256] + o[64:128, 128:256]

        def step(t, carry):
            near = (2 * t + 2 >= span) & (2 * t <= span + 1)
            pl.when(near)(lambda: chunk_body(t, True))
            pl.when(jnp.logical_not(near))(lambda: chunk_body(t, False))
            return carry

        lax.fori_loop(low, high, step, 0)
        for p in range(PAIRS):
            total = l_ref[p]
            lse_ref[i, p] = m_ref[p] + jnp.log(total)
            inv = 1.0 / total
            out = jnp.concatenate(
                [acc_ref[p, 0:64, :] * inv[:, 0:128], acc_ref[p, 64:128, :] * inv[:, 128:256]], axis=0
            )
            ot_ref[i, p] = out
            o_ref[my_rows, p * 128 : p * 128 + 128] = out.T.astype(jnp.bfloat16)
        return carry

    lax.fori_loop(0, own, one_span, 0)
    res = x_own.astype(jnp.float32) + dot(o_ref[...], w_ref[:, 3 * D : 4 * D])
    res_ref[...] = res
    inv_rms = lax.rsqrt(jnp.mean(res * res, axis=1, keepdims=True) + EPS)
    nf_ref[...] = (res * inv_rms * gain_ref[1:2, :]).astype(jnp.bfloat16)


def forward(ids, order, lengths, table, table_t, gains, xs, ws, local_rows):
    spans, own = order.shape[1], local_rows // SPAN
    rows = spans * SPAN
    n_x, n_w = sum(x.shape[0] for x in xs), sum(w.shape[0] for w in ws)
    bf, f32 = jnp.bfloat16, jnp.float32
    return pl.pallas_call(
        lambda *refs: forward_kernel((len(xs), len(ws)), *refs),
        name="forward",
        out_shape=(
            jax.ShapeDtypeStruct((local_rows, D), bf),
            jax.ShapeDtypeStruct((local_rows, D), f32),
            jax.ShapeDtypeStruct((local_rows, D), bf),
            jax.ShapeDtypeStruct((own, PAIRS, 128, 128), f32),
            jax.ShapeDtypeStruct((own, PAIRS, 1, 256), f32),
            jax.ShapeDtypeStruct((local_rows, D), bf),
            jax.ShapeDtypeStruct((rows, D), bf),
            jax.ShapeDtypeStruct((rows, D), bf),
            jax.ShapeDtypeStruct((rows, D), bf),
        ),
        in_specs=[smem()] * 4 + [vmem()] * 2 + [hbm()] * (len(xs) + len(ws)),
        out_specs=(vmem(),) * 9,
        scratch_shapes=[
            pltpu.SMEM((spans,), jnp.int32),
            pltpu.VMEM((rows, D), bf),
            pltpu.VMEM((D, 4 * D), bf),
            pltpu.VMEM((PAIRS, 256, 256), bf),
            pltpu.VMEM((4, PAIRS, 128, 256), f32),
            pltpu.VMEM((PAIRS, 256, 256), f32),
            pltpu.VMEM((PAIRS, 1, 256), f32),
            pltpu.VMEM((PAIRS, 1, 256), f32),
            pltpu.VMEM((PAIRS, 128, 128), f32),
            pltpu.SemaphoreType.DMA((n_x,)),
            pltpu.SemaphoreType.DMA((n_w,)),
        ],
        compiler_params=pltpu.CompilerParams(vmem_limit_bytes=VMEM_LIMIT),
    )(ids, order, lengths, table, table_t, gains, *xs, *ws)


def ffn_kernel(counts, *refs):
    n_t, n_w = counts
    ids_ref = refs[0]
    nf_refs, cot_refs = refs[1 : 1 + n_t], refs[1 + n_t : 1 + 2 * n_t]
    win_refs = refs[1 + 2 * n_t : 1 + 2 * n_t + n_w]
    wffn_ref, act_ref, dup_ref, dn_ref, w_ref, sem_w = refs[1 + 2 * n_t + n_w :]
    copies = load_pieces(expand(win_refs), w_ref, ids_ref[2], sem_w)
    for copy in copies:
        copy.wait()
    start = 0
    for nf_ref, cot_ref in zip(nf_refs, cot_refs):
        for piece in range(nf_ref.shape[0]):
            rows = slice(start, start + nf_ref.shape[1])
            up = dot(nf_ref[piece], w_ref[...])
            square = up * up
            th = jnp.tanh(GELU_C * (up + 0.044715 * square * up))
            half = 0.5 * (1.0 + th)
            act_ref[rows, :] = (up * half).astype(jnp.bfloat16)
            slope = half + 0.5 * up * (1.0 - th * th) * (GELU_C * (1.0 + 3 * 0.044715 * square))
            d_up = (dot(cot_ref[piece], wffn_ref[...], 1, 1) * slope).astype(jnp.bfloat16)
            dup_ref[rows, :] = d_up
            dn_ref[rows, :] = dot(d_up, w_ref[...], 1, 1).astype(jnp.bfloat16)
            start += nf_ref.shape[1]


def ffn(ids, nfs, cots, wins, wffn):
    rows = sum(x.shape[0] * x.shape[1] for x in nfs)
    width = wffn.shape[0]
    n_w = sum(w.shape[0] for w in wins)
    bf = jnp.bfloat16
    return pl.pallas_call(
        lambda *refs: ffn_kernel((len(nfs), len(wins)), *refs),
        name="ffn",
        out_shape=(
            jax.ShapeDtypeStruct((rows, width), bf),
            jax.ShapeDtypeStruct((rows, width), bf),
            jax.ShapeDtypeStruct((rows, D), bf),
        ),
        in_specs=[smem()] + [vmem()] * (2 * len(nfs)) + [hbm()] * len(wins) + [vmem()],
        out_specs=(vmem(),) * 3,
        scratch_shapes=[pltpu.VMEM((D, width), bf), pltpu.SemaphoreType.DMA((n_w,))],
        compiler_params=pltpu.CompilerParams(vmem_limit_bytes=VMEM_LIMIT),
    )(ids, *nfs, *cots, *wins, wffn)


def backward_kernel(counts, *refs):
    n_x, n_w = counts
    (
        ids_ref, order_ref, len_ref, tab_ref, table_t_ref, gain_ref,
        dnf_ref, res_ref, cot_ref, o_ref, ot_ref, lse_ref, q_ref, k_ref, v_ref,
    ) = refs[:15]
    x_refs, w_refs = refs[15 : 15 + n_x], refs[15 + n_x : 15 + n_x + n_w]
    (
        dres_ref, dlow_ref, dq_ref, dk_ref, dv_ref, dn_ref, dn_own_ref, dgain_ref, dtab_ref,
        inv_ref, x_ref, w_ref, do_ref, rhs_ref, dorhs_ref, qbd_ref, dobd_ref, near_ref, nacc_ref, acc_ref, far_ref,
        dkacc_ref, dvacc_ref, sem_x, sem_w,
    ) = refs[15 + n_x + n_w :]
    spans, own = order_ref.shape[1], q_ref.shape[0] // SPAN
    own_rows = own * SPAN
    b1 = len_ref[0, 0]
    b2 = b1 + len_ref[0, 1]
    b3 = b2 + len_ref[0, 2]
    t = pl.program_id(0)

    @pl.when(t == 0)
    def begin():
        copies_x = load_pieces(expand(x_refs), x_ref, jnp.int32(0), sem_x)
        copies_w = load_pieces(expand(w_refs), w_ref, ids_ref[2], sem_w)
        fill_inverse(order_ref, inv_ref, spans)
        fill_near_bias(table_t_ref[...], near_ref)
        nacc_ref[...] = jnp.zeros_like(nacc_ref)
        far_ref[...] = jnp.zeros_like(far_ref)

        res, dnf = res_ref[...], dnf_ref[...]
        inv_rms = lax.rsqrt(jnp.mean(res * res, axis=1, keepdims=True) + EPS)
        dgain_ref[...] = jnp.zeros_like(dgain_ref)
        dgain_ref[1:2, :] = jnp.sum(dnf * res * inv_rms, axis=0, keepdims=True)
        scaled = dnf * gain_ref[1:2, :]
        inner = jnp.mean(scaled * res, axis=1, keepdims=True)
        dres = cot_ref[...].astype(jnp.float32) + inv_rms * scaled - res * (inv_rms * inv_rms * inv_rms * inner)
        dres_ref[...] = dres
        dlow = dres.astype(jnp.bfloat16)
        dlow_ref[...] = dlow
        for copy in copies_w:
            copy.wait()
        do_ref[...] = dot(dlow, w_ref[:, 3 * D : 4 * D], 1, 1).astype(jnp.bfloat16)

        def prepare(i, carry):
            span = order_ref[0, ids_ref[0] * own + i]
            my_rows = pl.ds(pl.multiple_of(i * SPAN, SPAN), SPAN)
            for p in range(PAIRS):
                cols = slice(p * 128, p * 128 + 128)
                qp, dop = q_ref[my_rows, cols], do_ref[my_rows, cols]
                do_t = dop.T
                prod = do_t.astype(jnp.float32) * ot_ref[i, p]
                neg = -jnp.concatenate(
                    [jnp.sum(prod[0:64], axis=0, keepdims=True), jnp.sum(prod[64:128], axis=0, keepdims=True)], axis=1
                )
                rhs_ref[i, p, 0:128, :] = block_diagonal(qp.T)
                rhs_ref[i, p, 128:256, :] = query_features(span, p, tab_ref, b1, b2, b3, -lse_ref[i, p])
                row = lax.broadcasted_iota(jnp.int32, (128, 256), 0)
                h1 = neg.astype(jnp.bfloat16).astype(jnp.float32)
                h2 = (neg - h1).astype(jnp.bfloat16).astype(jnp.float32)
                h3 = neg - h1 - h2
                dfeat = jnp.where(row == 6, h1, jnp.where(row == 7, h2, jnp.where(row == 8, h3, 0.0)))
                dorhs_ref[i, p, 0:128, :] = block_diagonal(do_t)
                dorhs_ref[i, p, 128:256, :] = dfeat.astype(jnp.bfloat16)
                qbd_ref[i, p] = stacked_heads(qp)
                dobd_ref[i, p] = stacked_heads(dop)
            return carry

        lax.fori_loop(0, own, prepare, 0)
        acc_ref[...] = jnp.zeros_like(acc_ref)
        for copy in copies_x:
            copy.wait()


    def unit(x):
        x = x.astype(jnp.float32)
        return x * lax.rsqrt(jnp.mean(x * x, axis=1, keepdims=True) + EPS)

    dkacc_ref[...] = jnp.zeros_like(dkacc_ref)
    dvacc_ref[...] = jnp.zeros_like(dvacc_ref)

    def span_body(i, span, near):
        feat = key_features(t, span, b1, b2, b3)
        for p in range(PAIRS):
            cols = slice(p * 128, p * 128 + 128)
            kf = jnp.concatenate([k_ref[:, cols], feat], axis=1)
            s = dot(kf, rhs_ref[i, p])
            if near:
                n0, n1 = near_index(2 * t - span), near_index(2 * t + 1 - span)
                s = s + jnp.concatenate([near_ref[n0, p], near_ref[n1, p]], axis=0)
            prob = jnp.exp(s)
            ds = prob * dot(jnp.concatenate([v_ref[:, cols], feat], axis=1), dorhs_ref[i, p])
            if near:
                nacc_ref[n0, p] += ds[0:128]
                nacc_ref[n1, p] += ds[128:256]
            dsb = ds.astype(jnp.bfloat16)
            dvacc_ref[:, cols] += dot(prob.astype(jnp.bfloat16), dobd_ref[i, p])
            dkacc_ref[:, cols] += dot(dsb, qbd_ref[i, p])
            dq = dot(kf, dsb, 0, 0)
            acc_ref[i, p, 0:64, :] += dq[0:64, 0:128]
            acc_ref[i, p, 64:128, :] += dq[64:128, 128:256]
            far_ref[p] += dq[128:136, :]

    def one_span(i, used):
        span = order_ref[0, ids_ref[0] * own + i]
        low, high = key_range(span, b1, b2, b3, spans * SPAN)
        needed = (t >= low) & (t < high)
        near = (2 * t + 2 >= span) & (2 * t <= span + 1)
        pl.when(needed & near)(lambda: span_body(i, span, True))
        pl.when(needed & jnp.logical_not(near))(lambda: span_body(i, span, False))
        return used + needed.astype(jnp.int32)

    used = lax.fori_loop(0, own, one_span, jnp.int32(0))
    places = []
    for half in range(2):
        slot = inv_ref[2 * t + half]
        piece = lax.bitwise_xor(slot // own, ids_ref[1])
        places.append(pl.ds(pl.multiple_of(piece * own_rows + (slot % own) * SPAN, SPAN), SPAN))

    def fill():
        dkb, dvb = dkacc_ref[...].astype(jnp.bfloat16), dvacc_ref[...].astype(jnp.bfloat16)
        dk_ref[...] = dkb
        dv_ref[...] = dvb
        part = dot(dkb, w_ref[:, D : 2 * D], 1, 1) + dot(dvb, w_ref[:, 2 * D : 3 * D], 1, 1)
        x = jnp.concatenate([x_ref[places[0], :], x_ref[places[1], :]], axis=0)
        dgain_ref[0:1, :] += jnp.sum(part * unit(x), axis=0, keepdims=True)
        part = part.astype(jnp.bfloat16)
        dn_ref[places[0], :] = part[0:128]
        dn_ref[places[1], :] = part[128:256]

    def skip():
        zero = jnp.zeros((256, D), jnp.bfloat16)
        dk_ref[...] = zero
        dv_ref[...] = zero
        dn_ref[places[0], :] = zero[0:128]
        dn_ref[places[1], :] = zero[0:128]

    pl.when(used > 0)(fill)
    pl.when(used == 0)(skip)


    @pl.when(t == spans // 2 - 1)
    def finish():
        for i in range(own):
            for p in range(PAIRS):
                dq_ref[i * SPAN : (i + 1) * SPAN, p * 128 : p * 128 + 128] = acc_ref[i, p].T.astype(jnp.bfloat16)
        mine = pl.multiple_of(lax.bitwise_xor(ids_ref[0], ids_ref[1]) * own_rows, SPAN)
        own_part = dot(dq_ref[...], w_ref[:, 0:D], 1, 1)
        dn_own_ref[...] = own_part
        dgain_ref[0:1, :] += jnp.sum(own_part * unit(x_ref[pl.ds(mine, own_rows), :]), axis=0, keepdims=True)

        row16 = lax.broadcasted_iota(jnp.int32, (16, 128), 0)
        lane16 = lax.broadcasted_iota(jnp.int32, (16, 128), 1)
        grad = jnp.zeros((16, 128), jnp.float32)
        for head in range(H):
            half = slice((head % 2) * 128, (head % 2) * 128 + 128)
            sums = jnp.sum(far_ref[head // 2, 4:6, half], axis=1, keepdims=True)
            grad = grad + jnp.where((row16 == head) & (lane16 == NB // 2 - 1), sums[0:1], 0.0)
            grad = grad + jnp.where((row16 == head) & (lane16 == NB - 1), sums[1:2], 0.0)
        rowd = lax.broadcasted_iota(jnp.int32, (16, 256), 0)
        flip_row = lax.broadcasted_iota(jnp.int32, (128, 128), 0)
        flip_lane = lax.broadcasted_iota(jnp.int32, (128, 128), 1)
        flip = (flip_row + flip_lane == 127).astype(jnp.bfloat16)
        for index in range(3):
            sums = jnp.zeros((16, 256), jnp.float32)
            for p in range(PAIRS):
                both = nacc_ref[index, p]
                high = both.astype(jnp.bfloat16)
                rest = (both - high.astype(jnp.float32)).astype(jnp.bfloat16)
                turned = dot(flip, high) + dot(flip, rest)
                for side in range(2):
                    tile = turned[:, side * 128 : side * 128 + 128]
                    wide = jnp.concatenate([tile, jnp.zeros_like(tile)], axis=1)
                    shifted = pltpu.roll(wide, 0, 1, stride=1, stride_axis=0)
                    sums = sums + jnp.where(rowd == 2 * p + side, jnp.sum(shifted, axis=0, keepdims=True), 0.0)
            hot = diagonal_onehot(index - 1).astype(jnp.float32)
            grad = grad + lax.dot_general(
                sums, hot, (((1,), (1,)), ((), ())), preferred_element_type=jnp.float32, precision=lax.Precision.HIGHEST
            )
        dtab_ref[...] = grad


def backward(ids, order, lengths, table, table_t, gains, dnf, res, cot, o, ot, lse, q, k, v, xs, ws):
    spans, local_rows = order.shape[1], q.shape[0]
    rows, own = spans * SPAN, local_rows // SPAN
    n_x, n_w = sum(x.shape[0] for x in xs), sum(w.shape[0] for w in ws)
    bf, f32 = jnp.bfloat16, jnp.float32
    return pl.pallas_call(
        lambda *refs: backward_kernel((len(xs), len(ws)), *refs),
        name="backward",
        grid=(spans // 2,),
        out_shape=(
            jax.ShapeDtypeStruct((local_rows, D), f32),
            jax.ShapeDtypeStruct((local_rows, D), bf),
            jax.ShapeDtypeStruct((local_rows, D), bf),
            jax.ShapeDtypeStruct((rows, D), bf),
            jax.ShapeDtypeStruct((rows, D), bf),
            jax.ShapeDtypeStruct((rows, D), bf),
            jax.ShapeDtypeStruct((local_rows, D), f32),
            jax.ShapeDtypeStruct((8, D), f32),
            jax.ShapeDtypeStruct((16, 128), f32),
        ),
        in_specs=[smem()] * 4 + [once()] * 9 + [by_chunk()] * 2 + [hbm()] * (len(xs) + len(ws)),
        out_specs=(once(),) * 3 + (by_chunk(),) * 2 + (once(),) * 4,
        scratch_shapes=[
            pltpu.SMEM((spans,), jnp.int32),
            pltpu.VMEM((rows, D), bf),
            pltpu.VMEM((D, 4 * D), bf),
            pltpu.VMEM((local_rows, D), bf),
            pltpu.VMEM((own, PAIRS, 256, 256), bf),
            pltpu.VMEM((own, PAIRS, 256, 256), bf),
            pltpu.VMEM((own, PAIRS, 256, 128), bf),
            pltpu.VMEM((own, PAIRS, 256, 128), bf),
            pltpu.VMEM((4, PAIRS, 128, 256), f32),
            pltpu.VMEM((4, PAIRS, 128, 256), f32),
            pltpu.VMEM((own, PAIRS, 128, 128), f32),
            pltpu.VMEM((PAIRS, 8, 256), f32),
            pltpu.VMEM((256, D), f32),
            pltpu.VMEM((256, D), f32),
            pltpu.SemaphoreType.DMA((n_x,)),
            pltpu.SemaphoreType.DMA((n_w,)),
        ],
        compiler_params=pltpu.CompilerParams(vmem_limit_bytes=VMEM_LIMIT),
    )(ids, order, lengths, table, table_t, gains, dnf, res, cot, o, ot, lse, q, k, v, *xs, *ws)


def swap(x, axis, bit):
    count = lax.axis_size(axis)
    return lax.ppermute(x, axis, [(i, i ^ bit) for i in range(count)])


def block(x, index, count, dim=0):
    size = x.shape[dim] // count
    return lax.dynamic_slice_in_dim(x, index * size, size, dim)


def after(x, *others):
    return lax.optimization_barrier((x,) + others)[0]


def gather_four(x):
    across = swap(x, "fsdp", 2)
    return [x, swap(x, "fsdp", 1), across, swap(across, "fsdp", 1)]


def scatter_four(pieces):
    first, third = swap(pieces[1], "fsdp", 1), swap(pieces[3], "fsdp", 1)
    far = add(pieces[2], third)
    return pieces[0], first, swap(far, "fsdp", 2)


def exchange_four(pieces):
    side, corner = swap(pieces[1], "fsdp", 1), swap(pieces[3], "fsdp", 1)
    return [pieces[0], side, swap(pieces[2], "fsdp", 2), swap(corner, "fsdp", 2)]


def add(*terms):
    total = terms[0].astype(jnp.float32)
    for term in terms[1:]:
        total = total + term.astype(jnp.float32)
    return total.astype(jnp.bfloat16)


def on_device(
    tokens,
    lengths,
    span_order,
    w_query,
    w_key,
    w_value,
    w_out,
    w_in,
    w_ffn_out,
    gain_attn,
    gain_ffn,
    rel_table,
    cotangent,
):
    n_ctx, n_fsdp = lax.axis_size("ctx"), lax.axis_size("fsdp")
    fast = n_ctx == 8 and n_fsdp == 4
    place = lax.axis_index("ctx").astype(jnp.int32)
    shard = lax.axis_index("fsdp").astype(jnp.int32)
    local_rows = tokens.shape[1]
    own_rows = w_query.shape[0]
    bf, f32 = jnp.bfloat16, jnp.float32
    x, cot = tokens[0], cotangent[0]
    table_size = rel_table.size
    small = jnp.concatenate([gain_attn, gain_ffn, rel_table.reshape(-1)])
    small = jnp.pad(small[None], ((0, 15), (0, 4 * D - small.shape[0])))
    weights = jnp.concatenate([jnp.concatenate([w_query, w_key, w_value, w_out], axis=1), small], axis=0)
    width = w_ffn_out.shape[0]

    if fast:
        zero = jnp.int32(0)
        ids = jnp.stack([place, place, shard])
        x1, x2, x4 = swap(x, "ctx", 1), swap(x, "ctx", 2), swap(x, "ctx", 4)
        x3, x6 = swap(x2, "ctx", 1), swap(x4, "ctx", 2)
        x5, x7 = swap(x4, "ctx", 1), swap(x6, "ctx", 1)
        xs = [p[None] for p in (x, x1, x2, x3, x4, x5, x6, x7)]
        w_pieces = gather_four(weights)
        ws = [p[None] for p in w_pieces]
        order = [shard ^ r for r in range(4)]
        smalls = jnp.stack([p[own_rows] for p in w_pieces])
        smalls = jnp.stack([lax.dynamic_index_in_dim(smalls, order[i], 0, False) for i in range(4)])
        columns = after(w_in, w_pieces[2])
        wins = exchange_four([block(columns, order[r], 4, 1) for r in range(4)])
        cots = [p[None] for p in gather_four(after(cot, wins[3]))]
        wins = [p[None] for p in wins]
    else:
        ids = jnp.stack([place, jnp.int32(0), jnp.int32(0)])
        xs = [lax.all_gather(x, "ctx", axis=0)]
        ws = [lax.all_gather(weights, "fsdp", axis=0)]
        smalls = ws[0][:, own_rows]
        parts = jnp.stack([w_in[:, i * width : (i + 1) * width] for i in range(n_fsdp)])
        wins = [lax.all_to_all(parts, "fsdp", 0, 0)]
        cots = [lax.all_gather(cot, "fsdp", axis=0)]

    gains = jnp.stack([smalls[:, :own_rows].reshape(D), smalls[:, own_rows : 2 * own_rows].reshape(D)]).astype(f32)
    table_bf = smalls[:, 2 * own_rows : 2 * own_rows + table_size].reshape(NB, H)
    table = table_bf.astype(f32)
    table_t = jnp.pad(table_bf.T, ((0, 16 - H), (0, 128 - NB)))

    nf, res, o, ot, lse, q, k, v, xn = forward(
        ids, span_order, lengths, table, table_t, gains, xs, ws, local_rows
    )

    if fast:
        nfs = [p[None] for p in gather_four(nf)]
    else:
        nfs = [lax.all_gather(nf, "fsdp", axis=0)]
    act, dup, dn_part = ffn(ids, nfs, cots, wins, w_ffn_out)
    dn_part = dn_part.reshape(n_fsdp, local_rows, D)
    if fast:
        a, b, c = scatter_four([dn_part[r] for r in range(4)])
        dnf = a.astype(f32) + b.astype(f32) + c.astype(f32)
    else:
        dnf = lax.psum_scatter(dn_part, "fsdp", scatter_dimension=0).astype(f32)

    nf_all = jnp.concatenate([p.reshape(-1, D) for p in nfs])
    cot_all = jnp.concatenate([p.reshape(-1, D) for p in cots])
    out_part = dot(act, w_ffn_out).astype(bf).reshape(n_fsdp, local_rows, D)
    grad_ffn_out = dot(act, cot_all, 0, 0).astype(bf)
    grad_in = dot(nf_all, dup, 0, 0).astype(bf).reshape(n_fsdp, own_rows, width)
    if fast:
        a, b, c = scatter_four([out_part[r] for r in range(4)])
        output = (res + a.astype(f32) + b.astype(f32) + c.astype(f32)).astype(bf)
        got = exchange_four([lax.dynamic_index_in_dim(grad_in, order[r], 0, False) for r in range(4)])
        got = jnp.stack(got)
        grad_in = jnp.concatenate([lax.dynamic_index_in_dim(got, shard ^ i, 0, False) for i in range(4)], axis=1)
    else:
        output = (res + lax.psum_scatter(out_part, "fsdp", scatter_dimension=0).astype(f32)).astype(bf)
        got = lax.all_to_all(grad_in, "fsdp", 0, 0)
        grad_in = jnp.transpose(got, (1, 0, 2)).reshape(own_rows, n_fsdp * width)
    grad_ffn_out = lax.psum(grad_ffn_out, "ctx")
    grad_in = lax.psum(grad_in, "ctx")

    dres, dlow, dq, dk, dv, dn, dn_own, dgain, dtab = backward(
        ids, span_order, lengths, table, table_t, gains, dnf, res, cot, o, ot, lse, q, k, v, xs, ws
    )
    dn = dn.reshape(n_ctx, local_rows, D)
    if fast:
        got7, got5, got3, got1 = (swap(dn[r], "ctx", 1) for r in (7, 5, 3, 1))
        s6, s4, s2, s0 = add(dn[6], got7), add(dn[4], got5), add(dn[2], got3), add(dn[0], got1)
        t4 = add(s4, swap(s6, "ctx", 2))
        t2 = swap(s2, "ctx", 2)
        d_normed = dn_own + s0.astype(f32) + t2.astype(f32) + swap(t4, "ctx", 4).astype(f32)
    else:
        d_normed = dn_own + lax.psum_scatter(dn, "ctx", scatter_dimension=0).astype(f32)

    xf = x.astype(f32)
    inv_rms = lax.rsqrt(jnp.mean(xf * xf, axis=1, keepdims=True) + EPS)
    xn_own = (xf * inv_rms * gains[0:1]).astype(bf)
    scaled = d_normed * gains[0:1]
    inner = jnp.mean(scaled * xf, axis=1, keepdims=True)
    grad_tokens = (dres + inv_rms * scaled - xf * (inv_rms * inv_rms * inv_rms * inner)).astype(bf)

    grads = jnp.concatenate(
        [dot(xn_own, dq, 0, 0).astype(bf), dot(xn, dk, 0, 0).astype(bf), dot(xn, dv, 0, 0).astype(bf),
         dot(o, dlow, 0, 0).astype(bf)], axis=1
    )
    tiny = jnp.concatenate(
        [dgain[0].reshape(n_fsdp, own_rows), dgain[1].reshape(n_fsdp, own_rows),
         dtab[:H, :NB].T.reshape(n_fsdp, table_size)], axis=1
    ).astype(bf)
    tiny = jnp.pad(tiny[:, None, :], ((0, 0), (0, 15), (0, 4 * D - tiny.shape[1])))
    payload = jnp.concatenate([grads.reshape(n_fsdp, own_rows, 4 * D), tiny], axis=1)
    if fast:
        a, b, c = scatter_four([lax.dynamic_index_in_dim(payload, order[r], 0, False) for r in range(4)])
        payload = add(a, b, c)
    else:
        payload = lax.psum_scatter(payload, "fsdp", scatter_dimension=0)
    payload = lax.psum(payload, "ctx").astype(f32)
    tiny = payload[own_rows]
    return (
        output[None],
        grad_tokens[None],
        payload[:own_rows, 0:D],
        payload[:own_rows, D : 2 * D],
        payload[:own_rows, 2 * D : 3 * D],
        payload[:own_rows, 3 * D : 4 * D],
        grad_in.astype(f32),
        grad_ffn_out.astype(f32),
        tiny[:own_rows],
        tiny[own_rows : 2 * own_rows],
        tiny[2 * own_rows : 2 * own_rows + table_size].reshape(rel_table.shape),
    )


def solution(mesh):
    rows, vector, whole = P("fsdp", None), P("fsdp"), P("fsdp", "ctx", None)
    return jax.shard_map(
        on_device,
        mesh=mesh,
        in_specs=(whole,) + (rows,) * 8 + (vector, vector, rows, whole),
        out_specs=(whole, whole) + (rows,) * 6 + (vector, vector, rows),
        check_vma=False,
    )
```

```python
import jax
import jax.numpy as jnp
from jax import lax
from jax.experimental import pallas as pl
from jax.experimental.pallas import tpu as pltpu
from jax.sharding import PartitionSpec as P

D = 768
H = 12
DH = 64
NB = 32
SPAN = 128
PAIRS = H // 2
BIG = 1e30
VMEM_LIMIT = 56 * 2**20
EPS = 1e-06
GELU_C = 0.7978845608028654
ANY = pl.ANY


def bucket_of(relative):
    distance = jnp.abs(relative)
    far_steps = jnp.zeros_like(distance)
    for exponent in range(1, 8):
        far_steps = far_steps + (distance * distance >= 64 * 2**exponent).astype(jnp.int32)
    magnitude = jnp.where(distance < 8, distance, 8 + far_steps)
    return magnitude + jnp.where(relative > 0, 16, 0).astype(jnp.int32)


def dot(a, b, ca=1, cb=0):
    return lax.dot_general(a, b, (((ca,), (cb,)), ((), ())), preferred_element_type=jnp.float32)


def diagonal_onehot(offset):
    lane = lax.broadcasted_iota(jnp.int32, (128, 256), 1)
    row = lax.broadcasted_iota(jnp.int32, (128, 256), 0)
    return (bucket_of(offset * SPAN + 127 - lane) == row).astype(jnp.bfloat16)


def fill_inverse(order_ref, inv_ref, spans):
    def put(i, carry):
        inv_ref[order_ref[0, i]] = i
        return carry

    lax.fori_loop(0, spans, put, 0)


def fill_near_bias(table_t, near_ref):
    for index in range(3):
        rows = dot(table_t, diagonal_onehot(index - 1))
        for head in range(H):
            wide = jnp.broadcast_to(rows[head : head + 1, :], (128, 256))
            tile = pltpu.roll(wide, 129, 1, stride=1, stride_axis=0)[:, :128]
            near_ref[index, head // 2, :, (head % 2) * 128 : (head % 2) * 128 + 128] = tile
    near_ref[3] = jnp.zeros_like(near_ref[3])


def key_range(span, b1, b2, b3, total):
    first, last = span * SPAN, span * SPAN + SPAN - 1
    start = jnp.where(first >= b3, b3, jnp.where(first >= b2, b2, jnp.where(first >= b1, b1, 0)))
    end = jnp.where(last < b1, b1, jnp.where(last < b2, b2, jnp.where(last < b3, b3, total)))
    return start // 256, (end + 255) // 256


def key_features(chunk, span, b1, b2, b3):
    lane = lax.broadcasted_iota(jnp.int32, (256, 128), 1)
    pos = lax.broadcasted_iota(jnp.int32, (256, 128), 0) + chunk * 256
    seg = (pos >= b1).astype(jnp.int32) + (pos >= b2).astype(jnp.int32) + (pos >= b3).astype(jnp.int32)
    code = jnp.where(pos < (span - 1) * SPAN, 4, jnp.where(pos >= (span + 2) * SPAN, 5, seg))
    hot = (lane == seg) | (lane == code) | ((lane >= 6) & (lane < 9))
    return jnp.where(hot, 1.0, 0.0).astype(jnp.bfloat16)


def query_features(span, pair, tab_ref, b1, b2, b3, extra=None):
    row = lax.broadcasted_iota(jnp.int32, (128, 256), 0)
    lane = lax.broadcasted_iota(jnp.int32, (128, 256), 1)
    pos = (lane % SPAN) + span * SPAN
    seg = (pos >= b1).astype(jnp.int32) + (pos >= b2).astype(jnp.int32) + (pos >= b3).astype(jnp.int32)
    first = lane < 128
    below = jnp.where(first, tab_ref[NB // 2 - 1, 2 * pair], tab_ref[NB // 2 - 1, 2 * pair + 1])
    above = jnp.where(first, tab_ref[NB - 1, 2 * pair], tab_ref[NB - 1, 2 * pair + 1])
    feat = jnp.where((row < 4) & (row != seg), -BIG, 0.0)
    feat = jnp.where(row == 4, below, jnp.where(row == 5, above, feat))
    if extra is not None:
        high = extra.astype(jnp.bfloat16).astype(jnp.float32)
        rest = extra - high
        mid = rest.astype(jnp.bfloat16).astype(jnp.float32)
        low = rest - mid
        feat = jnp.where(row == 6, high, jnp.where(row == 7, mid, jnp.where(row == 8, low, feat)))
    return feat.astype(jnp.bfloat16)


def block_diagonal(x_t):
    row = lax.broadcasted_iota(jnp.int32, (128, 128), 0)
    zero = jnp.zeros_like(x_t)
    return jnp.concatenate([jnp.where(row < DH, x_t, zero), jnp.where(row >= DH, x_t, zero)], axis=1)


def stacked_heads(x):
    lane = lax.broadcasted_iota(jnp.int32, (128, 128), 1)
    zero = jnp.zeros_like(x)
    return jnp.concatenate([jnp.where(lane < DH, x, zero), jnp.where(lane >= DH, x, zero)], axis=0)


def near_index(delta):
    return jnp.where((delta >= -1) & (delta <= 1), delta + 1, 3)


def smem():
    return pl.BlockSpec(memory_space=pltpu.SMEM)


def vmem():
    return pl.BlockSpec(memory_space=pltpu.VMEM)


def once():
    return pl.BlockSpec(memory_space=pltpu.VMEM, pipeline_mode=pl.Buffered(1))


def by_chunk():
    return pl.BlockSpec((256, D), lambda t: (t, 0))


def hbm():
    return pl.BlockSpec(memory_space=ANY)


def cost(us):
    return pl.CostEstimate(flops=int(us * 1.0e9), bytes_accessed=int(us * 1.0e6), transcendentals=0)


def load_pieces(pieces, target_ref, flip, sem):
    copies = []
    rows = target_ref.shape[0] // len(pieces)
    for number, (ref, index, place) in enumerate(pieces):
        start = pl.multiple_of(lax.bitwise_xor(jnp.int32(place), flip) * rows, 16)
        source = ref.at[index, pl.ds(0, rows)]
        copies.append(pltpu.make_async_copy(source, target_ref.at[pl.ds(start, rows)], sem.at[number]))
    for copy in copies:
        copy.start()
    return copies


def expand(refs):
    out, place = [], 0
    for ref in refs:
        for index in range(ref.shape[0]):
            out.append((ref, index, place))
            place += 1
    return out


def forward_kernel(counts, *refs):
    n_x, n_w = counts
    ids_ref, order_ref, len_ref, tab_ref, table_t_ref, gain_ref = refs[:6]
    x_refs, w_refs = refs[6 : 6 + n_x], refs[6 + n_x : 6 + n_x + n_w]
    (
        nf_ref, res_ref, o_ref, ot_ref, lse_ref, q_ref, k_ref, v_ref, xn_ref,
        inv_ref, x_ref, w_ref, rhs_ref, near_ref, s_ref, m_ref, l_ref, acc_ref, sem_x, sem_w,
    ) = refs[6 + n_x + n_w :]
    spans, own = order_ref.shape[1], q_ref.shape[0] // SPAN
    b1 = len_ref[0, 0]
    b2 = b1 + len_ref[0, 1]
    b3 = b2 + len_ref[0, 2]
    copies = load_pieces(expand(x_refs), x_ref, jnp.int32(0), sem_x)
    copies += load_pieces(expand(w_refs), w_ref, ids_ref[2], sem_w)
    fill_inverse(order_ref, inv_ref, spans)
    fill_near_bias(table_t_ref[...], near_ref)
    for copy in copies:
        copy.wait()
    own_rows = own * SPAN
    gain = gain_ref[0:1, :]

    def normed(x):
        x = x.astype(jnp.float32)
        return (x * lax.rsqrt(jnp.mean(x * x, axis=1, keepdims=True) + EPS) * gain).astype(jnp.bfloat16)

    my_spans = [order_ref[0, ids_ref[0] * own + i] for i in range(own)]
    my_ranges = [key_range(span, b1, b2, b3, spans * SPAN) for span in my_spans]

    def project(t, carry):
        needed = jnp.bool_(False)
        for low, high in my_ranges:
            needed = needed | ((t >= low) & (t < high))
        rows = pl.ds(pl.multiple_of(t * 256, 256), 256)

        def fill():
            parts = []
            for half in range(2):
                slot = inv_ref[2 * t + half]
                piece = lax.bitwise_xor(slot // own, ids_ref[1])
                start = pl.multiple_of(piece * own_rows + (slot % own) * SPAN, SPAN)
                parts.append(x_ref[pl.ds(start, SPAN), :])
            xn = normed(jnp.concatenate(parts, axis=0))
            xn_ref[rows, :] = xn
            k_ref[rows, :] = dot(xn, w_ref[:, D : 2 * D]).astype(jnp.bfloat16)
            v_ref[rows, :] = dot(xn, w_ref[:, 2 * D : 3 * D]).astype(jnp.bfloat16)

        def skip():
            xn_ref[rows, :] = jnp.zeros((256, D), jnp.bfloat16)

        pl.when(needed)(fill)
        pl.when(jnp.logical_not(needed))(skip)
        return carry

    lax.fori_loop(0, spans // 2, project, 0)
    mine = pl.multiple_of(lax.bitwise_xor(ids_ref[0], ids_ref[1]) * own_rows, SPAN)
    x_own = x_ref[pl.ds(mine, own_rows), :]
    q_ref[...] = dot(normed(x_own), w_ref[:, 0:D]).astype(jnp.bfloat16)

    def one_span(i, carry):
        span = order_ref[0, ids_ref[0] * own + i]
        low, high = key_range(span, b1, b2, b3, spans * SPAN)
        my_rows = pl.ds(pl.multiple_of(i * SPAN, SPAN), SPAN)
        for p in range(PAIRS):
            q_t = q_ref[my_rows, p * 128 : p * 128 + 128].T
            rhs_ref[p, 0:128, :] = block_diagonal(q_t)
            rhs_ref[p, 128:256, :] = query_features(span, p, tab_ref, b1, b2, b3)
        m_ref[...] = jnp.full_like(m_ref, -BIG)
        l_ref[...] = jnp.zeros_like(l_ref)
        acc_ref[...] = jnp.zeros_like(acc_ref)

        def chunk_body(t, near):
            rows = pl.ds(pl.multiple_of(t * 256, 256), 256)
            feat = key_features(t, span, b1, b2, b3)
            scales, tops = [], []
            for p in range(PAIRS):
                kp = k_ref[rows, p * 128 : p * 128 + 128]
                s = dot(jnp.concatenate([kp, feat], axis=1), rhs_ref[p])
                if near:
                    n0, n1 = near_index(2 * t - span), near_index(2 * t + 1 - span)
                    s = s + jnp.concatenate([near_ref[n0, p], near_ref[n1, p]], axis=0)
                s_ref[p] = s
                old = m_ref[p]
                new = jnp.maximum(old, jnp.max(s, axis=0, keepdims=True))
                m_ref[p] = new
                scales.append(jnp.exp(old - new))
                tops.append(new)
            for p in range(PAIRS):
                scale = scales[p]
                e = jnp.exp(s_ref[p] - tops[p])
                l_ref[p] = l_ref[p] * scale + jnp.sum(e, axis=0, keepdims=True)
                vp = v_ref[rows, p * 128 : p * 128 + 128]
                o = dot(vp, e.astype(jnp.bfloat16), 0, 0)
                acc_ref[p, 0:64, :] = acc_ref[p, 0:64, :] * scale[:, 0:128] + o[0:64, 0:128]
                acc_ref[p, 64:128, :] = acc_ref[p, 64:128, :] * scale[:, 128:256] + o[64:128, 128:256]

        def step(t, carry):
            near = (2 * t + 2 >= span) & (2 * t <= span + 1)
            pl.when(near)(lambda: chunk_body(t, True))
            pl.when(jnp.logical_not(near))(lambda: chunk_body(t, False))
            return carry

        lax.fori_loop(low, high, step, 0)
        for p in range(PAIRS):
            total = l_ref[p]
            lse_ref[i, p] = m_ref[p] + jnp.log(total)
            inv = 1.0 / total
            out = jnp.concatenate(
                [acc_ref[p, 0:64, :] * inv[:, 0:128], acc_ref[p, 64:128, :] * inv[:, 128:256]], axis=0
            )
            ot_ref[i, p] = out
            o_ref[my_rows, p * 128 : p * 128 + 128] = out.T.astype(jnp.bfloat16)
        return carry

    lax.fori_loop(0, own, one_span, 0)
    res = x_own.astype(jnp.float32) + dot(o_ref[...], w_ref[:, 3 * D : 4 * D])
    res_ref[...] = res
    inv_rms = lax.rsqrt(jnp.mean(res * res, axis=1, keepdims=True) + EPS)
    nf_ref[...] = (res * inv_rms * gain_ref[1:2, :]).astype(jnp.bfloat16)


def forward(ids, order, lengths, table, table_t, gains, xs, ws, local_rows):
    spans, own = order.shape[1], local_rows // SPAN
    rows = spans * SPAN
    n_x, n_w = sum(x.shape[0] for x in xs), sum(w.shape[0] for w in ws)
    bf, f32 = jnp.bfloat16, jnp.float32
    return pl.pallas_call(
        lambda *refs: forward_kernel((len(xs), len(ws)), *refs),
        name="forward",
        cost_estimate=cost(22),
        out_shape=(
            jax.ShapeDtypeStruct((local_rows, D), bf),
            jax.ShapeDtypeStruct((local_rows, D), f32),
            jax.ShapeDtypeStruct((local_rows, D), bf),
            jax.ShapeDtypeStruct((own, PAIRS, 128, 128), f32),
            jax.ShapeDtypeStruct((own, PAIRS, 1, 256), f32),
            jax.ShapeDtypeStruct((local_rows, D), bf),
            jax.ShapeDtypeStruct((rows, D), bf),
            jax.ShapeDtypeStruct((rows, D), bf),
            jax.ShapeDtypeStruct((rows, D), bf),
        ),
        in_specs=[smem()] * 4 + [vmem()] * 2 + [hbm()] * (len(xs) + len(ws)),
        out_specs=(vmem(),) * 9,
        scratch_shapes=[
            pltpu.SMEM((spans,), jnp.int32),
            pltpu.VMEM((rows, D), bf),
            pltpu.VMEM((D, 4 * D), bf),
            pltpu.VMEM((PAIRS, 256, 256), bf),
            pltpu.VMEM((4, PAIRS, 128, 256), f32),
            pltpu.VMEM((PAIRS, 256, 256), f32),
            pltpu.VMEM((PAIRS, 1, 256), f32),
            pltpu.VMEM((PAIRS, 1, 256), f32),
            pltpu.VMEM((PAIRS, 128, 128), f32),
            pltpu.SemaphoreType.DMA((n_x,)),
            pltpu.SemaphoreType.DMA((n_w,)),
        ],
        compiler_params=pltpu.CompilerParams(vmem_limit_bytes=VMEM_LIMIT),
    )(ids, order, lengths, table, table_t, gains, *xs, *ws)


def join_kernel(counts, flip_at, *refs):
    ids_ref = refs[0]
    out_ref, sem = refs[1 + counts :]
    copies = load_pieces(expand(refs[1 : 1 + counts]), out_ref, ids_ref[flip_at], sem)
    for copy in copies:
        copy.wait()


def join(ids, pieces, flip_at):
    count, width = sum(p.shape[0] for p in pieces), pieces[0].shape[2]
    rows = pieces[0].shape[1] * count
    return pl.pallas_call(
        lambda *refs: join_kernel(len(pieces), flip_at, *refs),
        name="join",
        cost_estimate=cost(2),
        out_shape=jax.ShapeDtypeStruct((rows, width), jnp.bfloat16),
        in_specs=[smem()] + [hbm()] * len(pieces),
        out_specs=vmem(),
        scratch_shapes=[pltpu.SemaphoreType.DMA((count,))],
    )(ids, *pieces)


def ffn_kernel(nf_ref, cot_ref, w_ref, wffn_ref, act_ref, dup_ref, dn_ref):
    for piece in range(nf_ref.shape[0]):
        up = dot(nf_ref[piece], w_ref[...])
        d_act = dot(cot_ref[piece], wffn_ref[...], 1, 1)
        square = up * up
        th = jnp.tanh(GELU_C * (up + 0.044715 * square * up))
        half = 0.5 * (1.0 + th)
        act_ref[piece] = (up * half).astype(jnp.bfloat16)
        slope = half + 0.5 * up * (1.0 - th * th) * (GELU_C * (1.0 + 3 * 0.044715 * square))
        d_up = (d_act * slope).astype(jnp.bfloat16)
        dup_ref[piece] = d_up
        dn_ref[piece] = dot(d_up, w_ref[...], 1, 1).astype(jnp.bfloat16)


def ffn(nf, cot, win, wffn):
    count, rows, _ = nf.shape
    width = wffn.shape[0]
    bf = jnp.bfloat16
    return pl.pallas_call(
        ffn_kernel,
        name="ffn",
        cost_estimate=cost(3),
        out_shape=(
            jax.ShapeDtypeStruct((count, rows, width), bf),
            jax.ShapeDtypeStruct((count, rows, width), bf),
            jax.ShapeDtypeStruct((count, rows, D), bf),
        ),
        in_specs=[vmem()] * 4,
        out_specs=(vmem(),) * 3,
        compiler_params=pltpu.CompilerParams(vmem_limit_bytes=VMEM_LIMIT),
    )(nf, cot, win, wffn)


def ffn_grads_kernel(count, *refs):
    ids_ref = refs[0]
    nfs, cots, acts, dups = (refs[1 + i * count : 1 + (i + 1) * count] for i in range(4))
    gout_ref, gin_ref = refs[1 + 4 * count :]
    rows = nfs[0].shape[0] * nfs[0].shape[1]

    def joined(pieces):
        parts = [ref[...].reshape(rows, ref.shape[2]) for ref in pieces]
        return parts[0] if count == 1 else jnp.concatenate(parts, axis=0)

    gout_ref[...] = dot(joined(acts), joined(cots), 0, 0).astype(jnp.bfloat16)
    whole = dot(joined(nfs), joined(dups), 0, 0).astype(jnp.bfloat16)
    n, size = gin_ref.shape[0], gin_ref.shape[1]
    for i in range(n):
        gin_ref[lax.bitwise_xor(jnp.int32(i), ids_ref[3])] = whole[i * size : (i + 1) * size]


def ffn_grads(ids, nfs, cots, acts, dups, n_fsdp):
    count, width = len(nfs), acts[0].shape[2]
    bf = jnp.bfloat16
    return pl.pallas_call(
        lambda *refs: ffn_grads_kernel(count, *refs),
        name="ffn_grads",
        cost_estimate=cost(5),
        out_shape=(
            jax.ShapeDtypeStruct((width, D), bf),
            jax.ShapeDtypeStruct((n_fsdp, D // n_fsdp, width), bf),
        ),
        in_specs=[smem()] + [vmem()] * (4 * count),
        out_specs=(vmem(),) * 2,
        compiler_params=pltpu.CompilerParams(vmem_limit_bytes=VMEM_LIMIT),
    )(ids, *nfs, *cots, *acts, *dups)


def weight_grads_kernel(ids_ref, x_ref, xn_ref, gain_ref, dq_ref, dk_ref, dv_ref, o_ref, dlow_ref, tiny_ref, out_ref):
    n, parts, high, wide = out_ref.shape
    size = D // n
    x = x_ref[...].astype(jnp.float32)
    own = (x * lax.rsqrt(jnp.mean(x * x, axis=1, keepdims=True) + EPS) * gain_ref[0:1, :]).astype(jnp.bfloat16)
    results = (
        lambda: dot(own, dq_ref[...], 0, 0),
        lambda: dot(xn_ref[...], dk_ref[...], 0, 0),
        lambda: dot(xn_ref[...], dv_ref[...], 0, 0),
        lambda: dot(o_ref[...], dlow_ref[...], 0, 0),
    )
    step = min(D, wide)
    for column, result in enumerate(results):
        value = result().astype(jnp.bfloat16)
        for first in range(column * D, column * D + D, step):
            part = lax.bitwise_xor(jnp.int32(first // wide), ids_ref[1])
            inside = slice(first % wide, first % wide + step)
            here = slice(first - column * D, first - column * D + step)
            for i in range(n):
                place = lax.bitwise_xor(jnp.int32(i), ids_ref[3])
                out_ref[place, part, 0:size, inside] = value[i * size : (i + 1) * size, here]
    for i in range(n):
        place = lax.bitwise_xor(jnp.int32(i), ids_ref[3])
        for first in range(0, 4 * D, wide):
            part = lax.bitwise_xor(jnp.int32(first // wide), ids_ref[1])
            out_ref[place, part, size : size + 16, :] = tiny_ref[i, :, first : first + wide]


def weight_grads(ids, x, xn, gains, dq, dk, dv, o, dlow, tiny, parts):
    n = tiny.shape[0]
    return pl.pallas_call(
        weight_grads_kernel,
        name="weight_grads",
        cost_estimate=cost(9),
        out_shape=jax.ShapeDtypeStruct((n, parts, D // n + 16, 4 * D // parts), jnp.bfloat16),
        in_specs=[smem()] + [vmem()] * 9,
        out_specs=vmem(),
        compiler_params=pltpu.CompilerParams(vmem_limit_bytes=VMEM_LIMIT),
    )(ids, x, xn, gains, dq, dk, dv, o, dlow, tiny)


def finish_kernel(count, *refs):
    ids_ref = refs[0]
    parts = refs[1 : 1 + count]
    outs, tiny_ref, all_ref, sem = refs[1 + count : 5 + count], refs[5 + count], refs[6 + count], refs[7 + count]
    copies = []
    for number, ref in enumerate(parts):
        place = lax.bitwise_xor(jnp.int32(number), ids_ref[1])
        copies.append(pltpu.make_async_copy(ref, all_ref.at[place], sem.at[number]))
    for copy in copies:
        copy.start()
    for copy in copies:
        copy.wait()
    size, wide = outs[0].shape[0], all_ref.shape[2]
    step = min(D, wide)
    for first in range(0, 4 * D, step):
        value = all_ref[first // wide, :, first % wide : first % wide + step].astype(jnp.float32)
        outs[first // D][:, first % D : first % D + step] = value[0:size]
        tiny_ref[:, first : first + step] = value[size : size + 8]


def finish(ids, parts):
    high, wide = parts[0].shape
    f32 = jnp.float32
    return pl.pallas_call(
        lambda *refs: finish_kernel(len(parts), *refs),
        name="finish",
        cost_estimate=cost(3),
        out_shape=(jax.ShapeDtypeStruct((high - 16, D), f32),) * 4 + (jax.ShapeDtypeStruct((8, 4 * D), f32),),
        in_specs=[smem()] + [hbm()] * len(parts),
        out_specs=(vmem(),) * 5,
        scratch_shapes=[pltpu.VMEM((len(parts), high, wide), jnp.bfloat16), pltpu.SemaphoreType.DMA((len(parts),))],
        compiler_params=pltpu.CompilerParams(vmem_limit_bytes=VMEM_LIMIT),
    )(ids, *parts)


def backward_kernel(counts, *refs):
    n_x, n_w = counts
    (
        ids_ref, order_ref, len_ref, tab_ref, table_t_ref, gain_ref,
        dnf_ref, res_ref, cot_ref, o_ref, ot_ref, lse_ref, q_ref, k_ref, v_ref,
    ) = refs[:15]
    x_refs, w_refs = refs[15 : 15 + n_x], refs[15 + n_x : 15 + n_x + n_w]
    (
        dres_ref, dlow_ref, dq_ref, dk_ref, dv_ref, dn_ref, dn_own_ref, dgain_ref, dtab_ref,
        inv_ref, x_ref, w_ref, do_ref, rhs_ref, dorhs_ref, qbd_ref, dobd_ref, near_ref, nacc_ref, acc_ref, far_ref,
        dkacc_ref, dvacc_ref, sem_x, sem_w,
    ) = refs[15 + n_x + n_w :]
    spans, own = order_ref.shape[1], q_ref.shape[0] // SPAN
    own_rows = own * SPAN
    b1 = len_ref[0, 0]
    b2 = b1 + len_ref[0, 1]
    b3 = b2 + len_ref[0, 2]
    t = pl.program_id(0)

    @pl.when(t == 0)
    def begin():
        copies_x = load_pieces(expand(x_refs), x_ref, jnp.int32(0), sem_x)
        copies_w = load_pieces(expand(w_refs), w_ref, ids_ref[2], sem_w)
        fill_inverse(order_ref, inv_ref, spans)
        fill_near_bias(table_t_ref[...], near_ref)
        nacc_ref[...] = jnp.zeros_like(nacc_ref)
        far_ref[...] = jnp.zeros_like(far_ref)

        res, dnf = res_ref[...], dnf_ref[...]
        inv_rms = lax.rsqrt(jnp.mean(res * res, axis=1, keepdims=True) + EPS)
        dgain_ref[...] = jnp.zeros_like(dgain_ref)
        dgain_ref[1:2, :] = jnp.sum(dnf * res * inv_rms, axis=0, keepdims=True)
        scaled = dnf * gain_ref[1:2, :]
        inner = jnp.mean(scaled * res, axis=1, keepdims=True)
        dres = cot_ref[...].astype(jnp.float32) + inv_rms * scaled - res * (inv_rms * inv_rms * inv_rms * inner)
        dres_ref[...] = dres
        dlow = dres.astype(jnp.bfloat16)
        dlow_ref[...] = dlow
        for copy in copies_w:
            copy.wait()
        do_ref[...] = dot(dlow, w_ref[:, 3 * D : 4 * D], 1, 1).astype(jnp.bfloat16)

        def prepare(i, carry):
            span = order_ref[0, ids_ref[0] * own + i]
            my_rows = pl.ds(pl.multiple_of(i * SPAN, SPAN), SPAN)
            for p in range(PAIRS):
                cols = slice(p * 128, p * 128 + 128)
                qp, dop = q_ref[my_rows, cols], do_ref[my_rows, cols]
                do_t = dop.T
                prod = do_t.astype(jnp.float32) * ot_ref[i, p]
                neg = -jnp.concatenate(
                    [jnp.sum(prod[0:64], axis=0, keepdims=True), jnp.sum(prod[64:128], axis=0, keepdims=True)], axis=1
                )
                rhs_ref[i, p, 0:128, :] = block_diagonal(qp.T)
                rhs_ref[i, p, 128:256, :] = query_features(span, p, tab_ref, b1, b2, b3, -lse_ref[i, p])
                row = lax.broadcasted_iota(jnp.int32, (128, 256), 0)
                h1 = neg.astype(jnp.bfloat16).astype(jnp.float32)
                h2 = (neg - h1).astype(jnp.bfloat16).astype(jnp.float32)
                h3 = neg - h1 - h2
                dfeat = jnp.where(row == 6, h1, jnp.where(row == 7, h2, jnp.where(row == 8, h3, 0.0)))
                dorhs_ref[i, p, 0:128, :] = block_diagonal(do_t)
                dorhs_ref[i, p, 128:256, :] = dfeat.astype(jnp.bfloat16)
                qbd_ref[i, p] = stacked_heads(qp)
                dobd_ref[i, p] = stacked_heads(dop)
            return carry

        lax.fori_loop(0, own, prepare, 0)
        acc_ref[...] = jnp.zeros_like(acc_ref)
        for copy in copies_x:
            copy.wait()


    def unit(x):
        x = x.astype(jnp.float32)
        return x * lax.rsqrt(jnp.mean(x * x, axis=1, keepdims=True) + EPS)

    dkacc_ref[...] = jnp.zeros_like(dkacc_ref)
    dvacc_ref[...] = jnp.zeros_like(dvacc_ref)

    def span_body(i, span, near):
        feat = key_features(t, span, b1, b2, b3)
        for p in range(PAIRS):
            cols = slice(p * 128, p * 128 + 128)
            kf = jnp.concatenate([k_ref[:, cols], feat], axis=1)
            s = dot(kf, rhs_ref[i, p])
            if near:
                n0, n1 = near_index(2 * t - span), near_index(2 * t + 1 - span)
                s = s + jnp.concatenate([near_ref[n0, p], near_ref[n1, p]], axis=0)
            prob = jnp.exp(s)
            ds = prob * dot(jnp.concatenate([v_ref[:, cols], feat], axis=1), dorhs_ref[i, p])
            if near:
                nacc_ref[n0, p] += ds[0:128]
                nacc_ref[n1, p] += ds[128:256]
            dsb = ds.astype(jnp.bfloat16)
            dvacc_ref[:, cols] += dot(prob.astype(jnp.bfloat16), dobd_ref[i, p])
            dkacc_ref[:, cols] += dot(dsb, qbd_ref[i, p])
            dq = dot(kf, dsb, 0, 0)
            acc_ref[i, p, 0:64, :] += dq[0:64, 0:128]
            acc_ref[i, p, 64:128, :] += dq[64:128, 128:256]
            far_ref[p] += dq[128:136, :]

    def one_span(i, used):
        span = order_ref[0, ids_ref[0] * own + i]
        low, high = key_range(span, b1, b2, b3, spans * SPAN)
        needed = (t >= low) & (t < high)
        near = (2 * t + 2 >= span) & (2 * t <= span + 1)
        pl.when(needed & near)(lambda: span_body(i, span, True))
        pl.when(needed & jnp.logical_not(near))(lambda: span_body(i, span, False))
        return used + needed.astype(jnp.int32)

    used = lax.fori_loop(0, own, one_span, jnp.int32(0))
    places = []
    for half in range(2):
        slot = inv_ref[2 * t + half]
        piece = lax.bitwise_xor(slot // own, ids_ref[1])
        places.append(pl.ds(pl.multiple_of(piece * own_rows + (slot % own) * SPAN, SPAN), SPAN))

    def fill():
        dkb, dvb = dkacc_ref[...].astype(jnp.bfloat16), dvacc_ref[...].astype(jnp.bfloat16)
        dk_ref[...] = dkb
        dv_ref[...] = dvb
        part = dot(dkb, w_ref[:, D : 2 * D], 1, 1) + dot(dvb, w_ref[:, 2 * D : 3 * D], 1, 1)
        x = jnp.concatenate([x_ref[places[0], :], x_ref[places[1], :]], axis=0)
        dgain_ref[0:1, :] += jnp.sum(part * unit(x), axis=0, keepdims=True)
        part = part.astype(jnp.bfloat16)
        dn_ref[places[0], :] = part[0:128]
        dn_ref[places[1], :] = part[128:256]

    def skip():
        zero = jnp.zeros((256, D), jnp.bfloat16)
        dk_ref[...] = zero
        dv_ref[...] = zero
        dn_ref[places[0], :] = zero[0:128]
        dn_ref[places[1], :] = zero[0:128]

    pl.when(used > 0)(fill)
    pl.when(used == 0)(skip)


    @pl.when(t == spans // 2 - 1)
    def finish():
        for i in range(own):
            for p in range(PAIRS):
                dq_ref[i * SPAN : (i + 1) * SPAN, p * 128 : p * 128 + 128] = acc_ref[i, p].T.astype(jnp.bfloat16)
        mine = pl.multiple_of(lax.bitwise_xor(ids_ref[0], ids_ref[1]) * own_rows, SPAN)
        own_part = dot(dq_ref[...], w_ref[:, 0:D], 1, 1)
        dn_own_ref[...] = own_part
        dgain_ref[0:1, :] += jnp.sum(own_part * unit(x_ref[pl.ds(mine, own_rows), :]), axis=0, keepdims=True)

        row16 = lax.broadcasted_iota(jnp.int32, (16, 128), 0)
        lane16 = lax.broadcasted_iota(jnp.int32, (16, 128), 1)
        grad = jnp.zeros((16, 128), jnp.float32)
        for head in range(H):
            half = slice((head % 2) * 128, (head % 2) * 128 + 128)
            sums = jnp.sum(far_ref[head // 2, 4:6, half], axis=1, keepdims=True)
            grad = grad + jnp.where((row16 == head) & (lane16 == NB // 2 - 1), sums[0:1], 0.0)
            grad = grad + jnp.where((row16 == head) & (lane16 == NB - 1), sums[1:2], 0.0)
        rowd = lax.broadcasted_iota(jnp.int32, (16, 256), 0)
        flip_row = lax.broadcasted_iota(jnp.int32, (128, 128), 0)
        flip_lane = lax.broadcasted_iota(jnp.int32, (128, 128), 1)
        flip = (flip_row + flip_lane == 127).astype(jnp.bfloat16)
        for index in range(3):
            sums = jnp.zeros((16, 256), jnp.float32)
            for p in range(PAIRS):
                both = nacc_ref[index, p]
                high = both.astype(jnp.bfloat16)
                rest = (both - high.astype(jnp.float32)).astype(jnp.bfloat16)
                turned = dot(flip, high) + dot(flip, rest)
                for side in range(2):
                    tile = turned[:, side * 128 : side * 128 + 128]
                    wide = jnp.concatenate([tile, jnp.zeros_like(tile)], axis=1)
                    shifted = pltpu.roll(wide, 0, 1, stride=1, stride_axis=0)
                    sums = sums + jnp.where(rowd == 2 * p + side, jnp.sum(shifted, axis=0, keepdims=True), 0.0)
            hot = diagonal_onehot(index - 1).astype(jnp.float32)
            grad = grad + lax.dot_general(
                sums, hot, (((1,), (1,)), ((), ())), preferred_element_type=jnp.float32, precision=lax.Precision.HIGHEST
            )
        dtab_ref[...] = grad


def backward(ids, order, lengths, table, table_t, gains, dnf, res, cot, o, ot, lse, q, k, v, xs, ws):
    spans, local_rows = order.shape[1], q.shape[0]
    rows, own = spans * SPAN, local_rows // SPAN
    n_x, n_w = sum(x.shape[0] for x in xs), sum(w.shape[0] for w in ws)
    bf, f32 = jnp.bfloat16, jnp.float32
    return pl.pallas_call(
        lambda *refs: backward_kernel((len(xs), len(ws)), *refs),
        name="backward",
        cost_estimate=cost(36),
        grid=(spans // 2,),
        out_shape=(
            jax.ShapeDtypeStruct((local_rows, D), f32),
            jax.ShapeDtypeStruct((local_rows, D), bf),
            jax.ShapeDtypeStruct((local_rows, D), bf),
            jax.ShapeDtypeStruct((rows, D), bf),
            jax.ShapeDtypeStruct((rows, D), bf),
            jax.ShapeDtypeStruct((rows, D), bf),
            jax.ShapeDtypeStruct((local_rows, D), f32),
            jax.ShapeDtypeStruct((8, D), f32),
            jax.ShapeDtypeStruct((16, 128), f32),
        ),
        in_specs=[smem()] * 4 + [once()] * 9 + [by_chunk()] * 2 + [hbm()] * (len(xs) + len(ws)),
        out_specs=(once(),) * 3 + (by_chunk(),) * 2 + (once(),) * 4,
        scratch_shapes=[
            pltpu.SMEM((spans,), jnp.int32),
            pltpu.VMEM((rows, D), bf),
            pltpu.VMEM((D, 4 * D), bf),
            pltpu.VMEM((local_rows, D), bf),
            pltpu.VMEM((own, PAIRS, 256, 256), bf),
            pltpu.VMEM((own, PAIRS, 256, 256), bf),
            pltpu.VMEM((own, PAIRS, 256, 128), bf),
            pltpu.VMEM((own, PAIRS, 256, 128), bf),
            pltpu.VMEM((4, PAIRS, 128, 256), f32),
            pltpu.VMEM((4, PAIRS, 128, 256), f32),
            pltpu.VMEM((own, PAIRS, 128, 128), f32),
            pltpu.VMEM((PAIRS, 8, 256), f32),
            pltpu.VMEM((256, D), f32),
            pltpu.VMEM((256, D), f32),
            pltpu.SemaphoreType.DMA((n_x,)),
            pltpu.SemaphoreType.DMA((n_w,)),
        ],
        compiler_params=pltpu.CompilerParams(vmem_limit_bytes=VMEM_LIMIT),
    )(ids, order, lengths, table, table_t, gains, dnf, res, cot, o, ot, lse, q, k, v, *xs, *ws)


def swap(x, axis, bit):
    count = lax.axis_size(axis)
    return lax.ppermute(x, axis, [(i, i ^ bit) for i in range(count)])


def block(x, index, count, dim=0):
    size = x.shape[dim] // count
    return lax.dynamic_slice_in_dim(x, index * size, size, dim)


def after(x, *others):
    return lax.optimization_barrier((x,) + others)[0]


def gather_four(x):
    across = swap(x, "fsdp", 2)
    return [x, swap(x, "fsdp", 1), across, swap(across, "fsdp", 1)]


def scatter_four(pieces):
    first, third = swap(pieces[1], "fsdp", 1), swap(pieces[3], "fsdp", 1)
    far = add(pieces[2], third)
    return pieces[0], first, swap(far, "fsdp", 2)


def exchange_four(pieces):
    side, corner = swap(pieces[1], "fsdp", 1), swap(pieces[3], "fsdp", 1)
    return [pieces[0], side, swap(pieces[2], "fsdp", 2), swap(corner, "fsdp", 2)]


def ctx_scatter(p):
    got7, got5 = swap(p[7], "ctx", 1), swap(p[5], "ctx", 1)
    got3, got1 = swap(after(p[3], got7), "ctx", 1), swap(after(p[1], got5), "ctx", 1)
    s6, s4, s2 = add(p[6], got7), add(p[4], got5), add(p[2], got3)
    t4 = add(s4, swap(s6, "ctx", 2))
    return p[0], got1, swap(s2, "ctx", 2), swap(t4, "ctx", 4)


def ctx_gather(x):
    x1, x2, x4 = swap(x, "ctx", 1), swap(x, "ctx", 2), swap(x, "ctx", 4)
    x3, x6 = swap(after(x2, x1), "ctx", 1), swap(x4, "ctx", 2)
    x5 = swap(after(x4, x3), "ctx", 1)
    return [x, x1, x2, x3, x4, x5, x6, swap(after(x6, x5), "ctx", 1)]


def add(*terms):
    total = terms[0].astype(jnp.float32)
    for term in terms[1:]:
        total = total + term.astype(jnp.float32)
    return total.astype(jnp.bfloat16)


def on_device(
    tokens,
    lengths,
    span_order,
    w_query,
    w_key,
    w_value,
    w_out,
    w_in,
    w_ffn_out,
    gain_attn,
    gain_ffn,
    rel_table,
    cotangent,
):
    n_ctx, n_fsdp = lax.axis_size("ctx"), lax.axis_size("fsdp")
    fast = n_ctx == 8 and n_fsdp == 4
    place = lax.axis_index("ctx").astype(jnp.int32)
    shard = lax.axis_index("fsdp").astype(jnp.int32)
    local_rows = tokens.shape[1]
    own_rows = w_query.shape[0]
    bf, f32 = jnp.bfloat16, jnp.float32
    x, cot = tokens[0], cotangent[0]
    table_size = rel_table.size
    small = jnp.concatenate([gain_attn, gain_ffn, rel_table.reshape(-1)])
    small = jnp.pad(small[None], ((0, 15), (0, 4 * D - small.shape[0])))
    weights = jnp.concatenate([jnp.concatenate([w_query, w_key, w_value, w_out], axis=1), small], axis=0)
    width = w_ffn_out.shape[0]

    if fast:
        ids = jnp.stack([place, place, jnp.int32(0), shard])
        order = [shard ^ r for r in range(4)]
        parts = ctx_gather(x)
        xs = [p[None] for p in parts]
        columns = after(w_in, parts[6])
        columns = [block(columns, order[r], 4, 1) for r in range(4)]
        side, corner = swap(columns[1], "fsdp", 1), swap(columns[3], "fsdp", 1)
        wins = [columns[0], side, swap(columns[2], "fsdp", 2), swap(corner, "fsdp", 2)]
        cot2 = swap(after(cot, parts[5]), "fsdp", 2)
        cots = [p[None] for p in (cot, swap(after(cot, parts[5]), "fsdp", 1), cot2, swap(cot2, "fsdp", 1))]
        wins = [p[None] for p in wins]
    else:
        ids = jnp.stack([place, jnp.int32(0), jnp.int32(0), jnp.int32(0)])
        xs = [lax.all_gather(x, "ctx", axis=0)]
        parts = jnp.stack([w_in[:, i * width : (i + 1) * width] for i in range(n_fsdp)])
        wins = [lax.all_to_all(parts, "fsdp", 0, 0)]
        cots = [lax.all_gather(cot, "fsdp", axis=0)]

    ws = [lax.all_gather(weights, "fsdp", axis=0)]
    smalls = ws[0][:, own_rows]
    gains = jnp.stack([smalls[:, :own_rows].reshape(D), smalls[:, own_rows : 2 * own_rows].reshape(D)]).astype(f32)
    table_bf = smalls[:, 2 * own_rows : 2 * own_rows + table_size].reshape(NB, H)
    table = table_bf.astype(f32)
    table_t = jnp.pad(table_bf.T, ((0, 16 - H), (0, 128 - NB)))

    win = join(ids, wins, 3)
    nf, res, o, ot, lse, q, k, v, xn = forward(
        ids, span_order, lengths, table, table_t, gains, xs, ws, local_rows
    )

    if fast:
        nfs = [p[None] for p in gather_four(nf)]
    else:
        nfs = [lax.all_gather(nf, "fsdp", axis=0)]
    acts, dups, dns = zip(*(ffn(n, c, win, w_ffn_out) for n, c in zip(nfs, cots)))
    if fast:
        a, b, c = scatter_four([p[0] for p in dns])
        dnf = a.astype(f32) + b.astype(f32) + c.astype(f32)
    else:
        dnf = lax.psum_scatter(dns[0], "fsdp", scatter_dimension=0).astype(f32)
    grad_ffn_out, grad_in = ffn_grads(ids, nfs, cots, acts, dups, n_fsdp)
    if fast:
        grad_in = jnp.concatenate(exchange_four([grad_in[r] for r in range(4)]))
    else:
        grad_in = lax.all_to_all(grad_in, "fsdp", 0, 0).reshape(D, width)
    dnf = after(dnf, grad_in)
    grad_ffn_out = lax.psum_scatter(grad_ffn_out, "ctx", scatter_dimension=0, tiled=True)
    grad_in = lax.psum_scatter(grad_in, "ctx", scatter_dimension=0, tiled=True)
    out_parts = [dot(p.reshape(-1, width), w_ffn_out).astype(bf) for p in acts]
    if fast:
        a, b, c = scatter_four(out_parts)
        output = (res + a.astype(f32) + b.astype(f32) + c.astype(f32)).astype(bf)
    else:
        out_part = out_parts[0].reshape(n_fsdp, local_rows, D)
        output = (res + lax.psum_scatter(out_part, "fsdp", scatter_dimension=0).astype(f32)).astype(bf)

    dres, dlow, dq, dk, dv, dn, dn_own, dgain, dtab = backward(
        ids, span_order, lengths, table, table_t, gains, dnf, res, cot, o, ot, lse, q, k, v, xs, ws
    )
    dn = dn.reshape(n_ctx, local_rows, D)
    if fast:
        a, b, c, d = ctx_scatter([dn[r] for r in range(8)])
        d_normed = dn_own + a.astype(f32) + b.astype(f32) + c.astype(f32) + d.astype(f32)
    else:
        d_normed = dn_own + lax.psum_scatter(dn, "ctx", scatter_dimension=0).astype(f32)

    xf = x.astype(f32)
    inv_rms = lax.rsqrt(jnp.mean(xf * xf, axis=1, keepdims=True) + EPS)
    scaled = d_normed * gains[0:1]
    inner = jnp.mean(scaled * xf, axis=1, keepdims=True)
    grad_tokens = (dres + inv_rms * scaled - xf * (inv_rms * inv_rms * inv_rms * inner)).astype(bf)

    tiny = jnp.concatenate(
        [dgain[0].reshape(n_fsdp, own_rows), dgain[1].reshape(n_fsdp, own_rows),
         dtab[:H, :NB].T.reshape(n_fsdp, table_size)], axis=1
    ).astype(bf)
    tiny = jnp.pad(tiny[:, None, :], ((0, 0), (0, 15), (0, 4 * D - tiny.shape[1])))
    payload = weight_grads(ids, x, xn, gains, dq, dk, dv, o, dlow, tiny, 8 if fast else 1)
    if fast:
        payload = after(add(*scatter_four([payload[r] for r in range(4)])), d_normed)
        grads = ctx_gather(add(*ctx_scatter([payload[r] for r in range(8)])))
    else:
        payload = lax.psum_scatter(payload, "fsdp", scatter_dimension=0)
        grads = [lax.psum(payload, "ctx")[0]]
    g_query, g_key, g_value, g_out, tiny = finish(ids, grads)
    tiny = tiny[0]
    grad_ffn_out = lax.all_gather(grad_ffn_out, "ctx", axis=0, tiled=True)
    grad_in = lax.all_gather(grad_in, "ctx", axis=0, tiled=True).reshape(n_fsdp, own_rows, width)
    flip = shard if fast else jnp.int32(0)
    grad_in = jnp.concatenate([lax.dynamic_index_in_dim(grad_in, flip ^ i, 0, False) for i in range(n_fsdp)], axis=1)
    return (
        output[None],
        grad_tokens[None],
        g_query,
        g_key,
        g_value,
        g_out,
        grad_in.astype(f32),
        grad_ffn_out.astype(f32),
        tiny[:own_rows],
        tiny[own_rows : 2 * own_rows],
        tiny[2 * own_rows : 2 * own_rows + table_size].reshape(rel_table.shape),
    )


def solution(mesh):
    rows, vector, whole = P("fsdp", None), P("fsdp"), P("fsdp", "ctx", None)
    return jax.shard_map(
        on_device,
        mesh=mesh,
        in_specs=(whole,) + (rows,) * 8 + (vector, vector, rows, whole),
        out_specs=(whole, whole) + (rows,) * 6 + (vector, vector, rows),
        check_vma=False,
    )
```

```python
import jax
import jax.numpy as jnp
from jax import lax
from jax.experimental import pallas as pl
from jax.experimental.pallas import tpu as pltpu
from jax.sharding import PartitionSpec as P

D = 768
H = 12
DH = 64
NB = 32
SPAN = 128
PAIRS = H // 2
BIG = 1e30
VMEM_LIMIT = 56 * 2**20
EPS = 1e-06
GELU_C = 0.7978845608028654
ANY = pl.ANY


def bucket_of(relative):
    distance = jnp.abs(relative)
    far_steps = jnp.zeros_like(distance)
    for exponent in range(1, 8):
        far_steps = far_steps + (distance * distance >= 64 * 2**exponent).astype(jnp.int32)
    magnitude = jnp.where(distance < 8, distance, 8 + far_steps)
    return magnitude + jnp.where(relative > 0, 16, 0).astype(jnp.int32)


def dot(a, b, ca=1, cb=0):
    return lax.dot_general(a, b, (((ca,), (cb,)), ((), ())), preferred_element_type=jnp.float32)


def diagonal_onehot(offset):
    lane = lax.broadcasted_iota(jnp.int32, (128, 256), 1)
    row = lax.broadcasted_iota(jnp.int32, (128, 256), 0)
    return (bucket_of(offset * SPAN + 127 - lane) == row).astype(jnp.bfloat16)


def fill_inverse(order_ref, inv_ref, spans):
    def put(i, carry):
        inv_ref[order_ref[0, i]] = i
        return carry

    lax.fori_loop(0, spans, put, 0)


def fill_near_bias(table_t, near_ref):
    for index in range(3):
        rows = dot(table_t, diagonal_onehot(index - 1))
        for head in range(H):
            wide = jnp.broadcast_to(rows[head : head + 1, :], (128, 256))
            tile = pltpu.roll(wide, 129, 1, stride=1, stride_axis=0)[:, :128]
            near_ref[index, head // 2, :, (head % 2) * 128 : (head % 2) * 128 + 128] = tile
    near_ref[3] = jnp.zeros_like(near_ref[3])


def key_range(span, b1, b2, b3, total):
    first, last = span * SPAN, span * SPAN + SPAN - 1
    start = jnp.where(first >= b3, b3, jnp.where(first >= b2, b2, jnp.where(first >= b1, b1, 0)))
    end = jnp.where(last < b1, b1, jnp.where(last < b2, b2, jnp.where(last < b3, b3, total)))
    return start // 256, (end + 255) // 256


def key_features(chunk, span, b1, b2, b3):
    lane = lax.broadcasted_iota(jnp.int32, (256, 128), 1)
    pos = lax.broadcasted_iota(jnp.int32, (256, 128), 0) + chunk * 256
    seg = (pos >= b1).astype(jnp.int32) + (pos >= b2).astype(jnp.int32) + (pos >= b3).astype(jnp.int32)
    code = jnp.where(pos < (span - 1) * SPAN, 4, jnp.where(pos >= (span + 2) * SPAN, 5, seg))
    hot = (lane == seg) | (lane == code) | ((lane >= 6) & (lane < 9))
    return jnp.where(hot, 1.0, 0.0).astype(jnp.bfloat16)


def query_features(span, pair, tab_ref, b1, b2, b3, extra=None):
    row = lax.broadcasted_iota(jnp.int32, (128, 256), 0)
    lane = lax.broadcasted_iota(jnp.int32, (128, 256), 1)
    pos = (lane % SPAN) + span * SPAN
    seg = (pos >= b1).astype(jnp.int32) + (pos >= b2).astype(jnp.int32) + (pos >= b3).astype(jnp.int32)
    first = lane < 128
    below = jnp.where(first, tab_ref[NB // 2 - 1, 2 * pair], tab_ref[NB // 2 - 1, 2 * pair + 1])
    above = jnp.where(first, tab_ref[NB - 1, 2 * pair], tab_ref[NB - 1, 2 * pair + 1])
    feat = jnp.where((row < 4) & (row != seg), -BIG, 0.0)
    feat = jnp.where(row == 4, below, jnp.where(row == 5, above, feat))
    if extra is not None:
        high = extra.astype(jnp.bfloat16).astype(jnp.float32)
        rest = extra - high
        mid = rest.astype(jnp.bfloat16).astype(jnp.float32)
        low = rest - mid
        feat = jnp.where(row == 6, high, jnp.where(row == 7, mid, jnp.where(row == 8, low, feat)))
    return feat.astype(jnp.bfloat16)


def block_diagonal(x_t):
    row = lax.broadcasted_iota(jnp.int32, (128, 128), 0)
    zero = jnp.zeros_like(x_t)
    return jnp.concatenate([jnp.where(row < DH, x_t, zero), jnp.where(row >= DH, x_t, zero)], axis=1)


def stacked_heads(x):
    lane = lax.broadcasted_iota(jnp.int32, (128, 128), 1)
    zero = jnp.zeros_like(x)
    return jnp.concatenate([jnp.where(lane < DH, x, zero), jnp.where(lane >= DH, x, zero)], axis=0)


def near_index(delta):
    return jnp.where((delta >= -1) & (delta <= 1), delta + 1, 3)


def smem():
    return pl.BlockSpec(memory_space=pltpu.SMEM)


def vmem():
    return pl.BlockSpec(memory_space=pltpu.VMEM)


def once():
    return pl.BlockSpec(memory_space=pltpu.VMEM, pipeline_mode=pl.Buffered(1))


def by_chunk():
    return pl.BlockSpec((256, D), lambda t: (t, 0))


def hbm():
    return pl.BlockSpec(memory_space=ANY)


def cost(us):
    return pl.CostEstimate(flops=int(us * 1.0e9), bytes_accessed=int(us * 1.0e6), transcendentals=0)


def load_pieces(pieces, target_ref, flip, sem):
    copies = []
    rows = target_ref.shape[0] // len(pieces)
    for number, (ref, index, place) in enumerate(pieces):
        start = pl.multiple_of(lax.bitwise_xor(jnp.int32(place), flip) * rows, 16)
        source = ref.at[index, pl.ds(0, rows)]
        copies.append(pltpu.make_async_copy(source, target_ref.at[pl.ds(start, rows)], sem.at[number]))
    for copy in copies:
        copy.start()
    return copies


def expand(refs):
    out, place = [], 0
    for ref in refs:
        for index in range(ref.shape[0]):
            out.append((ref, index, place))
            place += 1
    return out


def forward_kernel(counts, *refs):
    n_x, n_w = counts
    ids_ref, order_ref, len_ref, tab_ref, table_t_ref, gain_ref = refs[:6]
    x_refs, w_refs = refs[6 : 6 + n_x], refs[6 + n_x : 6 + n_x + n_w]
    (
        nf_ref, res_ref, o_ref, ot_ref, lse_ref, q_ref, k_out_ref, v_out_ref,
        inv_ref, x_ref, w_ref, k_ref, v_ref, rhs_ref, near_ref, m_ref, l_ref, acc_ref, sem_x, sem_w, sem_k, sem_v,
    ) = refs[6 + n_x + n_w :]
    spans, own = order_ref.shape[1], q_ref.shape[0] // SPAN
    b1 = len_ref[0, 0]
    b2 = b1 + len_ref[0, 1]
    b3 = b2 + len_ref[0, 2]
    copies = load_pieces(expand(x_refs), x_ref, jnp.int32(0), sem_x)
    copies += load_pieces(expand(w_refs), w_ref, ids_ref[2], sem_w)
    fill_inverse(order_ref, inv_ref, spans)
    fill_near_bias(table_t_ref[...], near_ref)
    for copy in copies:
        copy.wait()
    own_rows = own * SPAN
    gain = gain_ref[0:1, :]

    def normed(x):
        x = x.astype(jnp.float32)
        return (x * lax.rsqrt(jnp.mean(x * x, axis=1, keepdims=True) + EPS) * gain).astype(jnp.bfloat16)

    my_spans = [order_ref[0, ids_ref[0] * own + i] for i in range(own)]
    my_ranges = [key_range(span, b1, b2, b3, spans * SPAN) for span in my_spans]

    def chunk_copies(t):
        rows = pl.ds(pl.multiple_of(t * 256, 256), 256)
        return (
            pltpu.make_async_copy(k_ref.at[rows], k_out_ref.at[rows], sem_k.at[t]),
            pltpu.make_async_copy(v_ref.at[rows], v_out_ref.at[rows], sem_v.at[t]),
        )

    def if_needed(t, body):
        needed = jnp.bool_(False)
        for low, high in my_ranges:
            needed = needed | ((t >= low) & (t < high))
        pl.when(needed)(body)

    def project(t, carry):
        def fill():
            rows = pl.ds(pl.multiple_of(t * 256, 256), 256)
            parts = []
            for half in range(2):
                slot = inv_ref[2 * t + half]
                piece = lax.bitwise_xor(slot // own, ids_ref[1])
                start = pl.multiple_of(piece * own_rows + (slot % own) * SPAN, SPAN)
                parts.append(x_ref[pl.ds(start, SPAN), :])
            xn = normed(jnp.concatenate(parts, axis=0))
            k_ref[rows, :] = dot(xn, w_ref[:, D : 2 * D]).astype(jnp.bfloat16)
            v_ref[rows, :] = dot(xn, w_ref[:, 2 * D : 3 * D]).astype(jnp.bfloat16)
            for copy in chunk_copies(t):
                copy.start()

        if_needed(t, fill)
        return carry

    lax.fori_loop(0, spans // 2, project, 0)
    mine = pl.multiple_of(lax.bitwise_xor(ids_ref[0], ids_ref[1]) * own_rows, SPAN)
    x_own = x_ref[pl.ds(mine, own_rows), :]
    q_ref[...] = dot(normed(x_own), w_ref[:, 0:D]).astype(jnp.bfloat16)

    def one_span(i, carry):
        span = order_ref[0, ids_ref[0] * own + i]
        low, high = key_range(span, b1, b2, b3, spans * SPAN)
        my_rows = pl.ds(pl.multiple_of(i * SPAN, SPAN), SPAN)
        for p in range(PAIRS):
            q_t = q_ref[my_rows, p * 128 : p * 128 + 128].T
            rhs_ref[p, 0:128, :] = block_diagonal(q_t)
            rhs_ref[p, 128:256, :] = query_features(span, p, tab_ref, b1, b2, b3)
        m_ref[...] = jnp.full_like(m_ref, -BIG)
        l_ref[...] = jnp.zeros_like(l_ref)
        acc_ref[...] = jnp.zeros_like(acc_ref)

        def chunk_body(t, near):
            rows = pl.ds(pl.multiple_of(t * 256, 256), 256)
            feat = key_features(t, span, b1, b2, b3)

            def scores(p):
                s = dot(jnp.concatenate([k_ref[rows, p * 128 : p * 128 + 128], feat], axis=1), rhs_ref[p])
                if near:
                    n0, n1 = near_index(2 * t - span), near_index(2 * t + 1 - span)
                    s = s + jnp.concatenate([near_ref[n0, p], near_ref[n1, p]], axis=0)
                return s

            def top(p, s):
                old = m_ref[p]
                new = jnp.maximum(old, jnp.max(s, axis=0, keepdims=True))
                m_ref[p] = new
                return new, jnp.exp(old - new)

            def weigh(p, s, new, scale):
                e = jnp.exp(s - new)
                l_ref[p] = l_ref[p] * scale + jnp.sum(e, axis=0, keepdims=True)
                return e.astype(jnp.bfloat16)

            def attend(p, e, scale):
                o = dot(v_ref[rows, p * 128 : p * 128 + 128], e, 0, 0)
                acc_ref[p, 0:64, :] = acc_ref[p, 0:64, :] * scale[:, 0:128] + o[0:64, 0:128]
                acc_ref[p, 64:128, :] = acc_ref[p, 64:128, :] * scale[:, 128:256] + o[64:128, 128:256]

            ss, tops, es = {}, {}, {}
            for p in range(PAIRS + 3):
                if p < PAIRS:
                    ss[p] = scores(p)
                if 1 <= p <= PAIRS:
                    tops[p - 1] = top(p - 1, ss[p - 1])
                if 2 <= p <= PAIRS + 1:
                    es[p - 2] = weigh(p - 2, ss[p - 2], *tops[p - 2])
                if p >= 3:
                    attend(p - 3, es[p - 3], tops[p - 3][1])

        def step(t, carry):
            near = (2 * t + 2 >= span) & (2 * t <= span + 1)
            pl.when(near)(lambda: chunk_body(t, True))
            pl.when(jnp.logical_not(near))(lambda: chunk_body(t, False))
            return carry

        lax.fori_loop(low, high, step, 0)
        for p in range(PAIRS):
            total = l_ref[p]
            lse_ref[i, p] = m_ref[p] + jnp.log(total)
            inv = 1.0 / total
            out = jnp.concatenate(
                [acc_ref[p, 0:64, :] * inv[:, 0:128], acc_ref[p, 64:128, :] * inv[:, 128:256]], axis=0
            )
            ot_ref[i, p] = out
            o_ref[my_rows, p * 128 : p * 128 + 128] = out.T.astype(jnp.bfloat16)
        return carry

    lax.fori_loop(0, own, one_span, 0)
    res = x_own.astype(jnp.float32) + dot(o_ref[...], w_ref[:, 3 * D : 4 * D])
    res_ref[...] = res
    inv_rms = lax.rsqrt(jnp.mean(res * res, axis=1, keepdims=True) + EPS)
    nf_ref[...] = (res * inv_rms * gain_ref[1:2, :]).astype(jnp.bfloat16)

    def settle(t, carry):
        def wait():
            for copy in chunk_copies(t):
                copy.wait()

        if_needed(t, wait)
        return carry

    lax.fori_loop(0, spans // 2, settle, 0)


def forward(ids, order, lengths, table, table_t, gains, xs, ws, local_rows):
    spans, own = order.shape[1], local_rows // SPAN
    rows = spans * SPAN
    n_x, n_w = sum(x.shape[0] for x in xs), sum(w.shape[0] for w in ws)
    bf, f32 = jnp.bfloat16, jnp.float32
    return pl.pallas_call(
        lambda *refs: forward_kernel((len(xs), len(ws)), *refs),
        name="forward",
        cost_estimate=cost(22),
        out_shape=(
            jax.ShapeDtypeStruct((local_rows, D), bf),
            jax.ShapeDtypeStruct((local_rows, D), f32),
            jax.ShapeDtypeStruct((local_rows, D), bf),
            jax.ShapeDtypeStruct((own, PAIRS, 128, 128), f32),
            jax.ShapeDtypeStruct((own, PAIRS, 1, 256), f32),
            jax.ShapeDtypeStruct((local_rows, D), bf),
            jax.ShapeDtypeStruct((rows, D), bf),
            jax.ShapeDtypeStruct((rows, D), bf),
        ),
        in_specs=[smem()] * 4 + [vmem()] * 2 + [hbm()] * (len(xs) + len(ws)),
        out_specs=(vmem(),) * 6 + (hbm(),) * 2,
        scratch_shapes=[
            pltpu.SMEM((spans,), jnp.int32),
            pltpu.VMEM((rows, D), bf),
            pltpu.VMEM((D, 4 * D), bf),
            pltpu.VMEM((rows, D), bf),
            pltpu.VMEM((rows, D), bf),
            pltpu.VMEM((PAIRS, 256, 256), bf),
            pltpu.VMEM((4, PAIRS, 128, 256), f32),
            pltpu.VMEM((PAIRS, 1, 256), f32),
            pltpu.VMEM((PAIRS, 1, 256), f32),
            pltpu.VMEM((PAIRS, 128, 128), f32),
            pltpu.SemaphoreType.DMA((n_x,)),
            pltpu.SemaphoreType.DMA((n_w,)),
            pltpu.SemaphoreType.DMA((spans // 2,)),
            pltpu.SemaphoreType.DMA((spans // 2,)),
        ],
        compiler_params=pltpu.CompilerParams(vmem_limit_bytes=VMEM_LIMIT),
    )(ids, order, lengths, table, table_t, gains, *xs, *ws)


def ffn_kernel(counts, *refs):
    count, n_w = counts
    ids_ref, refs = refs[0], refs[1:]
    nfs, cots, wins = refs[:count], refs[count : 2 * count], refs[2 * count : 2 * count + n_w]
    wffn_ref, act_ref, dup_ref = refs[2 * count + n_w : 2 * count + n_w + 3]
    refs = refs[2 * count + n_w + 3 :]
    dns, outs, (w_ref, sem) = refs[:count], refs[count : 2 * count], refs[2 * count :]
    done = 0
    for copy in load_pieces(expand(wins), w_ref, ids_ref[3], sem):
        copy.wait()
    for nf_ref, cot_ref, dn_ref, out_ref in zip(nfs, cots, dns, outs):
        for piece in range(nf_ref.shape[0]):
            up = dot(nf_ref[piece], w_ref[...])
            d_act = dot(cot_ref[piece], wffn_ref[...], 1, 1)
            square = up * up
            th = jnp.tanh(GELU_C * (up + 0.044715 * square * up))
            half = 0.5 * (1.0 + th)
            act = (up * half).astype(jnp.bfloat16)
            act_ref[done] = act
            slope = half + 0.5 * up * (1.0 - th * th) * (GELU_C * (1.0 + 3 * 0.044715 * square))
            d_up = (d_act * slope).astype(jnp.bfloat16)
            dup_ref[done] = d_up
            dn_ref[piece] = dot(d_up, w_ref[...], 1, 1).astype(jnp.bfloat16)
            out_ref[piece] = dot(act, wffn_ref[...]).astype(jnp.bfloat16)
            done += 1


def ffn(ids, nfs, cots, wins, wffn):
    total, rows, count = sum(n.shape[0] for n in nfs), nfs[0].shape[1], len(nfs)
    width = wffn.shape[0]
    bf = jnp.bfloat16
    act, dup, *rest = pl.pallas_call(
        lambda *refs: ffn_kernel((count, len(wins)), *refs),
        name="ffn",
        cost_estimate=cost(6),
        out_shape=(jax.ShapeDtypeStruct((total, rows, width), bf),) * 2
        + tuple(jax.ShapeDtypeStruct((n.shape[0], rows, D), bf) for n in nfs) * 2,
        in_specs=[smem()] + [vmem()] * (2 * count) + [hbm()] * len(wins) + [vmem()],
        out_specs=(vmem(),) * (2 + 2 * count),
        scratch_shapes=[
            pltpu.VMEM((D, width), bf),
            pltpu.SemaphoreType.DMA((sum(w.shape[0] for w in wins),)),
        ],
        compiler_params=pltpu.CompilerParams(vmem_limit_bytes=VMEM_LIMIT),
    )(ids, *nfs, *cots, *wins, wffn)
    return act, dup, rest[:count], rest[count:]


def by_turn(turn, refs, body):
    for number, ref in enumerate(refs):
        pl.when(turn == number)(lambda ref=ref: body(ref))


def ffn_grads_kernel(counts, parts, *refs):
    n, m = counts
    ids_ref = refs[0]
    groups, start = [], 1
    for count in (n, n, m, m):
        groups.append(refs[start : start + count])
        start += count
    nfs, cots, acts, dups = groups
    outs = refs[start:]

    def joined(pieces):
        flat = [ref[...].reshape(-1, ref.shape[2]) for ref in pieces]
        return flat[0] if len(flat) == 1 else jnp.concatenate(flat, axis=0)

    g_out = dot(joined(acts), joined(cots), 0, 0).astype(jnp.bfloat16)
    g_in = dot(joined(nfs), joined(dups), 0, 0).astype(jnp.bfloat16)
    if parts == 1:
        outs[0][...] = g_out
        size = outs[1].shape[1]
        for i in range(outs[1].shape[0]):
            outs[1][i] = g_in[i * size : (i + 1) * size]
        return
    out_ref, gin_ref = outs
    gin_ref[...] = g_in
    rows = D // parts
    for part in range(parts):
        out_ref[part, 0:rows, :] = g_out[part * rows : (part + 1) * rows]
        side = slice((part % 2) * 384, (part % 2) * 384 + 384)
        for place in range(4):
            owner = lax.bitwise_xor(jnp.int32(place), ids_ref[3])
            down = pl.ds(pl.multiple_of(owner * 192 + (part // 2) * 48, 16), 48)
            first, left = rows + (place // 2) * 48, (place % 2) * 384
            out_ref[part, first : first + 48, left : left + 384] = gin_ref[down, side]


def ffn_grads(ids, nfs, cots, acts, dups, n_fsdp, parts):
    width = acts[0].shape[2]
    bf = jnp.bfloat16
    if parts == 1:
        shapes = (jax.ShapeDtypeStruct((width, D), bf), jax.ShapeDtypeStruct((n_fsdp, D // n_fsdp, width), bf))
    else:
        shapes = (jax.ShapeDtypeStruct((parts, 2 * D // parts, D), bf),)
    scratch = [] if parts == 1 else [pltpu.VMEM((D, width), bf)]
    return pl.pallas_call(
        lambda *refs: ffn_grads_kernel((len(nfs), len(acts)), parts, *refs),
        name="ffn_grads",
        cost_estimate=cost(6),
        out_shape=shapes,
        in_specs=[smem()] + [vmem()] * (2 * len(nfs) + 2 * len(acts)),
        out_specs=(vmem(),) * len(shapes),
        scratch_shapes=scratch,
        compiler_params=pltpu.CompilerParams(vmem_limit_bytes=VMEM_LIMIT),
    )(ids, *nfs, *cots, *acts, *dups)


def fetch_turns(pieces, all_ref, flip, sem):
    copies = []
    for number, (ref, index, turn) in enumerate(pieces):
        place = lax.bitwise_xor(jnp.int32(turn), flip)
        copies.append(pltpu.make_async_copy(ref.at[index], all_ref.at[place], sem.at[number]))
    for copy in copies:
        copy.start()
    for copy in copies:
        copy.wait()


def with_turns(refs, turns):
    return [(ref, index, turn) for ref, group in zip(refs, turns) for index, turn in enumerate(group)]


def finish_ffn_kernel(turns, *refs):
    count = len(turns)
    ids_ref = refs[0]
    gout_ref, gin_ref, all_ref, sem = refs[1 + count :]
    fetch_turns(with_turns(refs[1 : 1 + count], turns), all_ref, ids_ref[1], sem)
    rows = all_ref.shape[1] // 2
    for p in range(all_ref.shape[0]):
        gout_ref[p * rows : (p + 1) * rows, :] = all_ref[p, 0:rows, :].astype(jnp.float32)
        for i in range(4):
            place = lax.bitwise_xor(jnp.int32(i), ids_ref[3])
            down = pl.ds(pl.multiple_of(rows + (place // 2) * 48, 16), 48)
            side = pl.ds(pl.multiple_of((place % 2) * 384, 128), 384)
            first = i * D + (p % 2) * 384
            gin_ref[(p // 2) * 48 : (p // 2) * 48 + 48, first : first + 384] = all_ref[p, down, side].astype(jnp.float32)


def finish_ffn(ids, arrays, turns):
    f32 = jnp.float32
    count = sum(a.shape[0] for a in arrays)
    return pl.pallas_call(
        lambda *refs: finish_ffn_kernel(turns, *refs),
        name="finish_ffn",
        cost_estimate=cost(4),
        out_shape=(jax.ShapeDtypeStruct((D, D), f32), jax.ShapeDtypeStruct((D // 4, 4 * D), f32)),
        in_specs=[smem()] + [hbm()] * len(arrays),
        out_specs=(vmem(),) * 2,
        scratch_shapes=[pltpu.VMEM((count, *arrays[0].shape[1:]), jnp.bfloat16), pltpu.SemaphoreType.DMA((count,))],
        compiler_params=pltpu.CompilerParams(vmem_limit_bytes=VMEM_LIMIT),
    )(ids, *arrays)


def put_grads(outs, all_ref, size, part_flip, fsdp_flip):
    n, parts, wide = sum(ref.shape[0] for ref in outs), outs[0].shape[1], outs[0].shape[3]
    for turn in range(n):
        owner = lax.bitwise_xor(jnp.int32(turn), fsdp_flip)
        rows = pl.ds(pl.multiple_of(owner * size, 16), size)
        for part in range(parts):
            source = lax.bitwise_xor(jnp.int32(part), part_flip)
            columns = pl.ds(pl.multiple_of(source * wide, 128), wide)
            outs[turn % len(outs)][turn // len(outs), part, 0:size, :] = all_ref[rows, columns].astype(jnp.bfloat16)


def grad_shapes(n, parts):
    high, wide = D // n + 16, 2 * D // parts
    if parts == 1:
        return (jax.ShapeDtypeStruct((n, parts, high, wide), jnp.bfloat16),)
    return (jax.ShapeDtypeStruct((n // 2, parts, high, wide), jnp.bfloat16),) * 2


def finish_kernel(turns, *refs):
    count = len(turns)
    ids_ref = refs[0]
    outs, tiny_ref, all_ref, sem = refs[1 + count : 5 + count], refs[5 + count], refs[6 + count], refs[7 + count]
    fetch_turns(with_turns(refs[1 : 1 + count], turns), all_ref, ids_ref[1], sem)
    size, wide = outs[0].shape[0], all_ref.shape[2]
    step = min(D, wide)
    for first in range(0, 4 * D, step):
        value = all_ref[first // wide, :, first % wide : first % wide + step].astype(jnp.float32)
        outs[first // D][:, first % D : first % D + step] = value[0:size]
        tiny_ref[:, first : first + step] = value[size : size + 16]


def finish(ids, arrays, turns):
    count, high, wide = sum(a.shape[0] for a in arrays), *arrays[0].shape[1:]
    f32 = jnp.float32
    return pl.pallas_call(
        lambda *refs: finish_kernel(turns, *refs),
        name="finish",
        cost_estimate=cost(3),
        out_shape=(jax.ShapeDtypeStruct((high - 16, D), f32),) * 4 + (jax.ShapeDtypeStruct((16, 4 * D), f32),),
        in_specs=[smem()] + [hbm()] * len(arrays),
        out_specs=(vmem(),) * 5,
        scratch_shapes=[pltpu.VMEM((count, high, wide), jnp.bfloat16), pltpu.SemaphoreType.DMA((count,))],
        compiler_params=pltpu.CompilerParams(vmem_limit_bytes=VMEM_LIMIT),
    )(ids, *arrays)


def backward_kernel(counts, *refs):
    n_x, n_w, n_dn, n_grad = counts
    (
        ids_ref, order_ref, len_ref, tab_ref, table_t_ref, gain_ref,
        dnf_ref, res_ref, cot_ref, o_ref, ot_ref, lse_ref, q_ref, k_ref, v_ref,
    ) = refs[:15]
    x_refs, w_refs = refs[15 : 15 + n_x], refs[15 + n_x : 15 + n_x + n_w]
    refs = refs[15 + n_x + n_w :]
    dn_refs, mine_refs, shared_refs = refs[:n_dn], refs[n_dn : n_dn + n_grad], refs[n_dn + n_grad : n_dn + 2 * n_grad]
    (
        dres_ref, dn_own_ref,
        dlow_ref, dq_ref, dgain_ref, own_ref, all_ref, inv_ref, x_ref, w_ref, do_ref, rhs_ref, dorhs_ref, qbd_ref, dobd_ref, near_ref, nacc_ref, acc_ref, far_ref,
        dkacc_ref, dvacc_ref, kt_ref, sem_x, sem_w,
    ) = refs[n_dn + 2 * n_grad :]
    spans, own = order_ref.shape[1], q_ref.shape[0] // SPAN
    own_rows = own * SPAN
    b1 = len_ref[0, 0]
    b2 = b1 + len_ref[0, 1]
    b3 = b2 + len_ref[0, 2]
    t = pl.program_id(0)

    @pl.when(t == 0)
    def begin():
        copies_x = load_pieces(expand(x_refs), x_ref, jnp.int32(0), sem_x)
        copies_w = load_pieces(expand(w_refs), w_ref, ids_ref[2], sem_w)
        fill_inverse(order_ref, inv_ref, spans)
        fill_near_bias(table_t_ref[...], near_ref)
        nacc_ref[...] = jnp.zeros_like(nacc_ref)
        far_ref[...] = jnp.zeros_like(far_ref)

        res, dnf = res_ref[...], dnf_ref[...]
        inv_rms = lax.rsqrt(jnp.mean(res * res, axis=1, keepdims=True) + EPS)
        dgain_ref[...] = jnp.zeros_like(dgain_ref)
        dgain_ref[1:2, :] = jnp.sum(dnf * res * inv_rms, axis=0, keepdims=True)
        scaled = dnf * gain_ref[1:2, :]
        inner = jnp.mean(scaled * res, axis=1, keepdims=True)
        dres = cot_ref[...].astype(jnp.float32) + inv_rms * scaled - res * (inv_rms * inv_rms * inv_rms * inner)
        dres_ref[...] = dres
        dlow = dres.astype(jnp.bfloat16)
        dlow_ref[...] = dlow
        for copy in copies_w:
            copy.wait()
        do_ref[...] = dot(dlow, w_ref[:, 3 * D : 4 * D], 1, 1).astype(jnp.bfloat16)
        own_ref[:, D : 2 * D] = dot(o_ref[...], dlow, 0, 0)
        all_ref[...] = jnp.zeros_like(all_ref)

        def prepare(i, carry):
            span = order_ref[0, ids_ref[0] * own + i]
            my_rows = pl.ds(pl.multiple_of(i * SPAN, SPAN), SPAN)
            for p in range(PAIRS):
                cols = slice(p * 128, p * 128 + 128)
                qp, dop = q_ref[my_rows, cols], do_ref[my_rows, cols]
                do_t = dop.T
                prod = do_t.astype(jnp.float32) * ot_ref[i, p]
                neg = -jnp.concatenate(
                    [jnp.sum(prod[0:64], axis=0, keepdims=True), jnp.sum(prod[64:128], axis=0, keepdims=True)], axis=1
                )
                rhs_ref[i, p, 0:128, :] = block_diagonal(qp.T)
                rhs_ref[i, p, 128:256, :] = query_features(span, p, tab_ref, b1, b2, b3, -lse_ref[i, p])
                row = lax.broadcasted_iota(jnp.int32, (128, 256), 0)
                h1 = neg.astype(jnp.bfloat16).astype(jnp.float32)
                h2 = (neg - h1).astype(jnp.bfloat16).astype(jnp.float32)
                h3 = neg - h1 - h2
                dfeat = jnp.where(row == 6, h1, jnp.where(row == 7, h2, jnp.where(row == 8, h3, 0.0)))
                dorhs_ref[i, p, 0:128, :] = block_diagonal(do_t)
                dorhs_ref[i, p, 128:256, :] = dfeat.astype(jnp.bfloat16)
                qbd_ref[i, p] = stacked_heads(qp)
                dobd_ref[i, p] = stacked_heads(dop)
            return carry

        lax.fori_loop(0, own, prepare, 0)
        acc_ref[...] = jnp.zeros_like(acc_ref)
        for copy in copies_x:
            copy.wait()


    def unit(x):
        x = x.astype(jnp.float32)
        return x * lax.rsqrt(jnp.mean(x * x, axis=1, keepdims=True) + EPS)

    dkacc_ref[...] = jnp.zeros_like(dkacc_ref)
    dvacc_ref[...] = jnp.zeros_like(dvacc_ref)
    for p in range(PAIRS):
        kt_ref[p, 0:128, :] = k_ref[:, p * 128 : p * 128 + 128].T

    def span_body(i, span, near):
        feat = key_features(t, span, b1, b2, b3)
        for p in range(PAIRS):
            kt_ref[p, 128:144, :] = feat.T[0:16]

        def first(p):
            cols = slice(p * 128, p * 128 + 128)
            return (
                dot(jnp.concatenate([k_ref[:, cols], feat], axis=1), rhs_ref[i, p]),
                dot(jnp.concatenate([v_ref[:, cols], feat], axis=1), dorhs_ref[i, p]),
            )

        def last(p, prob, ds):
            cols = slice(p * 128, p * 128 + 128)
            dvacc_ref[:, cols] += dot(prob, dobd_ref[i, p])
            dkacc_ref[:, cols] += dot(ds, qbd_ref[i, p])
            dq = dot(kt_ref[p], ds)
            acc_ref[i, p, 0:64, :] += dq[0:64, 0:128]
            acc_ref[i, p, 64:128, :] += dq[64:128, 128:256]
            far_ref[p] += dq[128:136, :]

        ahead, waiting = first(0), None
        for p in range(PAIRS):
            s, dp = ahead
            if p + 1 < PAIRS:
                ahead = first(p + 1)
            if near:
                n0, n1 = near_index(2 * t - span), near_index(2 * t + 1 - span)
                s = s + jnp.concatenate([near_ref[n0, p], near_ref[n1, p]], axis=0)
            prob = jnp.exp(s)
            ds = prob * dp
            if near:
                nacc_ref[n0, p] += ds[0:128]
                nacc_ref[n1, p] += ds[128:256]
            if waiting is not None:
                last(*waiting)
            waiting = (p, prob.astype(jnp.bfloat16), ds.astype(jnp.bfloat16))
        last(*waiting)

    def one_span(i, used):
        span = order_ref[0, ids_ref[0] * own + i]
        low, high = key_range(span, b1, b2, b3, spans * SPAN)
        needed = (t >= low) & (t < high)
        near = (2 * t + 2 >= span) & (2 * t <= span + 1)
        pl.when(needed & near)(lambda: span_body(i, span, True))
        pl.when(needed & jnp.logical_not(near))(lambda: span_body(i, span, False))
        return used + needed.astype(jnp.int32)

    used = lax.fori_loop(0, own, one_span, jnp.int32(0))
    places, targets = [], []
    for half in range(2):
        slot = inv_ref[2 * t + half]
        piece = lax.bitwise_xor(slot // own, ids_ref[1])
        inside = (slot % own) * SPAN
        places.append(pl.ds(pl.multiple_of(piece * own_rows + inside, SPAN), SPAN))
        targets.append((piece, inside))

    def store(half, value):
        piece, inside = targets[half]

        def put(ref, index):
            ref[pl.ds(pl.multiple_of(index * own_rows + inside, SPAN), SPAN), :] = value

        if n_dn == 1:
            put(dn_refs[0], piece)
        else:
            by_turn(piece, dn_refs, lambda ref: put(ref, 0))

    def fill():
        dkb, dvb = dkacc_ref[...].astype(jnp.bfloat16), dvacc_ref[...].astype(jnp.bfloat16)
        part = dot(dkb, w_ref[:, D : 2 * D], 1, 1) + dot(dvb, w_ref[:, 2 * D : 3 * D], 1, 1)
        x = unit(jnp.concatenate([x_ref[places[0], :], x_ref[places[1], :]], axis=0))
        dgain_ref[0:1, :] += jnp.sum(part * x, axis=0, keepdims=True)
        turned = (x * gain_ref[0:1, :]).astype(jnp.bfloat16).T
        all_ref[:, 0:D] += dot(turned, dkb)
        all_ref[:, D : 2 * D] += dot(turned, dvb)
        part = part.astype(jnp.bfloat16)
        store(0, part[0:128])
        store(1, part[128:256])

    def skip():
        zero = jnp.zeros((256, D), jnp.bfloat16)
        store(0, zero[0:128])
        store(1, zero[0:128])

    pl.when(used > 0)(fill)
    pl.when(used == 0)(skip)


    @pl.when(t == spans // 2 - 1)
    def finish():
        for i in range(own):
            for p in range(PAIRS):
                dq_ref[i * SPAN : (i + 1) * SPAN, p * 128 : p * 128 + 128] = acc_ref[i, p].T.astype(jnp.bfloat16)
        mine = pl.multiple_of(lax.bitwise_xor(ids_ref[0], ids_ref[1]) * own_rows, SPAN)
        own_part = dot(dq_ref[...], w_ref[:, 0:D], 1, 1)
        dn_own_ref[...] = own_part
        x_own = unit(x_ref[pl.ds(mine, own_rows), :])
        dgain_ref[0:1, :] += jnp.sum(own_part * x_own, axis=0, keepdims=True)
        own_ref[:, 0:D] = dot((x_own * gain_ref[0:1, :]).astype(jnp.bfloat16), dq_ref[...], 0, 0)
        parts, tall = mine_refs[0].shape[1:3]
        size, part_flip = tall - 16, ids_ref[1] & (parts - 1)
        put_grads(mine_refs, own_ref, size, part_flip, ids_ref[3])
        put_grads(shared_refs, all_ref, size, part_flip, ids_ref[3])

        row16 = lax.broadcasted_iota(jnp.int32, (16, 128), 0)
        lane16 = lax.broadcasted_iota(jnp.int32, (16, 128), 1)
        grad = jnp.zeros((16, 128), jnp.float32)
        for head in range(H):
            half = slice((head % 2) * 128, (head % 2) * 128 + 128)
            sums = jnp.sum(far_ref[head // 2, 4:6, half], axis=1, keepdims=True)
            grad = grad + jnp.where((row16 == head) & (lane16 == NB // 2 - 1), sums[0:1], 0.0)
            grad = grad + jnp.where((row16 == head) & (lane16 == NB - 1), sums[1:2], 0.0)
        rowd = lax.broadcasted_iota(jnp.int32, (16, 256), 0)
        flip_row = lax.broadcasted_iota(jnp.int32, (128, 128), 0)
        flip_lane = lax.broadcasted_iota(jnp.int32, (128, 128), 1)
        flip = (flip_row + flip_lane == 127).astype(jnp.bfloat16)
        for index in range(3):
            sums = jnp.zeros((16, 256), jnp.float32)
            for p in range(PAIRS):
                both = nacc_ref[index, p]
                high = both.astype(jnp.bfloat16)
                rest = (both - high.astype(jnp.float32)).astype(jnp.bfloat16)
                turned = dot(flip, high) + dot(flip, rest)
                for side in range(2):
                    tile = turned[:, side * 128 : side * 128 + 128]
                    wide = jnp.concatenate([tile, jnp.zeros_like(tile)], axis=1)
                    shifted = pltpu.roll(wide, 0, 1, stride=1, stride_axis=0)
                    sums = sums + jnp.where(rowd == 2 * p + side, jnp.sum(shifted, axis=0, keepdims=True), 0.0)
            hot = diagonal_onehot(index - 1).astype(jnp.float32)
            grad = grad + lax.dot_general(
                sums, hot, (((1,), (1,)), ((), ())), preferred_element_type=jnp.float32, precision=lax.Precision.HIGHEST
            )
        wide = mine_refs[0].shape[3]
        own_ref[0:1, 0:D] = dgain_ref[0:1, :]
        own_ref[0:1, D : 2 * D] = dgain_ref[1:2, :]
        own_ref[1:16, :] = jnp.zeros((15, 2 * D), jnp.float32)
        own_ref[16:32, :] = jnp.concatenate([grad, jnp.zeros((16, 2 * D - 128), jnp.float32)], axis=1)
        for refs, top in ((mine_refs, 0), (shared_refs, 16)):
            for part in range(parts):
                columns = pl.ds(pl.multiple_of(lax.bitwise_xor(jnp.int32(part), part_flip) * wide, 128), wide)
                value = own_ref[top : top + 16, columns].astype(jnp.bfloat16)
                for ref in refs:
                    for index in range(ref.shape[0]):
                        ref[index, part, size:tall, :] = value


def backward(ids, order, lengths, table, table_t, gains, dnf, res, cot, o, ot, lse, q, k, v, xs, ws, n_dn, n_fsdp):
    spans, local_rows = order.shape[1], q.shape[0]
    rows, own = spans * SPAN, local_rows // SPAN
    n_x, n_w = sum(x.shape[0] for x in xs), sum(w.shape[0] for w in ws)
    bf, f32 = jnp.bfloat16, jnp.float32
    shapes = grad_shapes(n_fsdp, 1 if n_dn == 1 else 4)
    return pl.pallas_call(
        lambda *refs: backward_kernel((len(xs), len(ws), n_dn, len(shapes)), *refs),
        name="backward",
        cost_estimate=cost(36),
        grid=(spans // 2,),
        out_shape=(jax.ShapeDtypeStruct((rows // n_dn, D), bf),) * n_dn
        + shapes * 2
        + (jax.ShapeDtypeStruct((local_rows, D), f32),) * 2,
        in_specs=[smem()] * 4 + [once()] * 9 + [by_chunk()] * 2 + [hbm()] * (len(xs) + len(ws)),
        out_specs=(once(),) * (n_dn + 2 * len(shapes) + 2),
        scratch_shapes=[
            pltpu.VMEM((local_rows, D), bf),
            pltpu.VMEM((local_rows, D), bf),
            pltpu.VMEM((8, D), f32),
            pltpu.VMEM((D, 2 * D), f32),
            pltpu.VMEM((D, 2 * D), f32),
            pltpu.SMEM((spans,), jnp.int32),
            pltpu.VMEM((rows, D), bf),
            pltpu.VMEM((D, 4 * D), bf),
            pltpu.VMEM((local_rows, D), bf),
            pltpu.VMEM((own, PAIRS, 256, 256), bf),
            pltpu.VMEM((own, PAIRS, 256, 256), bf),
            pltpu.VMEM((own, PAIRS, 256, 128), bf),
            pltpu.VMEM((own, PAIRS, 256, 128), bf),
            pltpu.VMEM((4, PAIRS, 128, 256), f32),
            pltpu.VMEM((4, PAIRS, 128, 256), f32),
            pltpu.VMEM((own, PAIRS, 128, 128), f32),
            pltpu.VMEM((PAIRS, 8, 256), f32),
            pltpu.VMEM((256, D), f32),
            pltpu.VMEM((256, D), f32),
            pltpu.VMEM((PAIRS, 144, 256), bf),
            pltpu.SemaphoreType.DMA((n_x,)),
            pltpu.SemaphoreType.DMA((n_w,)),
        ],
        compiler_params=pltpu.CompilerParams(vmem_limit_bytes=VMEM_LIMIT),
    )(ids, order, lengths, table, table_t, gains, dnf, res, cot, o, ot, lse, q, k, v, *xs, *ws)


def swap(x, axis, bit):
    count = lax.axis_size(axis)
    return lax.ppermute(x, axis, [(i, i ^ bit) for i in range(count)])


def hop(x, pairs):
    return lax.ppermute(x, "ctx", [(2 * a + i, 2 * b + i) for a, b in pairs for i in range(2)])


def block(x, index, count, dim=0):
    size = x.shape[dim] // count
    return lax.dynamic_slice_in_dim(x, index * size, size, dim)


def after(x, *others):
    return lax.optimization_barrier((x,) + others)[0]


def add(*terms):
    total = terms[0].astype(jnp.float32)
    for term in terms[1:]:
        total = total + term.astype(jnp.float32)
    return total.astype(jnp.bfloat16)


def gather_four(x):
    across = swap(x, "fsdp", 2)
    return [x, swap(x, "fsdp", 1), across, swap(across, "fsdp", 1)]


def scatter_four(pieces):
    first, third = swap(pieces[1], "fsdp", 1), swap(pieces[3], "fsdp", 1)
    far = add(pieces[2], third)
    return pieces[0], first, swap(far, "fsdp", 2), far


def scatter_pairs(keep, send):
    got = swap(send, "fsdp", 1)
    return keep[0], got[0], swap(add(keep[1], got[1]), "fsdp", 2)


TURNS = ((0,), (1,), (2, 6), (3, 7), (4,), (5,))


def tail(dn, mine, shared, ffn_own, high):
    g7, g3 = swap(dn[7], "ctx", 1), swap(dn[3], "ctx", 1)
    ffn4 = swap(ffn_own, "ctx", 4)
    mine, shared = (add(*scatter_pairs(*g)) for g in (mine, shared))
    g5, g1 = swap(after(dn[5], g7), "ctx", 1), swap(after(dn[1], g3), "ctx", 1)
    n4 = swap(add(dn[6], g7), "ctx", 2)
    ffn_pair = swap(jnp.concatenate([ffn_own, ffn4]), "ctx", 2)
    n0 = swap(after(add(dn[2], g3), n4), "ctx", 2)
    mine, shared = after((mine, shared), g5, n4)
    low_half, high_half = jnp.where(high, shared, mine), jnp.where(high, mine, shared)
    p = [jnp.stack([low_half[r], high_half[r]]) for r in range(4)]
    a = swap(p[3], "ctx", 1)
    b = swap(after(p[1], g1), "ctx", 1)
    near = swap(add(p[2], a), "ctx", 2)
    ffn1 = swap(after(ffn_own, a), "ctx", 1)
    half = after(add(p[0], b, near), ffn_pair)
    ffn5 = swap(after(ffn4, b), "ctx", 1)
    own = add(half[0], swap(half[1], "ctx", 4))[None]
    ffn_others = swap(after(ffn_pair, near, ffn1), "ctx", 1)
    own4 = swap(own, "ctx", 4)
    own1 = swap(after(own, ffn5), "ctx", 1)
    pair = swap(jnp.concatenate([own, own4]), "ctx", 2)
    own5 = swap(after(own4, own1), "ctx", 1)
    others = swap(after(pair, ffn_others, own5), "ctx", 1)
    far = swap(after(add(dn[4], g5, n4), own4), "ctx", 4)
    return (
        (dn[0], g1, n0, far),
        [ffn_own, ffn1, ffn_pair, ffn_others, ffn4, ffn5],
        [own, own1, pair, others, own4, own5],
    )


def line_gather(x, x1, early):
    line = lax.axis_index("ctx") // 2
    up1, down1 = hop(x, [(0, 1), (1, 2), (2, 3)]), hop(x, [(3, 2), (2, 1), (1, 0)])
    z1 = jnp.where(line % 2 == 0, down1, up1)
    z1, up1, down1 = after((z1, up1, down1), x1)
    x3 = swap(z1, "ctx", 1)
    up2, down2 = hop(up1, [(1, 2), (2, 3)]), hop(down1, [(2, 1), (1, 0)])
    z2 = jnp.where(line < 2, down2, up2)
    z2, up2, down2 = after((z2, up2, down2), x3, early)
    x5 = swap(z2, "ctx", 1)
    far = hop(jnp.where(line == 2, up2, down2), [(2, 3), (1, 0)])
    z3 = jnp.where(line == 1, down1, jnp.where(line == 2, up1, far))
    return [x, x1, z1, x3, z2, x5, z3, swap(after(z3, x5), "ctx", 1)], x3, x5


def on_device(
    tokens,
    lengths,
    span_order,
    w_query,
    w_key,
    w_value,
    w_out,
    w_in,
    w_ffn_out,
    gain_attn,
    gain_ffn,
    rel_table,
    cotangent,
):
    n_ctx, n_fsdp = lax.axis_size("ctx"), lax.axis_size("fsdp")
    fast = n_ctx == 8 and n_fsdp == 4
    place = lax.axis_index("ctx").astype(jnp.int32)
    shard = lax.axis_index("fsdp").astype(jnp.int32)
    local_rows = tokens.shape[1]
    own_rows = w_query.shape[0]
    bf, f32 = jnp.bfloat16, jnp.float32
    x, cot = tokens[0], cotangent[0]
    width = w_ffn_out.shape[0]
    table_size = rel_table.size
    small = jnp.concatenate([gain_attn, gain_ffn, rel_table.reshape(-1)])
    small = jnp.pad(small[None], ((0, 15), (0, 4 * D - small.shape[0])))
    weights = jnp.concatenate([jnp.concatenate([w_query, w_key, w_value, w_out], axis=1), small], axis=0)

    if fast:
        ids = jnp.stack([place, place, shard, shard, jnp.int32(n_ctx)])
        order = [shard ^ r for r in range(4)]
        tokens_got = swap(x, "ctx", 1)
        w2 = swap(weights, "fsdp", 2)
        w1 = swap(after(weights, tokens_got), "fsdp", 1)
        gathered, third, fifth = line_gather(x, tokens_got, w1)
        xs = [p[None] for p in gathered]
        w3 = swap(after(w2, third), "fsdp", 1)
        ws = [p[None] for p in (weights, w1, w2, w3)]
        w_in, cot_late = after((w_in, cot), third)
        columns = [block(w_in, order[r], 4, 1) for r in range(4)]
        side = swap(jnp.stack([columns[1], columns[3]]), "fsdp", 1)
        smalls = jnp.stack([p[own_rows] for p in (weights, w1, w2, w3)])
        smalls = jnp.stack([lax.dynamic_index_in_dim(smalls, order[i], 0, False) for i in range(4)])
        win2 = swap(after(jnp.stack([columns[2], side[1]]), w2), "fsdp", 2)
        wins = [columns[0][None], side[:1], win2]
        cot1 = swap(after(cot, fifth), "fsdp", 1)
        cot2 = swap(after(cot_late, w2), "fsdp", 2)
        cots = [p[None] for p in (cot, cot1, cot2, swap(cot2, "fsdp", 1))]
    else:
        ids = jnp.stack([place, jnp.int32(0), jnp.int32(0), jnp.int32(0), jnp.int32(n_ctx)])
        xs = [lax.all_gather(x, "ctx", axis=0)]
        ws = [lax.all_gather(weights, "fsdp", axis=0)]
        smalls = ws[0][:, own_rows]
        parts = jnp.stack([w_in[:, i * width : (i + 1) * width] for i in range(n_fsdp)])
        wins = [lax.all_to_all(parts, "fsdp", 0, 0)]
        cots = [lax.all_gather(cot, "fsdp", axis=0)]

    gains = jnp.stack([smalls[:, :own_rows].reshape(D), smalls[:, own_rows : 2 * own_rows].reshape(D)]).astype(f32)
    table_bf = smalls[:, 2 * own_rows : 2 * own_rows + table_size].reshape(NB, H)
    table = table_bf.astype(f32)
    table_t = jnp.pad(table_bf.T, ((0, 16 - H), (0, 128 - NB)))

    nf, res, o, ot, lse, q, k, v = forward(
        ids, span_order, lengths, table, table_t, gains, xs, ws, local_rows
    )

    if fast:
        nfs = [nf[None], swap(nf, "fsdp", 1)[None], swap(nf, "fsdp", 2)[None]]
        halves = [ffn(ids, nfs[:2], cots[:2], wins, w_ffn_out)]
        nfs.append(swap(after(nfs[2], halves[0][0]), "fsdp", 1))
        halves.append(ffn(ids, nfs[2:], cots[2:], wins, w_ffn_out))
    else:
        nfs = [lax.all_gather(nf, "fsdp", axis=0)]
        halves = [ffn(ids, nfs, cots, wins, w_ffn_out)]
    acts, dups = [h[0] for h in halves], [h[1] for h in halves]
    dns, outs = [d for h in halves for d in h[2]], [d for h in halves for d in h[3]]
    if fast:
        a, b, c, far = scatter_four([p[0] for p in dns])
        dnf = a.astype(f32) + b.astype(f32) + c.astype(f32)
        ffn_parts = ffn_grads(ids, nfs, cots, after(acts, far), dups, n_fsdp, 8)
        dnf = after(dnf, *ffn_parts)
        ffn_got = lax.all_to_all(after(ffn_parts[0], c), "ctx", 0, 0)
    else:
        dnf = lax.psum_scatter(dns[0], "fsdp", scatter_dimension=0).astype(f32)
        grad_ffn_out, grad_in = ffn_grads(ids, nfs, cots, acts, dups, n_fsdp, 1)
        grad_in = jnp.transpose(lax.all_to_all(grad_in, "fsdp", 0, 0), (1, 0, 2)).reshape(own_rows, n_fsdp * width)
        grad_ffn_out, grad_in = (lax.psum(g, "ctx").astype(f32) for g in (grad_ffn_out, grad_in))
    if fast:
        *out_terms, out_far = scatter_four([p[0] for p in outs])
        dnf = after(dnf, out_terms[1], out_far)
    else:
        out_terms = [lax.psum_scatter(outs[0], "fsdp", scatter_dimension=0)]

    *got, dres, dn_own = backward(
        ids, span_order, lengths, table, table_t, gains, dnf, res, cot, o, ot, lse, q, k, v, xs, ws,
        8 if fast else 1, n_fsdp,
    )
    if fast:
        got = after(got, ffn_got, *out_terms)
        dn, mine, shared = got[:8], got[8:10], got[10:12]
        ffn_own = jnp.sum(ffn_got.astype(f32), axis=0).astype(bf)
        blocks = ffn_own[D // 8 :]
        blocks = [blocks[48 * (r // 2) : 48 * (r // 2) + 48, 384 * (r % 2) : 384 * (r % 2) + 384] for r in range(4)]
        side = swap(jnp.stack([blocks[1], blocks[3]]), "fsdp", 1)
        across = swap(jnp.stack([blocks[2], side[1]]), "fsdp", 2)
        ffn_own = jnp.concatenate(
            [ffn_own[: D // 8], jnp.concatenate([blocks[0], side[0]], axis=1),
             jnp.concatenate([across[0], across[1]], axis=1)]
        )
        terms, ffn_all, grads = tail(dn, mine, shared, ffn_own[None], place >= 4)
        d_normed = dn_own
        for term in terms:
            d_normed = d_normed + term.astype(f32)
        grad_ffn_out, grad_in = finish_ffn(ids, ffn_all, TURNS)
    else:
        d_normed = dn_own + lax.psum_scatter(got[0].reshape(n_ctx, local_rows, D), "ctx", scatter_dimension=0).astype(f32)
        grads = [lax.psum(lax.psum_scatter(g, "fsdp", scatter_dimension=0), "ctx") for g in got[1:]]
    g_query, g_out, g_key, g_value, tiny = finish(ids, grads, TURNS if fast else ((0,), (1,)))
    table_row = tiny[:H, 2 * D : 2 * D + NB].T

    output = res
    for term in out_terms:
        output = output + term.astype(f32)
    output = output.astype(bf)
    xf = x.astype(f32)
    inv_rms = lax.rsqrt(jnp.mean(xf * xf, axis=1, keepdims=True) + EPS)
    scaled = d_normed * gains[0:1]
    inner = jnp.mean(scaled * xf, axis=1, keepdims=True)
    grad_tokens = (dres + inv_rms * scaled - xf * (inv_rms * inv_rms * inv_rms * inner)).astype(bf)
    return (
        output[None],
        grad_tokens[None],
        g_query,
        g_key,
        g_value,
        g_out,
        grad_in,
        grad_ffn_out,
        block(tiny[0, :D], shard, n_fsdp),
        block(tiny[0, D : 2 * D], shard, n_fsdp),
        block(table_row, shard, n_fsdp),
    )


def solution(mesh):
    rows, vector, whole = P("fsdp", None), P("fsdp"), P("fsdp", "ctx", None)
    return jax.shard_map(
        on_device,
        mesh=mesh,
        in_specs=(whole,) + (rows,) * 8 + (vector, vector, rows, whole),
        out_specs=(whole, whole) + (rows,) * 6 + (vector, vector, rows),
        check_vma=False,
    )
```

```python
import jax
import jax.numpy as jnp
from jax import lax
from jax.experimental import pallas as pl
from jax.experimental.pallas import tpu as pltpu
from jax.sharding import PartitionSpec as P

D = 768
H = 12
DH = 64
NB = 32
SPAN = 128
PAIRS = H // 2
BIG = 1e30
VMEM_LIMIT = 56 * 2**20
EPS = 1e-06
GELU_C = 0.7978845608028654
ANY = pl.ANY


def bucket_of(relative):
    distance = jnp.abs(relative)
    far_steps = jnp.zeros_like(distance)
    for exponent in range(1, 8):
        far_steps = far_steps + (distance * distance >= 64 * 2**exponent).astype(jnp.int32)
    magnitude = jnp.where(distance < 8, distance, 8 + far_steps)
    return magnitude + jnp.where(relative > 0, 16, 0).astype(jnp.int32)


def dot(a, b, ca=1, cb=0):
    return lax.dot_general(a, b, (((ca,), (cb,)), ((), ())), preferred_element_type=jnp.float32)


def diagonal_onehot(offset):
    lane = lax.broadcasted_iota(jnp.int32, (128, 256), 1)
    row = lax.broadcasted_iota(jnp.int32, (128, 256), 0)
    return (bucket_of(offset * SPAN + 127 - lane) == row).astype(jnp.bfloat16)


def fill_inverse(order_ref, inv_ref, spans):
    def put(i, carry):
        inv_ref[order_ref[0, i]] = i
        return carry

    lax.fori_loop(0, spans, put, 0)


def fill_near_bias(table_t, near_ref):
    for index in range(3):
        rows = dot(table_t, diagonal_onehot(index - 1))
        for head in range(H):
            wide = jnp.broadcast_to(rows[head : head + 1, :], (128, 256))
            tile = pltpu.roll(wide, 129, 1, stride=1, stride_axis=0)[:, :128]
            near_ref[index, head // 2, :, (head % 2) * 128 : (head % 2) * 128 + 128] = tile
    near_ref[3] = jnp.zeros_like(near_ref[3])


def key_range(span, b1, b2, b3, total):
    first, last = span * SPAN, span * SPAN + SPAN - 1
    start = jnp.where(first >= b3, b3, jnp.where(first >= b2, b2, jnp.where(first >= b1, b1, 0)))
    end = jnp.where(last < b1, b1, jnp.where(last < b2, b2, jnp.where(last < b3, b3, total)))
    return start // 256, (end + 255) // 256


def key_features(chunk, span, b1, b2, b3):
    lane = lax.broadcasted_iota(jnp.int32, (256, 128), 1)
    pos = lax.broadcasted_iota(jnp.int32, (256, 128), 0) + chunk * 256
    seg = (pos >= b1).astype(jnp.int32) + (pos >= b2).astype(jnp.int32) + (pos >= b3).astype(jnp.int32)
    code = jnp.where(pos < (span - 1) * SPAN, 4, jnp.where(pos >= (span + 2) * SPAN, 5, seg))
    hot = (lane == seg) | (lane == code) | ((lane >= 6) & (lane < 9))
    return jnp.where(hot, 1.0, 0.0).astype(jnp.bfloat16)


def query_features(span, pair, tab_ref, b1, b2, b3, extra=None):
    row = lax.broadcasted_iota(jnp.int32, (128, 256), 0)
    lane = lax.broadcasted_iota(jnp.int32, (128, 256), 1)
    pos = (lane % SPAN) + span * SPAN
    seg = (pos >= b1).astype(jnp.int32) + (pos >= b2).astype(jnp.int32) + (pos >= b3).astype(jnp.int32)
    first = lane < 128
    far = [
        jnp.where(
            first,
            jnp.broadcast_to(tab_ref[2 * pair : 2 * pair + 1, b : b + 1], (128, 256)),
            jnp.broadcast_to(tab_ref[2 * pair + 1 : 2 * pair + 2, b : b + 1], (128, 256)),
        )
        for b in (NB // 2 - 1, NB - 1)
    ]
    feat = jnp.where((row < 4) & (row != seg), -BIG, 0.0)
    feat = jnp.where(row == 4, far[0], jnp.where(row == 5, far[1], feat))
    if extra is not None:
        high = extra.astype(jnp.bfloat16).astype(jnp.float32)
        rest = extra - high
        mid = rest.astype(jnp.bfloat16).astype(jnp.float32)
        low = rest - mid
        feat = jnp.where(row == 6, high, jnp.where(row == 7, mid, jnp.where(row == 8, low, feat)))
    return feat.astype(jnp.bfloat16)


def block_diagonal(x_t):
    row = lax.broadcasted_iota(jnp.int32, (128, 128), 0)
    zero = jnp.zeros_like(x_t)
    return jnp.concatenate([jnp.where(row < DH, x_t, zero), jnp.where(row >= DH, x_t, zero)], axis=1)


def stacked_heads(x):
    lane = lax.broadcasted_iota(jnp.int32, (128, 128), 1)
    zero = jnp.zeros_like(x)
    return jnp.concatenate([jnp.where(lane < DH, x, zero), jnp.where(lane >= DH, x, zero)], axis=0)


def near_index(delta):
    return jnp.where((delta >= -1) & (delta <= 1), delta + 1, 3)


def smem():
    return pl.BlockSpec(memory_space=pltpu.SMEM)


def vmem():
    return pl.BlockSpec(memory_space=pltpu.VMEM)


def once():
    return pl.BlockSpec(memory_space=pltpu.VMEM, pipeline_mode=pl.Buffered(1))


def by_chunk():
    return pl.BlockSpec((256, D), lambda t: (t, 0))


def hbm():
    return pl.BlockSpec(memory_space=ANY)


def cost(us):
    return pl.CostEstimate(flops=int(us * 1.0e9), bytes_accessed=int(us * 1.0e6), transcendentals=0)


def load_pieces(pieces, target_ref, flip, sem):
    copies = []
    rows = target_ref.shape[0] // len(pieces)
    for number, (ref, index, place) in enumerate(pieces):
        start = pl.multiple_of(lax.bitwise_xor(jnp.int32(place), flip) * rows, 16)
        source = ref.at[index, pl.ds(0, rows)]
        copies.append(pltpu.make_async_copy(source, target_ref.at[pl.ds(start, rows)], sem.at[number]))
    for copy in copies:
        copy.start()
    return copies


def expand(refs):
    out, place = [], 0
    for ref in refs:
        for index in range(ref.shape[0]):
            out.append((ref, index, place))
            place += 1
    return out


def forward_kernel(counts, *refs):
    n_x, n_w = counts
    ids_ref, order_ref, len_ref = refs[:3]
    refs = refs[3:]
    x_refs, w_refs = refs[:n_x], refs[n_x : n_x + n_w]
    (
        nf_ref, res_ref, o_ref, ot_ref, lse_ref, q_ref, tab_ref, gain_ref, k_out_ref, v_out_ref,
        small_ref, inv_ref, x_ref, w_ref, k_ref, v_ref, rhs_ref, near_ref, m_ref, l_ref, acc_ref, sem_x, sem_w, sem_k, sem_v, sem_s,
    ) = refs[n_x + n_w :]
    spans, own = order_ref.shape[1], q_ref.shape[0] // SPAN
    b1 = len_ref[0, 0]
    b2 = b1 + len_ref[0, 1]
    b3 = b2 + len_ref[0, 2]
    copies = load_pieces(expand(x_refs), x_ref, jnp.int32(0), sem_x)
    copies += load_pieces(expand(w_refs), w_ref, ids_ref[2], sem_w)
    small_copies = []
    for number, (ref, index, _) in enumerate(expand(w_refs)):
        source = ref.at[index, pl.ds(ref.shape[1] - 16, 16)]
        small_copies.append(pltpu.make_async_copy(source, small_ref.at[number], sem_s.at[number]))
    for copy in small_copies:
        copy.start()
    fill_inverse(order_ref, inv_ref, spans)
    for copy in small_copies:
        copy.wait()
    small = small_ref[0, :, 0 : D + 128].astype(jnp.float32)
    for number in range(1, len(small_copies)):
        small = small + small_ref[number, :, 0 : D + 128].astype(jnp.float32)
    gain_ref[...] = small[0:8, 0:D]
    tab_ref[...] = small[:, D : D + 128]
    fill_near_bias(tab_ref[...].astype(jnp.bfloat16), near_ref)
    for copy in copies:
        copy.wait()
    own_rows = own * SPAN
    gain = gain_ref[0:1, :]

    def normed(x):
        x = x.astype(jnp.float32)
        return (x * lax.rsqrt(jnp.mean(x * x, axis=1, keepdims=True) + EPS) * gain).astype(jnp.bfloat16)

    my_spans = [order_ref[0, ids_ref[0] * own + i] for i in range(own)]
    my_ranges = [key_range(span, b1, b2, b3, spans * SPAN) for span in my_spans]

    def chunk_copies(t):
        rows = pl.ds(pl.multiple_of(t * 256, 256), 256)
        return (
            pltpu.make_async_copy(k_ref.at[rows], k_out_ref.at[rows], sem_k.at[t]),
            pltpu.make_async_copy(v_ref.at[rows], v_out_ref.at[rows], sem_v.at[t]),
        )

    def if_needed(t, body):
        needed = jnp.bool_(False)
        for low, high in my_ranges:
            needed = needed | ((t >= low) & (t < high))
        pl.when(needed)(body)

    def project(t, carry):
        def fill():
            rows = pl.ds(pl.multiple_of(t * 256, 256), 256)
            parts = []
            for half in range(2):
                slot = inv_ref[2 * t + half]
                piece = lax.bitwise_xor(slot // own, ids_ref[1])
                start = pl.multiple_of(piece * own_rows + (slot % own) * SPAN, SPAN)
                parts.append(x_ref[pl.ds(start, SPAN), :])
            xn = normed(jnp.concatenate(parts, axis=0))
            k_ref[rows, :] = dot(xn, w_ref[:, D : 2 * D]).astype(jnp.bfloat16)
            v_ref[rows, :] = dot(xn, w_ref[:, 2 * D : 3 * D]).astype(jnp.bfloat16)
            for copy in chunk_copies(t):
                copy.start()

        if_needed(t, fill)
        return carry

    lax.fori_loop(0, spans // 2, project, 0)
    mine = pl.multiple_of(lax.bitwise_xor(ids_ref[0], ids_ref[1]) * own_rows, SPAN)
    x_own = x_ref[pl.ds(mine, own_rows), :]
    q_ref[...] = dot(normed(x_own), w_ref[:, 0:D]).astype(jnp.bfloat16)

    def one_span(i, carry):
        span = order_ref[0, ids_ref[0] * own + i]
        low, high = key_range(span, b1, b2, b3, spans * SPAN)
        my_rows = pl.ds(pl.multiple_of(i * SPAN, SPAN), SPAN)
        for p in range(PAIRS):
            q_t = q_ref[my_rows, p * 128 : p * 128 + 128].T
            rhs_ref[p, 0:128, :] = block_diagonal(q_t)
            rhs_ref[p, 128:256, :] = query_features(span, p, tab_ref, b1, b2, b3)
        m_ref[...] = jnp.full_like(m_ref, -BIG)
        l_ref[...] = jnp.zeros_like(l_ref)
        acc_ref[...] = jnp.zeros_like(acc_ref)

        def chunk_body(t, near):
            rows = pl.ds(pl.multiple_of(t * 256, 256), 256)
            feat = key_features(t, span, b1, b2, b3)

            def scores(p):
                s = dot(jnp.concatenate([k_ref[rows, p * 128 : p * 128 + 128], feat], axis=1), rhs_ref[p])
                if near:
                    n0, n1 = near_index(2 * t - span), near_index(2 * t + 1 - span)
                    s = s + jnp.concatenate([near_ref[n0, p], near_ref[n1, p]], axis=0)
                return s

            def top(p, s):
                old = m_ref[p]
                new = jnp.maximum(old, jnp.max(s, axis=0, keepdims=True))
                m_ref[p] = new
                return new, jnp.exp(old - new)

            def weigh(p, s, new, scale):
                e = jnp.exp(s - new)
                l_ref[p] = l_ref[p] * scale + jnp.sum(e, axis=0, keepdims=True)
                return e.astype(jnp.bfloat16)

            def attend(p, e, scale):
                o = dot(v_ref[rows, p * 128 : p * 128 + 128], e, 0, 0)
                acc_ref[p, 0:64, :] = acc_ref[p, 0:64, :] * scale[:, 0:128] + o[0:64, 0:128]
                acc_ref[p, 64:128, :] = acc_ref[p, 64:128, :] * scale[:, 128:256] + o[64:128, 128:256]

            ss, tops, es = {}, {}, {}
            for p in range(PAIRS + 3):
                if p < PAIRS:
                    ss[p] = scores(p)
                if 1 <= p <= PAIRS:
                    tops[p - 1] = top(p - 1, ss[p - 1])
                if 2 <= p <= PAIRS + 1:
                    es[p - 2] = weigh(p - 2, ss[p - 2], *tops[p - 2])
                if p >= 3:
                    attend(p - 3, es[p - 3], tops[p - 3][1])

        def step(t, carry):
            near = (2 * t + 2 >= span) & (2 * t <= span + 1)
            pl.when(near)(lambda: chunk_body(t, True))
            pl.when(jnp.logical_not(near))(lambda: chunk_body(t, False))
            return carry

        lax.fori_loop(low, high, step, 0)
        for p in range(PAIRS):
            total = l_ref[p]
            lse_ref[i, p] = m_ref[p] + jnp.log(total)
            inv = 1.0 / total
            out = jnp.concatenate(
                [acc_ref[p, 0:64, :] * inv[:, 0:128], acc_ref[p, 64:128, :] * inv[:, 128:256]], axis=0
            )
            ot_ref[i, p] = out
            o_ref[my_rows, p * 128 : p * 128 + 128] = out.T.astype(jnp.bfloat16)
        return carry

    lax.fori_loop(0, own, one_span, 0)
    res = x_own.astype(jnp.float32) + dot(o_ref[...], w_ref[:, 3 * D : 4 * D])
    res_ref[...] = res
    inv_rms = lax.rsqrt(jnp.mean(res * res, axis=1, keepdims=True) + EPS)
    nf_ref[...] = (res * inv_rms * gain_ref[1:2, :]).astype(jnp.bfloat16)

    def settle(t, carry):
        def wait():
            for copy in chunk_copies(t):
                copy.wait()

        if_needed(t, wait)
        return carry

    lax.fori_loop(0, spans // 2, settle, 0)


def forward(ids, order, lengths, xs, ws, local_rows):
    spans, own = order.shape[1], local_rows // SPAN
    rows = spans * SPAN
    n_x, n_w = sum(x.shape[0] for x in xs), sum(w.shape[0] for w in ws)
    bf, f32 = jnp.bfloat16, jnp.float32
    return pl.pallas_call(
        lambda *refs: forward_kernel((len(xs), len(ws)), *refs),
        name="forward",
        cost_estimate=cost(22),
        out_shape=(
            jax.ShapeDtypeStruct((local_rows, D), bf),
            jax.ShapeDtypeStruct((local_rows, D), f32),
            jax.ShapeDtypeStruct((local_rows, D), bf),
            jax.ShapeDtypeStruct((own, PAIRS, 128, 128), f32),
            jax.ShapeDtypeStruct((own, PAIRS, 1, 256), f32),
            jax.ShapeDtypeStruct((local_rows, D), bf),
            jax.ShapeDtypeStruct((16, 128), f32),
            jax.ShapeDtypeStruct((8, D), f32),
            jax.ShapeDtypeStruct((rows, D), bf),
            jax.ShapeDtypeStruct((rows, D), bf),
        ),
        in_specs=[smem()] * 3 + [hbm()] * (len(xs) + len(ws)),
        out_specs=(vmem(),) * 8 + (hbm(),) * 2,
        scratch_shapes=[
            pltpu.VMEM((n_w, 16, 4 * D), bf),
            pltpu.SMEM((spans,), jnp.int32),
            pltpu.VMEM((rows, D), bf),
            pltpu.VMEM((D, 4 * D), bf),
            pltpu.VMEM((rows, D), bf),
            pltpu.VMEM((rows, D), bf),
            pltpu.VMEM((PAIRS, 256, 256), bf),
            pltpu.VMEM((4, PAIRS, 128, 256), f32),
            pltpu.VMEM((PAIRS, 1, 256), f32),
            pltpu.VMEM((PAIRS, 1, 256), f32),
            pltpu.VMEM((PAIRS, 128, 128), f32),
            pltpu.SemaphoreType.DMA((n_x,)),
            pltpu.SemaphoreType.DMA((n_w,)),
            pltpu.SemaphoreType.DMA((spans // 2,)),
            pltpu.SemaphoreType.DMA((spans // 2,)),
            pltpu.SemaphoreType.DMA((n_w,)),
        ],
        compiler_params=pltpu.CompilerParams(vmem_limit_bytes=VMEM_LIMIT),
    )(ids, order, lengths, *xs, *ws)


def ffn_kernel(counts, *refs):
    count, n_w = counts
    ids_ref, refs = refs[0], refs[1:]
    nfs, cots, wins = refs[:count], refs[count : 2 * count], refs[2 * count : 2 * count + n_w]
    wffn_ref, act_ref, dup_ref = refs[2 * count + n_w : 2 * count + n_w + 3]
    refs = refs[2 * count + n_w + 3 :]
    dns, outs, (w_ref, sem) = refs[:count], refs[count : 2 * count], refs[2 * count :]
    done = 0
    for copy in load_pieces(expand(wins), w_ref, ids_ref[3], sem):
        copy.wait()
    for nf_ref, cot_ref, dn_ref, out_ref in zip(nfs, cots, dns, outs):
        for piece in range(nf_ref.shape[0]):
            up = dot(nf_ref[piece], w_ref[...])
            d_act = dot(cot_ref[piece], wffn_ref[...], 1, 1)
            square = up * up
            th = jnp.tanh(GELU_C * (up + 0.044715 * square * up))
            half = 0.5 * (1.0 + th)
            act = (up * half).astype(jnp.bfloat16)
            act_ref[done] = act
            slope = half + 0.5 * up * (1.0 - th * th) * (GELU_C * (1.0 + 3 * 0.044715 * square))
            d_up = (d_act * slope).astype(jnp.bfloat16)
            dup_ref[done] = d_up
            dn_ref[piece] = dot(d_up, w_ref[...], 1, 1).astype(jnp.bfloat16)
            out_ref[piece] = dot(act, wffn_ref[...]).astype(jnp.bfloat16)
            done += 1


def ffn(ids, nfs, cots, wins, wffn):
    total, rows, count = sum(n.shape[0] for n in nfs), nfs[0].shape[1], len(nfs)
    width = wffn.shape[0]
    bf = jnp.bfloat16
    act, dup, *rest = pl.pallas_call(
        lambda *refs: ffn_kernel((count, len(wins)), *refs),
        name="ffn",
        cost_estimate=cost(6),
        out_shape=(jax.ShapeDtypeStruct((total, rows, width), bf),) * 2
        + tuple(jax.ShapeDtypeStruct((n.shape[0], rows, D), bf) for n in nfs) * 2,
        in_specs=[smem()] + [vmem()] * (2 * count) + [hbm()] * len(wins) + [vmem()],
        out_specs=(vmem(),) * (2 + 2 * count),
        scratch_shapes=[
            pltpu.VMEM((D, width), bf),
            pltpu.SemaphoreType.DMA((sum(w.shape[0] for w in wins),)),
        ],
        compiler_params=pltpu.CompilerParams(vmem_limit_bytes=VMEM_LIMIT),
    )(ids, *nfs, *cots, *wins, wffn)
    return act, dup, rest[:count], rest[count:]


def by_turn(turn, refs, body):
    for number, ref in enumerate(refs):
        pl.when(turn == number)(lambda ref=ref: body(ref))


def ffn_grads_kernel(counts, parts, *refs):
    n, m = counts
    ids_ref = refs[0]
    groups, start = [], 1
    for count in (n, n, m, m):
        groups.append(refs[start : start + count])
        start += count
    nfs, cots, acts, dups = groups
    outs = refs[start:]

    def joined(pieces):
        flat = [ref[...].reshape(-1, ref.shape[2]) for ref in pieces]
        return flat[0] if len(flat) == 1 else jnp.concatenate(flat, axis=0)

    g_out = dot(joined(acts), joined(cots), 0, 0).astype(jnp.bfloat16)
    g_in = dot(joined(nfs), joined(dups), 0, 0).astype(jnp.bfloat16)
    if parts == 1:
        outs[0][...] = g_out
        size = outs[1].shape[1]
        for i in range(outs[1].shape[0]):
            outs[1][i] = g_in[i * size : (i + 1) * size]
        return
    out_ref, gin_ref = outs
    gin_ref[...] = g_in
    rows = D // parts
    for part in range(parts):
        out_ref[part, 0:rows, :] = g_out[part * rows : (part + 1) * rows]
        side = slice((part % 2) * 384, (part % 2) * 384 + 384)
        for place in range(4):
            owner = lax.bitwise_xor(jnp.int32(place), ids_ref[3])
            down = pl.ds(pl.multiple_of(owner * 192 + (part // 2) * 48, 16), 48)
            first, left = rows + (place // 2) * 48, (place % 2) * 384
            out_ref[part, first : first + 48, left : left + 384] = gin_ref[down, side]


def ffn_grads(ids, nfs, cots, acts, dups, n_fsdp, parts):
    width = acts[0].shape[2]
    bf = jnp.bfloat16
    if parts == 1:
        shapes = (jax.ShapeDtypeStruct((width, D), bf), jax.ShapeDtypeStruct((n_fsdp, D // n_fsdp, width), bf))
    else:
        shapes = (jax.ShapeDtypeStruct((parts, 2 * D // parts, D), bf),)
    scratch = [] if parts == 1 else [pltpu.VMEM((D, width), bf)]
    return pl.pallas_call(
        lambda *refs: ffn_grads_kernel((len(nfs), len(acts)), parts, *refs),
        name="ffn_grads",
        cost_estimate=cost(6),
        out_shape=shapes,
        in_specs=[smem()] + [vmem()] * (2 * len(nfs) + 2 * len(acts)),
        out_specs=(vmem(),) * len(shapes),
        scratch_shapes=scratch,
        compiler_params=pltpu.CompilerParams(vmem_limit_bytes=VMEM_LIMIT),
    )(ids, *nfs, *cots, *acts, *dups)


def fetch_turns(pieces, all_ref, flip, sem):
    copies = []
    for number, (ref, index, turn) in enumerate(pieces):
        place = lax.bitwise_xor(jnp.int32(turn), flip)
        copies.append(pltpu.make_async_copy(ref.at[index], all_ref.at[place], sem.at[number]))
    for copy in copies:
        copy.start()
    for copy in copies:
        copy.wait()


def with_turns(refs, turns):
    return [(ref, index, turn) for ref, group in zip(refs, turns) for index, turn in enumerate(group)]


def finish_ffn_kernel(turns, *refs):
    count = len(turns)
    ids_ref = refs[0]
    gout_ref, gin_ref, all_ref, sem = refs[1 + count :]
    fetch_turns(with_turns(refs[1 : 1 + count], turns), all_ref, ids_ref[1], sem)
    rows = all_ref.shape[1] // 2
    for p in range(all_ref.shape[0]):
        gout_ref[p * rows : (p + 1) * rows, :] = all_ref[p, 0:rows, :].astype(jnp.float32)
        for i in range(4):
            place = lax.bitwise_xor(jnp.int32(i), ids_ref[3])
            down = pl.ds(pl.multiple_of(rows + (place // 2) * 48, 16), 48)
            side = pl.ds(pl.multiple_of((place % 2) * 384, 128), 384)
            first = i * D + (p % 2) * 384
            gin_ref[(p // 2) * 48 : (p // 2) * 48 + 48, first : first + 384] = all_ref[p, down, side].astype(jnp.float32)


def finish_ffn(ids, arrays, turns):
    f32 = jnp.float32
    count = sum(a.shape[0] for a in arrays)
    return pl.pallas_call(
        lambda *refs: finish_ffn_kernel(turns, *refs),
        name="finish_ffn",
        cost_estimate=cost(4),
        out_shape=(jax.ShapeDtypeStruct((D, D), f32), jax.ShapeDtypeStruct((D // 4, 4 * D), f32)),
        in_specs=[smem()] + [hbm()] * len(arrays),
        out_specs=(vmem(),) * 2,
        scratch_shapes=[pltpu.VMEM((count, *arrays[0].shape[1:]), jnp.bfloat16), pltpu.SemaphoreType.DMA((count,))],
        compiler_params=pltpu.CompilerParams(vmem_limit_bytes=VMEM_LIMIT),
    )(ids, *arrays)


def put_grads(outs, all_ref, size, part_flip, fsdp_flip):
    n, parts, wide = sum(ref.shape[0] for ref in outs), outs[0].shape[1], outs[0].shape[3]
    for turn in range(n):
        owner = lax.bitwise_xor(jnp.int32(turn), fsdp_flip)
        rows = pl.ds(pl.multiple_of(owner * size, 16), size)
        for part in range(parts):
            source = lax.bitwise_xor(jnp.int32(part), part_flip)
            columns = pl.ds(pl.multiple_of(source * wide, 128), wide)
            outs[turn % len(outs)][turn // len(outs), part, 0:size, :] = all_ref[rows, columns].astype(jnp.bfloat16)


def grad_shapes(n, parts):
    high, wide = D // n + 16, 2 * D // parts
    if parts == 1:
        return (jax.ShapeDtypeStruct((n, parts, high, wide), jnp.bfloat16),)
    return (jax.ShapeDtypeStruct((n // 2, parts, high, wide), jnp.bfloat16),) * 2


def finish_kernel(turns, *refs):
    count = len(turns)
    ids_ref = refs[0]
    outs, (attn_ref, ffn_ref, table_ref, all_ref, row_ref, sem) = refs[1 + count : 5 + count], refs[5 + count :]
    fetch_turns(with_turns(refs[1 : 1 + count], turns), all_ref, ids_ref[1], sem)
    size, wide = outs[0].shape[0], all_ref.shape[2]
    step = min(D, wide)
    for first in range(0, 4 * D, step):
        outs[first // D][:, first % D : first % D + step] = all_ref[
            first // wide, 0:size, first % wide : first % wide + step
        ].astype(jnp.float32)

    def row(first):
        cuts = [all_ref[i // wide, size : size + 16, i % wide : i % wide + step] for i in range(first, first + D, step)]
        return jnp.concatenate(cuts, axis=1).astype(jnp.float32)[0:8]

    back = D - ids_ref[4] * size
    attn_ref[...] = pltpu.roll(row(0), back, 1)[0:1, 0:size]
    ffn_ref[...] = pltpu.roll(row(D), back, 1)[0:1, 0:size]
    table = all_ref[2 * D // wide, size : size + 16, 2 * D % wide : 2 * D % wide + 128].astype(jnp.float32)
    row_ref[...] = jnp.concatenate([table, jnp.zeros((112, 128), jnp.float32)], axis=0).T
    high = table_ref.shape[0]
    table_ref[...] = row_ref[pl.ds(ids_ref[4] * high, high), 0:H]


def finish(ids, arrays, turns, high):
    count, tall, wide = sum(a.shape[0] for a in arrays), *arrays[0].shape[1:]
    size, f32 = tall - 16, jnp.float32
    return pl.pallas_call(
        lambda *refs: finish_kernel(turns, *refs),
        name="finish",
        cost_estimate=cost(3),
        out_shape=(jax.ShapeDtypeStruct((size, D), f32),) * 4
        + (jax.ShapeDtypeStruct((1, size), f32),) * 2
        + (jax.ShapeDtypeStruct((high, H), f32),),
        in_specs=[smem()] + [hbm()] * len(arrays),
        out_specs=(vmem(),) * 7,
        scratch_shapes=[
            pltpu.VMEM((count, tall, wide), jnp.bfloat16),
            pltpu.VMEM((128, 128), f32),
            pltpu.SemaphoreType.DMA((count,)),
        ],
        compiler_params=pltpu.CompilerParams(vmem_limit_bytes=VMEM_LIMIT),
    )(ids, *arrays)


def backward_kernel(counts, *refs):
    n_x, n_w, n_dnf, n_dn, n_grad = counts
    (
        ids_ref, order_ref, len_ref, tab_ref, gain_ref,
        res_ref, cot_ref, o_ref, ot_ref, lse_ref, q_ref, k_ref, v_ref,
    ) = refs[:13]
    refs = refs[13:]
    x_refs, w_refs, dnf_refs = refs[:n_x], refs[n_x : n_x + n_w], refs[n_x + n_w : n_x + n_w + n_dnf]
    refs = refs[n_x + n_w + n_dnf :]
    dn_refs, mine_refs, shared_refs = refs[:n_dn], refs[n_dn : n_dn + n_grad], refs[n_dn + n_grad : n_dn + 2 * n_grad]
    (
        dres_ref, dn_own_ref,
        dlow_ref, dq_ref, dgain_ref, own_ref, all_ref, inv_ref, x_ref, w_ref, do_ref, rhs_ref, dorhs_ref, qbd_ref, dobd_ref, near_ref, nacc_ref, acc_ref, far_ref,
        dkacc_ref, dvacc_ref, kt_ref, sem_x, sem_w,
    ) = refs[n_dn + 2 * n_grad :]
    spans, own = order_ref.shape[1], q_ref.shape[0] // SPAN
    own_rows = own * SPAN
    b1 = len_ref[0, 0]
    b2 = b1 + len_ref[0, 1]
    b3 = b2 + len_ref[0, 2]
    t = pl.program_id(0)

    @pl.when(t == 0)
    def begin():
        copies_x = load_pieces(expand(x_refs), x_ref, jnp.int32(0), sem_x)
        copies_w = load_pieces(expand(w_refs), w_ref, ids_ref[2], sem_w)
        fill_inverse(order_ref, inv_ref, spans)
        fill_near_bias(tab_ref[...].astype(jnp.bfloat16), near_ref)
        nacc_ref[...] = jnp.zeros_like(nacc_ref)
        far_ref[...] = jnp.zeros_like(far_ref)

        res, dnf = res_ref[...], dnf_refs[0][...].astype(jnp.float32)
        for ref in dnf_refs[1:]:
            dnf = dnf + ref[...].astype(jnp.float32)
        inv_rms = lax.rsqrt(jnp.mean(res * res, axis=1, keepdims=True) + EPS)
        dgain_ref[...] = jnp.zeros_like(dgain_ref)
        dgain_ref[1:2, :] = jnp.sum(dnf * res * inv_rms, axis=0, keepdims=True)
        scaled = dnf * gain_ref[1:2, :]
        inner = jnp.mean(scaled * res, axis=1, keepdims=True)
        dres = cot_ref[...].astype(jnp.float32) + inv_rms * scaled - res * (inv_rms * inv_rms * inv_rms * inner)
        dres_ref[...] = dres
        dlow = dres.astype(jnp.bfloat16)
        dlow_ref[...] = dlow
        for copy in copies_w:
            copy.wait()
        do_ref[...] = dot(dlow, w_ref[:, 3 * D : 4 * D], 1, 1).astype(jnp.bfloat16)
        own_ref[:, D : 2 * D] = dot(o_ref[...], dlow, 0, 0)
        all_ref[...] = jnp.zeros_like(all_ref)

        def prepare(i, carry):
            span = order_ref[0, ids_ref[0] * own + i]
            my_rows = pl.ds(pl.multiple_of(i * SPAN, SPAN), SPAN)
            for p in range(PAIRS):
                cols = slice(p * 128, p * 128 + 128)
                qp, dop = q_ref[my_rows, cols], do_ref[my_rows, cols]
                do_t = dop.T
                prod = do_t.astype(jnp.float32) * ot_ref[i, p]
                neg = -jnp.concatenate(
                    [jnp.sum(prod[0:64], axis=0, keepdims=True), jnp.sum(prod[64:128], axis=0, keepdims=True)], axis=1
                )
                rhs_ref[i, p, 0:128, :] = block_diagonal(qp.T)
                rhs_ref[i, p, 128:256, :] = query_features(span, p, tab_ref, b1, b2, b3, -lse_ref[i, p])
                row = lax.broadcasted_iota(jnp.int32, (128, 256), 0)
                h1 = neg.astype(jnp.bfloat16).astype(jnp.float32)
                h2 = (neg - h1).astype(jnp.bfloat16).astype(jnp.float32)
                h3 = neg - h1 - h2
                dfeat = jnp.where(row == 6, h1, jnp.where(row == 7, h2, jnp.where(row == 8, h3, 0.0)))
                dorhs_ref[i, p, 0:128, :] = block_diagonal(do_t)
                dorhs_ref[i, p, 128:256, :] = dfeat.astype(jnp.bfloat16)
                qbd_ref[i, p] = stacked_heads(qp)
                dobd_ref[i, p] = stacked_heads(dop)
            return carry

        lax.fori_loop(0, own, prepare, 0)
        acc_ref[...] = jnp.zeros_like(acc_ref)
        for copy in copies_x:
            copy.wait()


    def unit(x):
        x = x.astype(jnp.float32)
        return x * lax.rsqrt(jnp.mean(x * x, axis=1, keepdims=True) + EPS)

    my_spans = [order_ref[0, ids_ref[0] * own + i] for i in range(own)]
    used = jnp.bool_(False)
    for span in my_spans:
        low, high = key_range(span, b1, b2, b3, spans * SPAN)
        used = used | ((t >= low) & (t < high))

    @pl.when(used)
    def ready():
        dkacc_ref[...] = jnp.zeros_like(dkacc_ref)
        dvacc_ref[...] = jnp.zeros_like(dvacc_ref)
        for p in range(PAIRS):
            kt_ref[p, 0:128, :] = k_ref[:, p * 128 : p * 128 + 128].T

    def span_body(i, span, near):
        feat = key_features(t, span, b1, b2, b3)
        for p in range(PAIRS):
            kt_ref[p, 128:144, :] = feat.T[0:16]

        def first(p):
            cols = slice(p * 128, p * 128 + 128)
            return (
                dot(jnp.concatenate([k_ref[:, cols], feat], axis=1), rhs_ref[i, p]),
                dot(jnp.concatenate([v_ref[:, cols], feat], axis=1), dorhs_ref[i, p]),
            )

        def last(p, prob, ds):
            cols = slice(p * 128, p * 128 + 128)
            dvacc_ref[:, cols] += dot(prob, dobd_ref[i, p])
            dkacc_ref[:, cols] += dot(ds, qbd_ref[i, p])
            dq = dot(kt_ref[p], ds)
            acc_ref[i, p, 0:64, :] += dq[0:64, 0:128]
            acc_ref[i, p, 64:128, :] += dq[64:128, 128:256]
            far_ref[p] += dq[128:136, :]

        ahead, waiting = first(0), None
        for p in range(PAIRS):
            s, dp = ahead
            if p + 1 < PAIRS:
                ahead = first(p + 1)
            if near:
                n0, n1 = near_index(2 * t - span), near_index(2 * t + 1 - span)
                s = s + jnp.concatenate([near_ref[n0, p], near_ref[n1, p]], axis=0)
            prob = jnp.exp(s)
            ds = prob * dp
            if near:
                nacc_ref[n0, p] += ds[0:128]
                nacc_ref[n1, p] += ds[128:256]
            if waiting is not None:
                last(*waiting)
            waiting = (p, prob.astype(jnp.bfloat16), ds.astype(jnp.bfloat16))
        last(*waiting)

    def one_span(i, carry):
        span = order_ref[0, ids_ref[0] * own + i]
        low, high = key_range(span, b1, b2, b3, spans * SPAN)
        needed = (t >= low) & (t < high)
        near = (2 * t + 2 >= span) & (2 * t <= span + 1)
        pl.when(needed & near)(lambda: span_body(i, span, True))
        pl.when(needed & jnp.logical_not(near))(lambda: span_body(i, span, False))
        return carry

    lax.fori_loop(0, own, one_span, 0)
    places, targets = [], []
    for half in range(2):
        slot = inv_ref[2 * t + half]
        piece = lax.bitwise_xor(slot // own, ids_ref[1])
        inside = (slot % own) * SPAN
        places.append(pl.ds(pl.multiple_of(piece * own_rows + inside, SPAN), SPAN))
        targets.append((piece, inside))

    def store(half, value):
        piece, inside = targets[half]

        def put(ref, index):
            ref[pl.ds(pl.multiple_of(index * own_rows + inside, SPAN), SPAN), :] = value

        if n_dn == 1:
            put(dn_refs[0], piece)
        else:
            by_turn(piece, dn_refs, lambda ref: put(ref, 0))

    def fill():
        dkb, dvb = dkacc_ref[...].astype(jnp.bfloat16), dvacc_ref[...].astype(jnp.bfloat16)
        part = dot(dkb, w_ref[:, D : 2 * D], 1, 1) + dot(dvb, w_ref[:, 2 * D : 3 * D], 1, 1)
        x = unit(jnp.concatenate([x_ref[places[0], :], x_ref[places[1], :]], axis=0))
        dgain_ref[0:1, :] += jnp.sum(part * x, axis=0, keepdims=True)
        turned = (x * gain_ref[0:1, :]).astype(jnp.bfloat16).T
        all_ref[:, 0:D] += dot(turned, dkb)
        all_ref[:, D : 2 * D] += dot(turned, dvb)
        part = part.astype(jnp.bfloat16)
        store(0, part[0:128])
        store(1, part[128:256])

    def skip():
        zero = jnp.zeros((256, D), jnp.bfloat16)
        store(0, zero[0:128])
        store(1, zero[0:128])

    pl.when(used)(fill)
    pl.when(jnp.logical_not(used))(skip)


    @pl.when(t == spans // 2 - 1)
    def finish():
        for i in range(own):
            for p in range(PAIRS):
                dq_ref[i * SPAN : (i + 1) * SPAN, p * 128 : p * 128 + 128] = acc_ref[i, p].T.astype(jnp.bfloat16)
        mine = pl.multiple_of(lax.bitwise_xor(ids_ref[0], ids_ref[1]) * own_rows, SPAN)
        own_part = dot(dq_ref[...], w_ref[:, 0:D], 1, 1)
        dn_own_ref[...] = own_part
        x_own = unit(x_ref[pl.ds(mine, own_rows), :])
        dgain_ref[0:1, :] += jnp.sum(own_part * x_own, axis=0, keepdims=True)
        own_ref[:, 0:D] = dot((x_own * gain_ref[0:1, :]).astype(jnp.bfloat16), dq_ref[...], 0, 0)
        parts, tall = mine_refs[0].shape[1:3]
        size, part_flip = tall - 16, ids_ref[1] & (parts - 1)
        put_grads(mine_refs, own_ref, size, part_flip, ids_ref[3])
        put_grads(shared_refs, all_ref, size, part_flip, ids_ref[3])

        row16 = lax.broadcasted_iota(jnp.int32, (16, 128), 0)
        lane16 = lax.broadcasted_iota(jnp.int32, (16, 128), 1)
        grad = jnp.zeros((16, 128), jnp.float32)
        for head in range(H):
            half = slice((head % 2) * 128, (head % 2) * 128 + 128)
            sums = jnp.sum(far_ref[head // 2, 4:6, half], axis=1, keepdims=True)
            grad = grad + jnp.where((row16 == head) & (lane16 == NB // 2 - 1), sums[0:1], 0.0)
            grad = grad + jnp.where((row16 == head) & (lane16 == NB - 1), sums[1:2], 0.0)
        rowd = lax.broadcasted_iota(jnp.int32, (16, 256), 0)
        flip_row = lax.broadcasted_iota(jnp.int32, (128, 128), 0)
        flip_lane = lax.broadcasted_iota(jnp.int32, (128, 128), 1)
        flip = (flip_row + flip_lane == 127).astype(jnp.bfloat16)
        for index in range(3):
            sums = jnp.zeros((16, 256), jnp.float32)
            for p in range(PAIRS):
                both = nacc_ref[index, p]
                high = both.astype(jnp.bfloat16)
                rest = (both - high.astype(jnp.float32)).astype(jnp.bfloat16)
                turned = dot(flip, high) + dot(flip, rest)
                for side in range(2):
                    tile = turned[:, side * 128 : side * 128 + 128]
                    wide = jnp.concatenate([tile, jnp.zeros_like(tile)], axis=1)
                    shifted = pltpu.roll(wide, 0, 1, stride=1, stride_axis=0)
                    sums = sums + jnp.where(rowd == 2 * p + side, jnp.sum(shifted, axis=0, keepdims=True), 0.0)
            hot = diagonal_onehot(index - 1).astype(jnp.float32)
            grad = grad + lax.dot_general(
                sums, hot, (((1,), (1,)), ((), ())), preferred_element_type=jnp.float32, precision=lax.Precision.HIGHEST
            )
        wide = mine_refs[0].shape[3]
        own_ref[0:1, 0:D] = dgain_ref[0:1, :]
        own_ref[0:1, D : 2 * D] = dgain_ref[1:2, :]
        own_ref[1:16, :] = jnp.zeros((15, 2 * D), jnp.float32)
        own_ref[16:32, :] = jnp.concatenate([grad, jnp.zeros((16, 2 * D - 128), jnp.float32)], axis=1)
        for refs, top in ((mine_refs, 0), (shared_refs, 16)):
            for part in range(parts):
                columns = pl.ds(pl.multiple_of(lax.bitwise_xor(jnp.int32(part), part_flip) * wide, 128), wide)
                value = own_ref[top : top + 16, columns].astype(jnp.bfloat16)
                for ref in refs:
                    for index in range(ref.shape[0]):
                        ref[index, part, size:tall, :] = value


def backward(ids, order, lengths, table, gains, dnf, res, cot, o, ot, lse, q, k, v, xs, ws, n_dn, n_fsdp):
    spans, local_rows = order.shape[1], q.shape[0]
    rows, own = spans * SPAN, local_rows // SPAN
    n_x, n_w = sum(x.shape[0] for x in xs), sum(w.shape[0] for w in ws)
    bf, f32 = jnp.bfloat16, jnp.float32
    shapes = grad_shapes(n_fsdp, 1 if n_dn == 1 else 4)
    return pl.pallas_call(
        lambda *refs: backward_kernel((len(xs), len(ws), len(dnf), n_dn, len(shapes)), *refs),
        name="backward",
        cost_estimate=cost(36),
        grid=(spans // 2,),
        out_shape=(jax.ShapeDtypeStruct((rows // n_dn, D), bf),) * n_dn
        + shapes * 2
        + (jax.ShapeDtypeStruct((local_rows, D), f32),) * 2,
        in_specs=[smem()] * 3 + [once()] * 8 + [by_chunk()] * 2 + [hbm()] * (len(xs) + len(ws)) + [once()] * len(dnf),
        out_specs=(once(),) * (n_dn + 2 * len(shapes) + 2),
        scratch_shapes=[
            pltpu.VMEM((local_rows, D), bf),
            pltpu.VMEM((local_rows, D), bf),
            pltpu.VMEM((8, D), f32),
            pltpu.VMEM((D, 2 * D), f32),
            pltpu.VMEM((D, 2 * D), f32),
            pltpu.SMEM((spans,), jnp.int32),
            pltpu.VMEM((rows, D), bf),
            pltpu.VMEM((D, 4 * D), bf),
            pltpu.VMEM((local_rows, D), bf),
            pltpu.VMEM((own, PAIRS, 256, 256), bf),
            pltpu.VMEM((own, PAIRS, 256, 256), bf),
            pltpu.VMEM((own, PAIRS, 256, 128), bf),
            pltpu.VMEM((own, PAIRS, 256, 128), bf),
            pltpu.VMEM((4, PAIRS, 128, 256), f32),
            pltpu.VMEM((4, PAIRS, 128, 256), f32),
            pltpu.VMEM((own, PAIRS, 128, 128), f32),
            pltpu.VMEM((PAIRS, 8, 256), f32),
            pltpu.VMEM((256, D), f32),
            pltpu.VMEM((256, D), f32),
            pltpu.VMEM((PAIRS, 144, 256), bf),
            pltpu.SemaphoreType.DMA((n_x,)),
            pltpu.SemaphoreType.DMA((n_w,)),
        ],
        compiler_params=pltpu.CompilerParams(vmem_limit_bytes=VMEM_LIMIT),
    )(ids, order, lengths, table, gains, res, cot, o, ot, lse, q, k, v, *xs, *ws, *dnf)


def swap(x, axis, bit):
    count = lax.axis_size(axis)
    return lax.ppermute(x, axis, [(i, i ^ bit) for i in range(count)])


def hop(x, pairs):
    return lax.ppermute(x, "ctx", [(2 * a + i, 2 * b + i) for a, b in pairs for i in range(2)])


def block(x, index, count, dim=0):
    size = x.shape[dim] // count
    return lax.dynamic_slice_in_dim(x, index * size, size, dim)


def after(x, *others):
    return lax.optimization_barrier((x,) + others)[0]


def add(*terms):
    total = terms[0].astype(jnp.float32)
    for term in terms[1:]:
        total = total + term.astype(jnp.float32)
    return total.astype(jnp.bfloat16)


def gather_four(x):
    across = swap(x, "fsdp", 2)
    return [x, swap(x, "fsdp", 1), across, swap(across, "fsdp", 1)]


def scatter_four(pieces):
    first, third = swap(pieces[1], "fsdp", 1), swap(pieces[3], "fsdp", 1)
    far = add(pieces[2], third)
    return pieces[0], first, swap(far, "fsdp", 2), far


def scatter_pairs(keep, send):
    got = swap(send, "fsdp", 1)
    far = add(keep[1], got[1])
    return (keep[0], got[0], swap(far, "fsdp", 2)), far


TURNS = ((0,), (1,), (2, 6), (3, 7), (4,), (5,))


def tail(dn, mine, shared, ffn_own, high):
    g7, g3 = swap(dn[7], "ctx", 1), swap(dn[3], "ctx", 1)
    (mine, _), (shared, _) = scatter_pairs(*mine), scatter_pairs(*shared)
    top, blocks = ffn_own[: D // 8], ffn_own[D // 8 :]
    blocks = [blocks[48 * (r // 2) : 48 * (r // 2) + 48, 384 * (r % 2) : 384 * (r % 2) + 384] for r in range(4)]
    side = swap(jnp.stack([blocks[1], blocks[3]]), "fsdp", 1)
    across = swap(jnp.stack([blocks[2], side[1]]), "fsdp", 2)
    ffn_own = jnp.concatenate(
        [top, jnp.concatenate([blocks[0], side[0]], axis=1), jnp.concatenate([across[0], across[1]], axis=1)]
    )[None]
    ffn4 = swap(ffn_own, "ctx", 4)
    mine, shared = add(*mine), add(*shared)
    g5, g1 = swap(after(dn[5], g7), "ctx", 1), swap(after(dn[1], g3), "ctx", 1)
    n4 = swap(add(dn[6], g7), "ctx", 2)
    ffn_pair = swap(jnp.concatenate([ffn_own, ffn4]), "ctx", 2)
    n0 = swap(after(add(dn[2], g3), n4), "ctx", 2)
    mine, shared = after((mine, shared), g5, n4)
    low_half, high_half = jnp.where(high, shared, mine), jnp.where(high, mine, shared)
    p = [jnp.stack([low_half[r], high_half[r]]) for r in range(4)]
    a = swap(p[3], "ctx", 1)
    b = swap(after(p[1], g1), "ctx", 1)
    near = swap(add(p[2], a), "ctx", 2)
    ffn1 = swap(after(ffn_own, a), "ctx", 1)
    half = after(add(p[0], b, near), ffn_pair)
    ffn5 = swap(after(ffn4, b), "ctx", 1)
    own = add(half[0], swap(half[1], "ctx", 4))[None]
    ffn_others = swap(after(ffn_pair, near, ffn1), "ctx", 1)
    own4 = swap(own, "ctx", 4)
    own1 = swap(after(own, ffn5), "ctx", 1)
    pair = swap(jnp.concatenate([own, own4]), "ctx", 2)
    own5 = swap(own4, "ctx", 1)
    others = swap(after(pair, ffn_others, own5), "ctx", 1)
    far = swap(after(add(dn[4], g5, n4), own4), "ctx", 4)
    return (
        (dn[0], g1, n0, far),
        [ffn_own, ffn1, ffn_pair, ffn_others, ffn4, ffn5],
        [own, own1, pair, others, own4, own5],
    )


def line_gather(x, x1, early, late):
    line = lax.axis_index("ctx") // 2
    up1, down1 = hop(x, [(0, 1), (1, 2), (2, 3)]), hop(x, [(3, 2), (2, 1), (1, 0)])
    z1 = jnp.where(line % 2 == 0, down1, up1)
    z1, up1, down1 = after((z1, up1, down1), x1)
    x3 = swap(z1, "ctx", 1)
    up2, down2 = hop(up1, [(1, 2), (2, 3)]), hop(down1, [(2, 1), (1, 0)])
    z2 = jnp.where(line < 2, down2, up2)
    z2, up2, down2 = after((z2, up2, down2), x3, early)
    x5 = swap(z2, "ctx", 1)
    far = hop(jnp.where(line == 2, up2, down2), [(2, 3), (1, 0)])
    z3 = jnp.where(line == 1, down1, jnp.where(line == 2, up1, far))
    return [x, x1, z1, x3, z2, x5, z3, swap(after(z3, x5, late), "ctx", 1)], (far, x5)


def on_device(
    tokens,
    lengths,
    span_order,
    w_query,
    w_key,
    w_value,
    w_out,
    w_in,
    w_ffn_out,
    gain_attn,
    gain_ffn,
    rel_table,
    cotangent,
):
    n_ctx, n_fsdp = lax.axis_size("ctx"), lax.axis_size("fsdp")
    fast = n_ctx == 8 and n_fsdp == 4
    place = lax.axis_index("ctx").astype(jnp.int32)
    shard = lax.axis_index("fsdp").astype(jnp.int32)
    local_rows = tokens.shape[1]
    own_rows = w_query.shape[0]
    bf, f32 = jnp.bfloat16, jnp.float32
    x, cot = tokens[0], cotangent[0]
    width = w_ffn_out.shape[0]
    high = rel_table.shape[0]
    spread = jnp.zeros((16, 4 * D), bf)
    spread = lax.dynamic_update_slice(spread, gain_attn[None], (0, shard * own_rows))
    spread = lax.dynamic_update_slice(spread, gain_ffn[None], (1, shard * own_rows))
    spread = lax.dynamic_update_slice(spread, rel_table.T, (0, D + shard * high))
    weights = jnp.concatenate([jnp.concatenate([w_query, w_key, w_value, w_out], axis=1), spread], axis=0)[None]
    (weights,) = lax.optimization_barrier((weights,))

    if fast:
        ids = jnp.stack([place, place, shard, shard, shard])
        order = [shard ^ r for r in range(4)]
        tokens_got = swap(x, "ctx", 1)
        w2 = swap(weights, "fsdp", 2)
        w1 = swap(after(weights, tokens_got), "fsdp", 1)
        columns = [block(w_in, order[r], 4, 1) for r in range(4)]
        columns = [columns[0], columns[2], jnp.stack([columns[1], columns[3]])]
        gathered, fifth = line_gather(x, tokens_got, w1, columns)
        xs = [p[None] for p in gathered]
        w3 = swap(after(w2, gathered[7]), "fsdp", 1)
        ws = [weights, w1, w2, w3]
        cot_late = after(cot, *fifth)
        side = swap(after(columns[2], *fifth), "fsdp", 1)
        win2 = swap(after(jnp.stack([columns[1], side[1]]), w2), "fsdp", 2)
        wins = [columns[0][None], side[:1], win2]
        cot1 = swap(after(cot, *fifth), "fsdp", 1)
        cot2 = swap(after(cot_late, w2), "fsdp", 2)
        cots = [p[None] for p in (cot, cot1, cot2, swap(cot2, "fsdp", 1))]
    else:
        ids = jnp.stack([place, jnp.int32(0), jnp.int32(0), jnp.int32(0), shard])
        xs = [lax.all_gather(x, "ctx", axis=0)]
        ws = [lax.all_gather(weights[0], "fsdp", axis=0)]
        parts = jnp.stack([w_in[:, i * width : (i + 1) * width] for i in range(n_fsdp)])
        wins = [lax.all_to_all(parts, "fsdp", 0, 0)]
        cots = [lax.all_gather(cot, "fsdp", axis=0)]

    nf, res, o, ot, lse, q, table, gains, k, v = forward(ids, span_order, lengths, xs, ws, local_rows)

    if fast:
        nfs = [nf[None], swap(nf, "fsdp", 1)[None], swap(nf, "fsdp", 2)[None]]
        halves = [ffn(ids, nfs[:2], cots[:2], wins, w_ffn_out)]
        nfs.append(swap(after(nfs[2], halves[0][0]), "fsdp", 1))
        halves.append(ffn(ids, nfs[2:], cots[2:], wins, w_ffn_out))
    else:
        nfs = [lax.all_gather(nf, "fsdp", axis=0)]
        halves = [ffn(ids, nfs, cots, wins, w_ffn_out)]
    acts, dups = [h[0] for h in halves], [h[1] for h in halves]
    dns, outs = [d for h in halves for d in h[2]], [d for h in halves for d in h[3]]
    if fast:
        first, third = swap(dns[1][0], "fsdp", 1), swap(dns[3][0], "fsdp", 1)
        far = add(dns[2][0], third)
        c = swap(far, "fsdp", 2)
        dnf = [dns[0][0], first, c]
        ffn_parts = ffn_grads(ids, nfs, cots, after(acts, far), dups, n_fsdp, 8)
        dnf = after(dnf, *ffn_parts)
        ffn_got = lax.all_to_all(after(ffn_parts[0], c), "ctx", 0, 0)
    else:
        dnf = [lax.psum_scatter(dns[0], "fsdp", scatter_dimension=0)]
        grad_ffn_out, grad_in = ffn_grads(ids, nfs, cots, acts, dups, n_fsdp, 1)
        grad_in = jnp.transpose(lax.all_to_all(grad_in, "fsdp", 0, 0), (1, 0, 2)).reshape(own_rows, n_fsdp * width)
        grad_ffn_out, grad_in = (lax.psum(g, "ctx").astype(f32) for g in (grad_ffn_out, grad_in))
    if fast:
        *out_terms, out_far = scatter_four([p[0] for p in outs])
        dnf = after(dnf, out_terms[1], out_far)
    else:
        out_terms = [lax.psum_scatter(outs[0], "fsdp", scatter_dimension=0)]

    *got, dres, dn_own = backward(
        ids, span_order, lengths, table, gains, dnf, res, cot, o, ot, lse, q, k, v, xs, ws,
        8 if fast else 1, n_fsdp,
    )
    if fast:
        got = after(got, ffn_got, *out_terms)
        dn, mine, shared = got[:8], got[8:10], got[10:12]
        ffn_own = jnp.sum(ffn_got.astype(f32), axis=0).astype(bf)
        terms, ffn_all, grads = tail(dn, mine, shared, ffn_own, place >= 4)
        d_normed = dn_own
        for term in terms:
            d_normed = d_normed + term.astype(f32)
        grad_ffn_out, grad_in = finish_ffn(ids, ffn_all, TURNS)
    else:
        d_normed = dn_own + lax.psum_scatter(got[0].reshape(n_ctx, local_rows, D), "ctx", scatter_dimension=0).astype(f32)
        grads = [lax.psum(lax.psum_scatter(g, "fsdp", scatter_dimension=0), "ctx") for g in got[1:]]
    g_query, g_out, g_key, g_value, g_attn, g_ffn, g_table = finish(
        ids, grads, TURNS if fast else ((0,), (1,)), rel_table.shape[0]
    )

    output = res
    for term in out_terms:
        output = output + term.astype(f32)
    output = output.astype(bf)
    xf = x.astype(f32)
    inv_rms = lax.rsqrt(jnp.mean(xf * xf, axis=1, keepdims=True) + EPS)
    scaled = d_normed * gains[0:1]
    inner = jnp.mean(scaled * xf, axis=1, keepdims=True)
    grad_tokens = (dres + inv_rms * scaled - xf * (inv_rms * inv_rms * inv_rms * inner)).astype(bf)
    return (
        output[None],
        grad_tokens[None],
        g_query,
        g_key,
        g_value,
        g_out,
        grad_in,
        grad_ffn_out,
        g_attn[0],
        g_ffn[0],
        g_table,
    )


def solution(mesh):
    rows, vector, whole = P("fsdp", None), P("fsdp"), P("fsdp", "ctx", None)
    return jax.shard_map(
        on_device,
        mesh=mesh,
        in_specs=(whole,) + (rows,) * 8 + (vector, vector, rows, whole),
        out_specs=(whole, whole) + (rows,) * 6 + (vector, vector, rows),
        check_vma=False,
    )
```

```python
import jax
import jax.numpy as jnp
from jax import lax
from jax.experimental import pallas as pl
from jax.experimental.pallas import tpu as pltpu
from jax.sharding import PartitionSpec as P

D = 768
H = 12
DH = 64
NB = 32
SPAN = 128
PAIRS = H // 2
BIG = 1e30
VMEM_LIMIT = 56 * 2**20
EPS = 1e-06
GELU_C = 0.7978845608028654
ANY = pl.ANY


def bucket_of(relative):
    distance = jnp.abs(relative)
    far_steps = jnp.zeros_like(distance)
    for exponent in range(1, 8):
        far_steps = far_steps + (distance * distance >= 64 * 2**exponent).astype(jnp.int32)
    magnitude = jnp.where(distance < 8, distance, 8 + far_steps)
    return magnitude + jnp.where(relative > 0, 16, 0).astype(jnp.int32)


def dot(a, b, ca=1, cb=0):
    return lax.dot_general(a, b, (((ca,), (cb,)), ((), ())), preferred_element_type=jnp.float32)


def diagonal_onehot(offset):
    lane = lax.broadcasted_iota(jnp.int32, (128, 256), 1)
    row = lax.broadcasted_iota(jnp.int32, (128, 256), 0)
    return (bucket_of(offset * SPAN + 127 - lane) == row).astype(jnp.bfloat16)


def fill_inverse(order_ref, inv_ref, spans):
    def put(i, carry):
        inv_ref[order_ref[0, i]] = i
        return carry

    lax.fori_loop(0, spans, put, 0)


def fill_near_bias(table_t, near_ref):
    for index in range(3):
        rows = dot(table_t, diagonal_onehot(index - 1))
        for head in range(H):
            wide = jnp.broadcast_to(rows[head : head + 1, :], (128, 256))
            tile = pltpu.roll(wide, 129, 1, stride=1, stride_axis=0)[:, :128]
            near_ref[index, head // 2, :, (head % 2) * 128 : (head % 2) * 128 + 128] = tile
    near_ref[3] = jnp.zeros_like(near_ref[3])


def key_range(span, b1, b2, b3, total):
    first, last = span * SPAN, span * SPAN + SPAN - 1
    start = jnp.where(first >= b3, b3, jnp.where(first >= b2, b2, jnp.where(first >= b1, b1, 0)))
    end = jnp.where(last < b1, b1, jnp.where(last < b2, b2, jnp.where(last < b3, b3, total)))
    return start // 256, (end + 255) // 256


def key_features(chunk, span, b1, b2, b3):
    lane = lax.broadcasted_iota(jnp.int32, (256, 128), 1)
    pos = lax.broadcasted_iota(jnp.int32, (256, 128), 0) + chunk * 256
    seg = (pos >= b1).astype(jnp.int32) + (pos >= b2).astype(jnp.int32) + (pos >= b3).astype(jnp.int32)
    code = jnp.where(pos < (span - 1) * SPAN, 4, jnp.where(pos >= (span + 2) * SPAN, 5, seg))
    hot = (lane == seg) | (lane == code) | ((lane >= 6) & (lane < 9))
    return jnp.where(hot, 1.0, 0.0).astype(jnp.bfloat16)


def query_features(span, pair, tab_ref, b1, b2, b3, extra=None):
    row = lax.broadcasted_iota(jnp.int32, (128, 256), 0)
    lane = lax.broadcasted_iota(jnp.int32, (128, 256), 1)
    pos = (lane % SPAN) + span * SPAN
    seg = (pos >= b1).astype(jnp.int32) + (pos >= b2).astype(jnp.int32) + (pos >= b3).astype(jnp.int32)
    first = lane < 128
    far = [
        jnp.where(
            first,
            jnp.broadcast_to(tab_ref[2 * pair : 2 * pair + 1, b : b + 1], (128, 256)),
            jnp.broadcast_to(tab_ref[2 * pair + 1 : 2 * pair + 2, b : b + 1], (128, 256)),
        )
        for b in (NB // 2 - 1, NB - 1)
    ]
    feat = jnp.where((row < 4) & (row != seg), -BIG, 0.0)
    feat = jnp.where(row == 4, far[0], jnp.where(row == 5, far[1], feat))
    if extra is not None:
        high = extra.astype(jnp.bfloat16).astype(jnp.float32)
        rest = extra - high
        mid = rest.astype(jnp.bfloat16).astype(jnp.float32)
        low = rest - mid
        feat = jnp.where(row == 6, high, jnp.where(row == 7, mid, jnp.where(row == 8, low, feat)))
    return feat.astype(jnp.bfloat16)


def block_diagonal(x_t):
    row = lax.broadcasted_iota(jnp.int32, (128, 128), 0)
    zero = jnp.zeros_like(x_t)
    return jnp.concatenate([jnp.where(row < DH, x_t, zero), jnp.where(row >= DH, x_t, zero)], axis=1)


def stacked_heads(x):
    lane = lax.broadcasted_iota(jnp.int32, (128, 128), 1)
    zero = jnp.zeros_like(x)
    return jnp.concatenate([jnp.where(lane < DH, x, zero), jnp.where(lane >= DH, x, zero)], axis=0)


def near_index(delta):
    return jnp.where((delta >= -1) & (delta <= 1), delta + 1, 3)


def smem():
    return pl.BlockSpec(memory_space=pltpu.SMEM)


def vmem():
    return pl.BlockSpec(memory_space=pltpu.VMEM)


def once():
    return pl.BlockSpec(memory_space=pltpu.VMEM, pipeline_mode=pl.Buffered(1))


def by_chunk():
    return pl.BlockSpec((256, D), lambda t: (t, 0))


def hbm():
    return pl.BlockSpec(memory_space=ANY)


def cost(us):
    return pl.CostEstimate(flops=int(us * 1.0e9), bytes_accessed=int(us * 1.0e6), transcendentals=0)


def load_pieces(pieces, target_ref, flip, sem, first=0, columns=None):
    copies = []
    rows = target_ref.shape[0] // len(pieces)
    for number, (ref, index, place) in enumerate(pieces):
        start = pl.multiple_of(lax.bitwise_xor(jnp.int32(place), flip) * rows, 16)
        source, target = ref.at[index, pl.ds(0, rows)], target_ref.at[pl.ds(start, rows)]
        if columns is not None:
            source, target = ref.at[index, pl.ds(0, rows), columns], target_ref.at[pl.ds(start, rows), columns]
        copies.append(pltpu.make_async_copy(source, target, sem.at[first + number]))
    for copy in copies:
        copy.start()
    return copies


def expand(refs):
    out, place = [], 0
    for ref in refs:
        for index in range(ref.shape[0]):
            out.append((ref, index, place))
            place += 1
    return out


def forward_kernel(counts, *refs):
    n_x, n_w = counts
    ids_ref, order_ref, len_ref = refs[:3]
    refs = refs[3:]
    x_refs, w_refs = refs[:n_x], refs[n_x : n_x + n_w]
    (
        nf_ref, res_ref, o_ref, ot_ref, lse_ref, q_ref, tab_ref, gain_ref, k_out_ref, v_out_ref,
        small_ref, inv_ref, x_ref, w_ref, k_ref, v_ref, rhs_ref, near_ref, m_ref, l_ref, acc_ref, sem_x, sem_w, sem_k, sem_v, sem_s,
    ) = refs[n_x + n_w :]
    spans, own = order_ref.shape[1], q_ref.shape[0] // SPAN
    b1 = len_ref[0, 0]
    b2 = b1 + len_ref[0, 1]
    b3 = b2 + len_ref[0, 2]
    copies = load_pieces(expand(x_refs), x_ref, jnp.int32(0), sem_x)
    pieces = expand(w_refs)
    copies += load_pieces(pieces, w_ref, ids_ref[2], sem_w, 0, pl.ds(D, 2 * D))
    late = load_pieces(pieces, w_ref, ids_ref[2], sem_w, len(pieces), pl.ds(0, D))
    late += load_pieces(pieces, w_ref, ids_ref[2], sem_w, 2 * len(pieces), pl.ds(3 * D, D))
    small_copies = []
    for number, (ref, index, _) in enumerate(expand(w_refs)):
        source = ref.at[index, pl.ds(ref.shape[1] - 16, 16)]
        small_copies.append(pltpu.make_async_copy(source, small_ref.at[number], sem_s.at[number]))
    for copy in small_copies:
        copy.start()
    fill_inverse(order_ref, inv_ref, spans)
    for copy in small_copies:
        copy.wait()
    small = small_ref[0, :, 0 : D + 128].astype(jnp.float32)
    for number in range(1, len(small_copies)):
        small = small + small_ref[number, :, 0 : D + 128].astype(jnp.float32)
    gain_ref[...] = small[0:8, 0:D]
    tab_ref[...] = small[:, D : D + 128]
    fill_near_bias(tab_ref[...].astype(jnp.bfloat16), near_ref)
    for copy in copies:
        copy.wait()
    own_rows = own * SPAN
    gain = gain_ref[0:1, :]

    def normed(x):
        x = x.astype(jnp.float32)
        return (x * lax.rsqrt(jnp.mean(x * x, axis=1, keepdims=True) + EPS) * gain).astype(jnp.bfloat16)

    my_spans = [order_ref[0, ids_ref[0] * own + i] for i in range(own)]
    my_ranges = [key_range(span, b1, b2, b3, spans * SPAN) for span in my_spans]

    def chunk_copies(t):
        rows = pl.ds(pl.multiple_of(t * 256, 256), 256)
        return (
            pltpu.make_async_copy(k_ref.at[rows], k_out_ref.at[rows], sem_k.at[t]),
            pltpu.make_async_copy(v_ref.at[rows], v_out_ref.at[rows], sem_v.at[t]),
        )

    def if_needed(t, body):
        needed = jnp.bool_(False)
        for low, high in my_ranges:
            needed = needed | ((t >= low) & (t < high))
        pl.when(needed)(body)

    def project(t, carry):
        def fill():
            rows = pl.ds(pl.multiple_of(t * 256, 256), 256)
            parts = []
            for half in range(2):
                slot = inv_ref[2 * t + half]
                piece = lax.bitwise_xor(slot // own, ids_ref[1])
                start = pl.multiple_of(piece * own_rows + (slot % own) * SPAN, SPAN)
                parts.append(x_ref[pl.ds(start, SPAN), :])
            xn = normed(jnp.concatenate(parts, axis=0))
            k_ref[rows, :] = dot(xn, w_ref[:, D : 2 * D]).astype(jnp.bfloat16)
            v_ref[rows, :] = dot(xn, w_ref[:, 2 * D : 3 * D]).astype(jnp.bfloat16)
            for copy in chunk_copies(t):
                copy.start()

        if_needed(t, fill)
        return carry

    lax.fori_loop(0, spans // 2, project, 0)
    mine = pl.multiple_of(lax.bitwise_xor(ids_ref[0], ids_ref[1]) * own_rows, SPAN)
    x_own = x_ref[pl.ds(mine, own_rows), :]
    for copy in late:
        copy.wait()
    q_ref[...] = dot(normed(x_own), w_ref[:, 0:D]).astype(jnp.bfloat16)

    def one_span(i, carry):
        span = order_ref[0, ids_ref[0] * own + i]
        low, high = key_range(span, b1, b2, b3, spans * SPAN)
        my_rows = pl.ds(pl.multiple_of(i * SPAN, SPAN), SPAN)
        for p in range(PAIRS):
            q_t = q_ref[my_rows, p * 128 : p * 128 + 128].T
            rhs_ref[p, 0:128, :] = block_diagonal(q_t)
            rhs_ref[p, 128:256, :] = query_features(span, p, tab_ref, b1, b2, b3)
        m_ref[...] = jnp.full_like(m_ref, -BIG)
        l_ref[...] = jnp.zeros_like(l_ref)
        acc_ref[...] = jnp.zeros_like(acc_ref)

        def chunk_body(t, near):
            rows = pl.ds(pl.multiple_of(t * 256, 256), 256)
            feat = key_features(t, span, b1, b2, b3)

            def scores(p):
                s = dot(jnp.concatenate([k_ref[rows, p * 128 : p * 128 + 128], feat], axis=1), rhs_ref[p])
                if near:
                    n0, n1 = near_index(2 * t - span), near_index(2 * t + 1 - span)
                    s = s + jnp.concatenate([near_ref[n0, p], near_ref[n1, p]], axis=0)
                return s

            def top(p, s):
                old = m_ref[p]
                new = jnp.maximum(old, jnp.max(s, axis=0, keepdims=True))
                m_ref[p] = new
                return new, jnp.exp(old - new)

            def weigh(p, s, new, scale):
                e = jnp.exp(s - new)
                l_ref[p] = l_ref[p] * scale + jnp.sum(e, axis=0, keepdims=True)
                return e.astype(jnp.bfloat16)

            def attend(p, e, scale):
                o = dot(v_ref[rows, p * 128 : p * 128 + 128], e, 0, 0)
                acc_ref[p, 0:64, :] = acc_ref[p, 0:64, :] * scale[:, 0:128] + o[0:64, 0:128]
                acc_ref[p, 64:128, :] = acc_ref[p, 64:128, :] * scale[:, 128:256] + o[64:128, 128:256]

            ss, tops, es = {}, {}, {}
            for p in range(PAIRS + 3):
                if p < PAIRS:
                    ss[p] = scores(p)
                if 1 <= p <= PAIRS:
                    tops[p - 1] = top(p - 1, ss[p - 1])
                if 2 <= p <= PAIRS + 1:
                    es[p - 2] = weigh(p - 2, ss[p - 2], *tops[p - 2])
                if p >= 3:
                    attend(p - 3, es[p - 3], tops[p - 3][1])

        def step(t, carry):
            near = (2 * t + 2 >= span) & (2 * t <= span + 1)
            pl.when(near)(lambda: chunk_body(t, True))
            pl.when(jnp.logical_not(near))(lambda: chunk_body(t, False))
            return carry

        lax.fori_loop(low, high, step, 0)
        for p in range(PAIRS):
            total = l_ref[p]
            lse_ref[i, p] = m_ref[p] + jnp.log(total)
            inv = 1.0 / total
            out = jnp.concatenate(
                [acc_ref[p, 0:64, :] * inv[:, 0:128], acc_ref[p, 64:128, :] * inv[:, 128:256]], axis=0
            )
            ot_ref[i, p] = out
            o_ref[my_rows, p * 128 : p * 128 + 128] = out.T.astype(jnp.bfloat16)
        return carry

    lax.fori_loop(0, own, one_span, 0)
    res = x_own.astype(jnp.float32) + dot(o_ref[...], w_ref[:, 3 * D : 4 * D])
    res_ref[...] = res
    inv_rms = lax.rsqrt(jnp.mean(res * res, axis=1, keepdims=True) + EPS)
    nf_ref[...] = (res * inv_rms * gain_ref[1:2, :]).astype(jnp.bfloat16)

    def settle(t, carry):
        def wait():
            for copy in chunk_copies(t):
                copy.wait()

        if_needed(t, wait)
        return carry

    lax.fori_loop(0, spans // 2, settle, 0)


def forward(ids, order, lengths, xs, ws, local_rows):
    spans, own = order.shape[1], local_rows // SPAN
    rows = spans * SPAN
    n_x, n_w = sum(x.shape[0] for x in xs), sum(w.shape[0] for w in ws)
    bf, f32 = jnp.bfloat16, jnp.float32
    return pl.pallas_call(
        lambda *refs: forward_kernel((len(xs), len(ws)), *refs),
        name="forward",
        cost_estimate=cost(22),
        out_shape=(
            jax.ShapeDtypeStruct((local_rows, D), bf),
            jax.ShapeDtypeStruct((local_rows, D), f32),
            jax.ShapeDtypeStruct((local_rows, D), bf),
            jax.ShapeDtypeStruct((own, PAIRS, 128, 128), f32),
            jax.ShapeDtypeStruct((own, PAIRS, 1, 256), f32),
            jax.ShapeDtypeStruct((local_rows, D), bf),
            jax.ShapeDtypeStruct((16, 128), f32),
            jax.ShapeDtypeStruct((8, D), f32),
            jax.ShapeDtypeStruct((rows, D), bf),
            jax.ShapeDtypeStruct((rows, D), bf),
        ),
        in_specs=[smem()] * 3 + [hbm()] * (len(xs) + len(ws)),
        out_specs=(vmem(),) * 8 + (hbm(),) * 2,
        scratch_shapes=[
            pltpu.VMEM((n_w, 16, 4 * D), bf),
            pltpu.SMEM((spans,), jnp.int32),
            pltpu.VMEM((rows, D), bf),
            pltpu.VMEM((D, 4 * D), bf),
            pltpu.VMEM((rows, D), bf),
            pltpu.VMEM((rows, D), bf),
            pltpu.VMEM((PAIRS, 256, 256), bf),
            pltpu.VMEM((4, PAIRS, 128, 256), f32),
            pltpu.VMEM((PAIRS, 1, 256), f32),
            pltpu.VMEM((PAIRS, 1, 256), f32),
            pltpu.VMEM((PAIRS, 128, 128), f32),
            pltpu.SemaphoreType.DMA((n_x,)),
            pltpu.SemaphoreType.DMA((3 * n_w,)),
            pltpu.SemaphoreType.DMA((spans // 2,)),
            pltpu.SemaphoreType.DMA((spans // 2,)),
            pltpu.SemaphoreType.DMA((n_w,)),
        ],
        compiler_params=pltpu.CompilerParams(vmem_limit_bytes=VMEM_LIMIT),
    )(ids, order, lengths, *xs, *ws)


def ffn_kernel(counts, *refs):
    count, n_w = counts
    ids_ref, refs = refs[0], refs[1:]
    nfs, cots, wins = refs[:count], refs[count : 2 * count], refs[2 * count : 2 * count + n_w]
    wffn_ref, act_ref, dup_ref = refs[2 * count + n_w : 2 * count + n_w + 3]
    refs = refs[2 * count + n_w + 3 :]
    dns, outs, (w_ref, sem) = refs[:count], refs[count : 2 * count], refs[2 * count :]
    done = 0
    for copy in load_pieces(expand(wins), w_ref, ids_ref[3], sem):
        copy.wait()
    for nf_ref, cot_ref, dn_ref, out_ref in zip(nfs, cots, dns, outs):
        for piece in range(nf_ref.shape[0]):
            up = dot(nf_ref[piece], w_ref[...])
            d_act = dot(cot_ref[piece], wffn_ref[...], 1, 1)
            square = up * up
            th = jnp.tanh(GELU_C * (up + 0.044715 * square * up))
            half = 0.5 * (1.0 + th)
            act = (up * half).astype(jnp.bfloat16)
            act_ref[done] = act
            slope = half + 0.5 * up * (1.0 - th * th) * (GELU_C * (1.0 + 3 * 0.044715 * square))
            d_up = (d_act * slope).astype(jnp.bfloat16)
            dup_ref[done] = d_up
            dn_ref[piece] = dot(d_up, w_ref[...], 1, 1).astype(jnp.bfloat16)
            out_ref[piece] = dot(act, wffn_ref[...]).astype(jnp.bfloat16)
            done += 1


def ffn(ids, nfs, cots, wins, wffn):
    total, rows, count = sum(n.shape[0] for n in nfs), nfs[0].shape[1], len(nfs)
    width = wffn.shape[0]
    bf = jnp.bfloat16
    act, dup, *rest = pl.pallas_call(
        lambda *refs: ffn_kernel((count, len(wins)), *refs),
        name="ffn",
        cost_estimate=cost(6),
        out_shape=(jax.ShapeDtypeStruct((total, rows, width), bf),) * 2
        + tuple(jax.ShapeDtypeStruct((n.shape[0], rows, D), bf) for n in nfs) * 2,
        in_specs=[smem()] + [vmem()] * (2 * count) + [hbm()] * len(wins) + [vmem()],
        out_specs=(vmem(),) * (2 + 2 * count),
        scratch_shapes=[
            pltpu.VMEM((D, width), bf),
            pltpu.SemaphoreType.DMA((sum(w.shape[0] for w in wins),)),
        ],
        compiler_params=pltpu.CompilerParams(vmem_limit_bytes=VMEM_LIMIT),
    )(ids, *nfs, *cots, *wins, wffn)
    return act, dup, rest[:count], rest[count:]


def by_turn(turn, refs, body):
    for number, ref in enumerate(refs):
        pl.when(turn == number)(lambda ref=ref: body(ref))


def ffn_grads_kernel(counts, parts, *refs):
    n, m = counts
    ids_ref = refs[0]
    groups, start = [], 1
    for count in (n, n, m, m):
        groups.append(refs[start : start + count])
        start += count
    nfs, cots, acts, dups = groups
    outs = refs[start:]

    def joined(pieces):
        flat = [ref[...].reshape(-1, ref.shape[2]) for ref in pieces]
        return flat[0] if len(flat) == 1 else jnp.concatenate(flat, axis=0)

    g_out = dot(joined(acts), joined(cots), 0, 0).astype(jnp.bfloat16)
    g_in = dot(joined(nfs), joined(dups), 0, 0).astype(jnp.bfloat16)
    if parts == 1:
        outs[0][...] = g_out
        size = outs[1].shape[1]
        for i in range(outs[1].shape[0]):
            outs[1][i] = g_in[i * size : (i + 1) * size]
        return
    out_ref, gin_ref = outs
    gin_ref[...] = g_in
    rows = D // parts
    for part in range(parts):
        out_ref[part, 0:rows, :] = g_out[part * rows : (part + 1) * rows]
        side = slice((part % 2) * 384, (part % 2) * 384 + 384)
        for place in range(4):
            owner = lax.bitwise_xor(jnp.int32(place), ids_ref[3])
            down = pl.ds(pl.multiple_of(owner * 192 + (part // 2) * 48, 16), 48)
            first, left = rows + (place // 2) * 48, (place % 2) * 384
            out_ref[part, first : first + 48, left : left + 384] = gin_ref[down, side]


def ffn_grads(ids, nfs, cots, acts, dups, n_fsdp, parts):
    width = acts[0].shape[2]
    bf = jnp.bfloat16
    if parts == 1:
        shapes = (jax.ShapeDtypeStruct((width, D), bf), jax.ShapeDtypeStruct((n_fsdp, D // n_fsdp, width), bf))
    else:
        shapes = (jax.ShapeDtypeStruct((parts, 2 * D // parts, D), bf),)
    scratch = [] if parts == 1 else [pltpu.VMEM((D, width), bf)]
    return pl.pallas_call(
        lambda *refs: ffn_grads_kernel((len(nfs), len(acts)), parts, *refs),
        name="ffn_grads",
        cost_estimate=cost(6),
        out_shape=shapes,
        in_specs=[smem()] + [vmem()] * (2 * len(nfs) + 2 * len(acts)),
        out_specs=(vmem(),) * len(shapes),
        scratch_shapes=scratch,
        compiler_params=pltpu.CompilerParams(vmem_limit_bytes=VMEM_LIMIT),
    )(ids, *nfs, *cots, *acts, *dups)


def fetch_turns(pieces, all_ref, flip, sem):
    copies = []
    for number, (ref, index, turn) in enumerate(pieces):
        place = lax.bitwise_xor(jnp.int32(turn), flip)
        copies.append(pltpu.make_async_copy(ref.at[index], all_ref.at[place], sem.at[number]))
    for copy in copies:
        copy.start()
    for copy in copies:
        copy.wait()


def with_turns(refs, turns):
    return [(ref, index, turn) for ref, group in zip(refs, turns) for index, turn in enumerate(group)]


def finish_ffn_kernel(turns, *refs):
    count = len(turns)
    ids_ref = refs[0]
    gout_ref, gin_ref, all_ref, sem = refs[1 + count :]
    fetch_turns(with_turns(refs[1 : 1 + count], turns), all_ref, ids_ref[1], sem)
    rows = all_ref.shape[1] // 2
    for p in range(all_ref.shape[0]):
        gout_ref[p * rows : (p + 1) * rows, :] = all_ref[p, 0:rows, :].astype(jnp.float32)
        for i in range(4):
            place = lax.bitwise_xor(jnp.int32(i), ids_ref[3])
            down = pl.ds(pl.multiple_of(rows + (place // 2) * 48, 16), 48)
            side = pl.ds(pl.multiple_of((place % 2) * 384, 128), 384)
            first = i * D + (p % 2) * 384
            gin_ref[(p // 2) * 48 : (p // 2) * 48 + 48, first : first + 384] = all_ref[p, down, side].astype(jnp.float32)


def finish_ffn(ids, arrays, turns):
    f32 = jnp.float32
    count = sum(a.shape[0] for a in arrays)
    return pl.pallas_call(
        lambda *refs: finish_ffn_kernel(turns, *refs),
        name="finish_ffn",
        cost_estimate=cost(4),
        out_shape=(jax.ShapeDtypeStruct((D, D), f32), jax.ShapeDtypeStruct((D // 4, 4 * D), f32)),
        in_specs=[smem()] + [hbm()] * len(arrays),
        out_specs=(vmem(),) * 2,
        scratch_shapes=[pltpu.VMEM((count, *arrays[0].shape[1:]), jnp.bfloat16), pltpu.SemaphoreType.DMA((count,))],
        compiler_params=pltpu.CompilerParams(vmem_limit_bytes=VMEM_LIMIT),
    )(ids, *arrays)


def put_grads(outs, all_ref, size, part_flip, fsdp_flip):
    n, parts, wide = sum(ref.shape[0] for ref in outs), outs[0].shape[1], outs[0].shape[3]
    for turn in range(n):
        owner = lax.bitwise_xor(jnp.int32(turn), fsdp_flip)
        rows = pl.ds(pl.multiple_of(owner * size, 16), size)
        for part in range(parts):
            source = lax.bitwise_xor(jnp.int32(part), part_flip)
            columns = pl.ds(pl.multiple_of(source * wide, 128), wide)
            outs[turn % len(outs)][turn // len(outs), part, 0:size, :] = all_ref[rows, columns].astype(jnp.bfloat16)


def grad_shapes(n, parts):
    high, wide = D // n + 16, 2 * D // parts
    if parts == 1:
        return (jax.ShapeDtypeStruct((n, parts, high, wide), jnp.bfloat16),)
    return (jax.ShapeDtypeStruct((n // 2, parts, high, wide), jnp.bfloat16),) * 2


def finish_kernel(turns, *refs):
    count = len(turns)
    ids_ref = refs[0]
    outs, (attn_ref, ffn_ref, table_ref, all_ref, row_ref, sem) = refs[1 + count : 5 + count], refs[5 + count :]
    fetch_turns(with_turns(refs[1 : 1 + count], turns), all_ref, ids_ref[1], sem)
    size, wide = outs[0].shape[0], all_ref.shape[2]
    step = min(D, wide)
    for first in range(0, 4 * D, step):
        outs[first // D][:, first % D : first % D + step] = all_ref[
            first // wide, 0:size, first % wide : first % wide + step
        ].astype(jnp.float32)

    def row(first):
        cuts = [all_ref[i // wide, size : size + 16, i % wide : i % wide + step] for i in range(first, first + D, step)]
        return jnp.concatenate(cuts, axis=1).astype(jnp.float32)[0:8]

    back = D - ids_ref[4] * size
    attn_ref[...] = pltpu.roll(row(0), back, 1)[0:1, 0:size]
    ffn_ref[...] = pltpu.roll(row(D), back, 1)[0:1, 0:size]
    table = all_ref[2 * D // wide, size : size + 16, 2 * D % wide : 2 * D % wide + 128].astype(jnp.float32)
    row_ref[...] = jnp.concatenate([table, jnp.zeros((112, 128), jnp.float32)], axis=0).T
    high = table_ref.shape[0]
    table_ref[...] = row_ref[pl.ds(ids_ref[4] * high, high), 0:H]


def finish(ids, arrays, turns, high):
    count, tall, wide = sum(a.shape[0] for a in arrays), *arrays[0].shape[1:]
    size, f32 = tall - 16, jnp.float32
    return pl.pallas_call(
        lambda *refs: finish_kernel(turns, *refs),
        name="finish",
        cost_estimate=cost(3),
        out_shape=(jax.ShapeDtypeStruct((size, D), f32),) * 4
        + (jax.ShapeDtypeStruct((1, size), f32),) * 2
        + (jax.ShapeDtypeStruct((high, H), f32),),
        in_specs=[smem()] + [hbm()] * len(arrays),
        out_specs=(vmem(),) * 7,
        scratch_shapes=[
            pltpu.VMEM((count, tall, wide), jnp.bfloat16),
            pltpu.VMEM((128, 128), f32),
            pltpu.SemaphoreType.DMA((count,)),
        ],
        compiler_params=pltpu.CompilerParams(vmem_limit_bytes=VMEM_LIMIT),
    )(ids, *arrays)


def backward_kernel(counts, *refs):
    n_x, n_w, n_dnf, n_dn, n_grad = counts
    (
        ids_ref, order_ref, len_ref, tab_ref, gain_ref,
        res_ref, cot_ref, o_ref, ot_ref, lse_ref, q_ref, k_ref, v_ref,
    ) = refs[:13]
    refs = refs[13:]
    x_refs, w_refs, dnf_refs = refs[:n_x], refs[n_x : n_x + n_w], refs[n_x + n_w : n_x + n_w + n_dnf]
    refs = refs[n_x + n_w + n_dnf :]
    dn_refs, mine_refs, shared_refs = refs[:n_dn], refs[n_dn : n_dn + n_grad], refs[n_dn + n_grad : n_dn + 2 * n_grad]
    (
        dres_ref, dn_own_ref,
        dlow_ref, dq_ref, dgain_ref, own_ref, all_ref, inv_ref, x_ref, w_ref, do_ref, rhs_ref, dorhs_ref, qbd_ref, dobd_ref, near_ref, nacc_ref, acc_ref, far_ref,
        dkacc_ref, dvacc_ref, kt_ref, sem_x, sem_w,
    ) = refs[n_dn + 2 * n_grad :]
    spans, own = order_ref.shape[1], q_ref.shape[0] // SPAN
    own_rows = own * SPAN
    b1 = len_ref[0, 0]
    b2 = b1 + len_ref[0, 1]
    b3 = b2 + len_ref[0, 2]
    t = pl.program_id(0)

    @pl.when(t == 0)
    def begin():
        copies_x = load_pieces(expand(x_refs), x_ref, jnp.int32(0), sem_x)
        copies_w = load_pieces(expand(w_refs), w_ref, ids_ref[2], sem_w)
        fill_inverse(order_ref, inv_ref, spans)
        fill_near_bias(tab_ref[...].astype(jnp.bfloat16), near_ref)
        nacc_ref[...] = jnp.zeros_like(nacc_ref)
        far_ref[...] = jnp.zeros_like(far_ref)

        res, dnf = res_ref[...], dnf_refs[0][...].astype(jnp.float32)
        for ref in dnf_refs[1:]:
            dnf = dnf + ref[...].astype(jnp.float32)
        inv_rms = lax.rsqrt(jnp.mean(res * res, axis=1, keepdims=True) + EPS)
        dgain_ref[...] = jnp.zeros_like(dgain_ref)
        dgain_ref[1:2, :] = jnp.sum(dnf * res * inv_rms, axis=0, keepdims=True)
        scaled = dnf * gain_ref[1:2, :]
        inner = jnp.mean(scaled * res, axis=1, keepdims=True)
        dres = cot_ref[...].astype(jnp.float32) + inv_rms * scaled - res * (inv_rms * inv_rms * inv_rms * inner)
        dres_ref[...] = dres
        dlow = dres.astype(jnp.bfloat16)
        dlow_ref[...] = dlow
        for copy in copies_w:
            copy.wait()
        do_ref[...] = dot(dlow, w_ref[:, 3 * D : 4 * D], 1, 1).astype(jnp.bfloat16)
        own_ref[:, D : 2 * D] = dot(o_ref[...], dlow, 0, 0)
        all_ref[...] = jnp.zeros_like(all_ref)

        def prepare(i, carry):
            span = order_ref[0, ids_ref[0] * own + i]
            my_rows = pl.ds(pl.multiple_of(i * SPAN, SPAN), SPAN)
            for p in range(PAIRS):
                cols = slice(p * 128, p * 128 + 128)
                qp, dop = q_ref[my_rows, cols], do_ref[my_rows, cols]
                do_t = dop.T
                prod = do_t.astype(jnp.float32) * ot_ref[i, p]
                neg = -jnp.concatenate(
                    [jnp.sum(prod[0:64], axis=0, keepdims=True), jnp.sum(prod[64:128], axis=0, keepdims=True)], axis=1
                )
                rhs_ref[i, p, 0:128, :] = block_diagonal(qp.T)
                rhs_ref[i, p, 128:256, :] = query_features(span, p, tab_ref, b1, b2, b3, -lse_ref[i, p])
                row = lax.broadcasted_iota(jnp.int32, (128, 256), 0)
                h1 = neg.astype(jnp.bfloat16).astype(jnp.float32)
                h2 = (neg - h1).astype(jnp.bfloat16).astype(jnp.float32)
                h3 = neg - h1 - h2
                dfeat = jnp.where(row == 6, h1, jnp.where(row == 7, h2, jnp.where(row == 8, h3, 0.0)))
                dorhs_ref[i, p, 0:128, :] = block_diagonal(do_t)
                dorhs_ref[i, p, 128:256, :] = dfeat.astype(jnp.bfloat16)
                qbd_ref[i, p] = stacked_heads(qp)
                dobd_ref[i, p] = stacked_heads(dop)
            return carry

        lax.fori_loop(0, own, prepare, 0)
        acc_ref[...] = jnp.zeros_like(acc_ref)
        for copy in copies_x:
            copy.wait()


    def unit(x):
        x = x.astype(jnp.float32)
        return x * lax.rsqrt(jnp.mean(x * x, axis=1, keepdims=True) + EPS)

    my_spans = [order_ref[0, ids_ref[0] * own + i] for i in range(own)]
    used = jnp.bool_(False)
    for span in my_spans:
        low, high = key_range(span, b1, b2, b3, spans * SPAN)
        used = used | ((t >= low) & (t < high))

    @pl.when(used)
    def ready():
        dkacc_ref[...] = jnp.zeros_like(dkacc_ref)
        dvacc_ref[...] = jnp.zeros_like(dvacc_ref)
        for p in range(PAIRS):
            kt_ref[p, 0:128, :] = k_ref[:, p * 128 : p * 128 + 128].T

    def span_body(i, span, near):
        feat = key_features(t, span, b1, b2, b3)
        for p in range(PAIRS):
            kt_ref[p, 128:144, :] = feat.T[0:16]

        def first(p):
            cols = slice(p * 128, p * 128 + 128)
            return (
                dot(jnp.concatenate([k_ref[:, cols], feat], axis=1), rhs_ref[i, p]),
                dot(jnp.concatenate([v_ref[:, cols], feat], axis=1), dorhs_ref[i, p]),
            )

        def last(p, prob, ds):
            cols = slice(p * 128, p * 128 + 128)
            dvacc_ref[:, cols] += dot(prob, dobd_ref[i, p])
            dkacc_ref[:, cols] += dot(ds, qbd_ref[i, p])
            dq = dot(kt_ref[p], ds)
            acc_ref[i, p, 0:64, :] += dq[0:64, 0:128]
            acc_ref[i, p, 64:128, :] += dq[64:128, 128:256]
            far_ref[p] += dq[128:136, :]

        ahead, waiting = first(0), None
        for p in range(PAIRS):
            s, dp = ahead
            if p + 1 < PAIRS:
                ahead = first(p + 1)
            if near:
                n0, n1 = near_index(2 * t - span), near_index(2 * t + 1 - span)
                s = s + jnp.concatenate([near_ref[n0, p], near_ref[n1, p]], axis=0)
            prob = jnp.exp(s)
            ds = prob * dp
            if near:
                nacc_ref[n0, p] += ds[0:128]
                nacc_ref[n1, p] += ds[128:256]
            if waiting is not None:
                last(*waiting)
            waiting = (p, prob.astype(jnp.bfloat16), ds.astype(jnp.bfloat16))
        last(*waiting)

    def one_span(i, carry):
        span = order_ref[0, ids_ref[0] * own + i]
        low, high = key_range(span, b1, b2, b3, spans * SPAN)
        needed = (t >= low) & (t < high)
        near = (2 * t + 2 >= span) & (2 * t <= span + 1)
        pl.when(needed & near)(lambda: span_body(i, span, True))
        pl.when(needed & jnp.logical_not(near))(lambda: span_body(i, span, False))
        return carry

    lax.fori_loop(0, own, one_span, 0)
    places, targets = [], []
    for half in range(2):
        slot = inv_ref[2 * t + half]
        piece = lax.bitwise_xor(slot // own, ids_ref[1])
        inside = (slot % own) * SPAN
        places.append(pl.ds(pl.multiple_of(piece * own_rows + inside, SPAN), SPAN))
        targets.append((piece, inside))

    def store(half, value):
        piece, inside = targets[half]

        def put(ref, index):
            ref[pl.ds(pl.multiple_of(index * own_rows + inside, SPAN), SPAN), :] = value

        if n_dn == 1:
            put(dn_refs[0], piece)
        else:
            by_turn(piece, dn_refs, lambda ref: put(ref, 0))

    def fill():
        dkb, dvb = dkacc_ref[...].astype(jnp.bfloat16), dvacc_ref[...].astype(jnp.bfloat16)
        part = dot(dkb, w_ref[:, D : 2 * D], 1, 1) + dot(dvb, w_ref[:, 2 * D : 3 * D], 1, 1)
        x = unit(jnp.concatenate([x_ref[places[0], :], x_ref[places[1], :]], axis=0))
        dgain_ref[0:1, :] += jnp.sum(part * x, axis=0, keepdims=True)
        turned = (x * gain_ref[0:1, :]).astype(jnp.bfloat16).T
        all_ref[:, 0:D] += dot(turned, dkb)
        all_ref[:, D : 2 * D] += dot(turned, dvb)
        part = part.astype(jnp.bfloat16)
        store(0, part[0:128])
        store(1, part[128:256])

    def skip():
        zero = jnp.zeros((256, D), jnp.bfloat16)
        store(0, zero[0:128])
        store(1, zero[0:128])

    pl.when(used)(fill)
    pl.when(jnp.logical_not(used))(skip)


    @pl.when(t == spans // 2 - 1)
    def finish():
        for i in range(own):
            for p in range(PAIRS):
                dq_ref[i * SPAN : (i + 1) * SPAN, p * 128 : p * 128 + 128] = acc_ref[i, p].T.astype(jnp.bfloat16)
        mine = pl.multiple_of(lax.bitwise_xor(ids_ref[0], ids_ref[1]) * own_rows, SPAN)
        own_part = dot(dq_ref[...], w_ref[:, 0:D], 1, 1)
        dn_own_ref[...] = own_part
        x_own = unit(x_ref[pl.ds(mine, own_rows), :])
        dgain_ref[0:1, :] += jnp.sum(own_part * x_own, axis=0, keepdims=True)
        own_ref[:, 0:D] = dot((x_own * gain_ref[0:1, :]).astype(jnp.bfloat16), dq_ref[...], 0, 0)
        parts, tall = mine_refs[0].shape[1:3]
        size, part_flip = tall - 16, ids_ref[1] & (parts - 1)
        put_grads(mine_refs, own_ref, size, part_flip, ids_ref[3])
        put_grads(shared_refs, all_ref, size, part_flip, ids_ref[3])

        row16 = lax.broadcasted_iota(jnp.int32, (16, 128), 0)
        lane16 = lax.broadcasted_iota(jnp.int32, (16, 128), 1)
        grad = jnp.zeros((16, 128), jnp.float32)
        for head in range(H):
            half = slice((head % 2) * 128, (head % 2) * 128 + 128)
            sums = jnp.sum(far_ref[head // 2, 4:6, half], axis=1, keepdims=True)
            grad = grad + jnp.where((row16 == head) & (lane16 == NB // 2 - 1), sums[0:1], 0.0)
            grad = grad + jnp.where((row16 == head) & (lane16 == NB - 1), sums[1:2], 0.0)
        rowd = lax.broadcasted_iota(jnp.int32, (16, 256), 0)
        flip_row = lax.broadcasted_iota(jnp.int32, (128, 128), 0)
        flip_lane = lax.broadcasted_iota(jnp.int32, (128, 128), 1)
        flip = (flip_row + flip_lane == 127).astype(jnp.bfloat16)
        for index in range(3):
            sums = jnp.zeros((16, 256), jnp.float32)
            for p in range(PAIRS):
                both = nacc_ref[index, p]
                high = both.astype(jnp.bfloat16)
                rest = (both - high.astype(jnp.float32)).astype(jnp.bfloat16)
                turned = dot(flip, high) + dot(flip, rest)
                for side in range(2):
                    tile = turned[:, side * 128 : side * 128 + 128]
                    wide = jnp.concatenate([tile, jnp.zeros_like(tile)], axis=1)
                    shifted = pltpu.roll(wide, 0, 1, stride=1, stride_axis=0)
                    sums = sums + jnp.where(rowd == 2 * p + side, jnp.sum(shifted, axis=0, keepdims=True), 0.0)
            hot = diagonal_onehot(index - 1).astype(jnp.float32)
            grad = grad + lax.dot_general(
                sums, hot, (((1,), (1,)), ((), ())), preferred_element_type=jnp.float32, precision=lax.Precision.HIGHEST
            )
        wide = mine_refs[0].shape[3]
        own_ref[0:1, 0:D] = dgain_ref[0:1, :]
        own_ref[0:1, D : 2 * D] = dgain_ref[1:2, :]
        own_ref[1:16, :] = jnp.zeros((15, 2 * D), jnp.float32)
        own_ref[16:32, :] = jnp.concatenate([grad, jnp.zeros((16, 2 * D - 128), jnp.float32)], axis=1)
        for refs, top in ((mine_refs, 0), (shared_refs, 16)):
            for part in range(parts):
                columns = pl.ds(pl.multiple_of(lax.bitwise_xor(jnp.int32(part), part_flip) * wide, 128), wide)
                value = own_ref[top : top + 16, columns].astype(jnp.bfloat16)
                for ref in refs:
                    for index in range(ref.shape[0]):
                        ref[index, part, size:tall, :] = value


def backward(ids, order, lengths, table, gains, dnf, res, cot, o, ot, lse, q, k, v, xs, ws, n_dn, n_fsdp):
    spans, local_rows = order.shape[1], q.shape[0]
    rows, own = spans * SPAN, local_rows // SPAN
    n_x, n_w = sum(x.shape[0] for x in xs), sum(w.shape[0] for w in ws)
    bf, f32 = jnp.bfloat16, jnp.float32
    shapes = grad_shapes(n_fsdp, 1 if n_dn == 1 else 4)
    return pl.pallas_call(
        lambda *refs: backward_kernel((len(xs), len(ws), len(dnf), n_dn, len(shapes)), *refs),
        name="backward",
        cost_estimate=cost(36),
        grid=(spans // 2,),
        out_shape=(jax.ShapeDtypeStruct((rows // n_dn, D), bf),) * n_dn
        + shapes * 2
        + (jax.ShapeDtypeStruct((local_rows, D), f32),) * 2,
        in_specs=[smem()] * 3 + [once()] * 8 + [by_chunk()] * 2 + [hbm()] * (len(xs) + len(ws)) + [once()] * len(dnf),
        out_specs=(once(),) * (n_dn + 2 * len(shapes) + 2),
        scratch_shapes=[
            pltpu.VMEM((local_rows, D), bf),
            pltpu.VMEM((local_rows, D), bf),
            pltpu.VMEM((8, D), f32),
            pltpu.VMEM((D, 2 * D), f32),
            pltpu.VMEM((D, 2 * D), f32),
            pltpu.SMEM((spans,), jnp.int32),
            pltpu.VMEM((rows, D), bf),
            pltpu.VMEM((D, 4 * D), bf),
            pltpu.VMEM((local_rows, D), bf),
            pltpu.VMEM((own, PAIRS, 256, 256), bf),
            pltpu.VMEM((own, PAIRS, 256, 256), bf),
            pltpu.VMEM((own, PAIRS, 256, 128), bf),
            pltpu.VMEM((own, PAIRS, 256, 128), bf),
            pltpu.VMEM((4, PAIRS, 128, 256), f32),
            pltpu.VMEM((4, PAIRS, 128, 256), f32),
            pltpu.VMEM((own, PAIRS, 128, 128), f32),
            pltpu.VMEM((PAIRS, 8, 256), f32),
            pltpu.VMEM((256, D), f32),
            pltpu.VMEM((256, D), f32),
            pltpu.VMEM((PAIRS, 144, 256), bf),
            pltpu.SemaphoreType.DMA((n_x,)),
            pltpu.SemaphoreType.DMA((n_w,)),
        ],
        compiler_params=pltpu.CompilerParams(vmem_limit_bytes=VMEM_LIMIT),
    )(ids, order, lengths, table, gains, res, cot, o, ot, lse, q, k, v, *xs, *ws, *dnf)


def swap(x, axis, bit):
    count = lax.axis_size(axis)
    return lax.ppermute(x, axis, [(i, i ^ bit) for i in range(count)])


def hop(x, pairs):
    return lax.ppermute(x, "ctx", [(2 * a + i, 2 * b + i) for a, b in pairs for i in range(2)])


def block(x, index, count, dim=0):
    size = x.shape[dim] // count
    return lax.dynamic_slice_in_dim(x, index * size, size, dim)


def after(x, *others):
    return lax.optimization_barrier((x,) + others)[0]


def add(*terms):
    total = terms[0].astype(jnp.float32)
    for term in terms[1:]:
        total = total + term.astype(jnp.float32)
    return total.astype(jnp.bfloat16)


def gather_four(x):
    across = swap(x, "fsdp", 2)
    return [x, swap(x, "fsdp", 1), across, swap(across, "fsdp", 1)]


def scatter_four(pieces):
    first, third = swap(pieces[1], "fsdp", 1), swap(pieces[3], "fsdp", 1)
    far = add(pieces[2], third)
    return pieces[0], first, swap(far, "fsdp", 2), far


def scatter_pairs(keep, send):
    got = swap(send, "fsdp", 1)
    far = add(keep[1], got[1])
    return (keep[0], got[0], swap(far, "fsdp", 2)), far


TURNS = ((0,), (1,), (2, 6), (3, 7), (4,), (5,))


def tail(dn, mine, shared, ffn_own, high):
    g7, g3 = swap(dn[7], "ctx", 1), swap(dn[3], "ctx", 1)
    (mine, _), (shared, _) = scatter_pairs(*mine), scatter_pairs(*shared)
    top, blocks = ffn_own[: D // 8], ffn_own[D // 8 :]
    blocks = [blocks[48 * (r // 2) : 48 * (r // 2) + 48, 384 * (r % 2) : 384 * (r % 2) + 384] for r in range(4)]
    side = swap(jnp.stack([blocks[1], blocks[3]]), "fsdp", 1)
    across = swap(jnp.stack([blocks[2], side[1]]), "fsdp", 2)
    ffn_own = jnp.concatenate(
        [top, jnp.concatenate([blocks[0], side[0]], axis=1), jnp.concatenate([across[0], across[1]], axis=1)]
    )[None]
    ffn4 = swap(ffn_own, "ctx", 4)
    mine, shared = add(*mine), add(*shared)
    g5, g1 = swap(after(dn[5], g7), "ctx", 1), swap(after(dn[1], g3), "ctx", 1)
    n4 = swap(add(dn[6], g7), "ctx", 2)
    ffn_pair = swap(jnp.concatenate([ffn_own, ffn4]), "ctx", 2)
    n0 = swap(after(add(dn[2], g3), n4), "ctx", 2)
    mine, shared = after((mine, shared), g5, n4)
    low_half, high_half = jnp.where(high, shared, mine), jnp.where(high, mine, shared)
    p = [jnp.stack([low_half[r], high_half[r]]) for r in range(4)]
    a = swap(p[3], "ctx", 1)
    b = swap(after(p[1], g1), "ctx", 1)
    near = swap(add(p[2], a), "ctx", 2)
    ffn1 = swap(after(ffn_own, a), "ctx", 1)
    half = after(add(p[0], b, near), ffn_pair)
    ffn5 = swap(after(ffn4, b), "ctx", 1)
    own = add(half[0], swap(half[1], "ctx", 4))[None]
    ffn_others = swap(after(ffn_pair, near, ffn1), "ctx", 1)
    own4 = swap(own, "ctx", 4)
    own1 = swap(after(own, ffn5), "ctx", 1)
    pair = swap(jnp.concatenate([own, own4]), "ctx", 2)
    own5 = swap(own4, "ctx", 1)
    others = swap(after(pair, ffn_others, own5), "ctx", 1)
    far = swap(after(add(dn[4], g5, n4), own4), "ctx", 4)
    return (
        (dn[0], g1, n0, far),
        [ffn_own, ffn1, ffn_pair, ffn_others, ffn4, ffn5],
        [own, own1, pair, others, own4, own5],
    )


def line_gather(x, x1, early, late):
    line = lax.axis_index("ctx") // 2
    up1, down1 = hop(x, [(0, 1), (1, 2), (2, 3)]), hop(x, [(3, 2), (2, 1), (1, 0)])
    z1 = jnp.where(line % 2 == 0, down1, up1)
    z1, up1, down1 = after((z1, up1, down1), x1)
    x3 = swap(z1, "ctx", 1)
    up2, down2 = hop(up1, [(1, 2), (2, 3)]), hop(down1, [(2, 1), (1, 0)])
    z2 = jnp.where(line < 2, down2, up2)
    z2, up2, down2 = after((z2, up2, down2), x3, early)
    x5 = swap(z2, "ctx", 1)
    far = hop(jnp.where(line == 2, up2, down2), [(2, 3), (1, 0)])
    z3 = jnp.where(line == 1, down1, jnp.where(line == 2, up1, far))
    return [x, x1, z1, x3, z2, x5, z3, swap(after(z3, x5, late), "ctx", 1)], (far, x5)


def on_device(
    tokens,
    lengths,
    span_order,
    w_query,
    w_key,
    w_value,
    w_out,
    w_in,
    w_ffn_out,
    gain_attn,
    gain_ffn,
    rel_table,
    cotangent,
):
    n_ctx, n_fsdp = lax.axis_size("ctx"), lax.axis_size("fsdp")
    fast = n_ctx == 8 and n_fsdp == 4
    place = lax.axis_index("ctx").astype(jnp.int32)
    shard = lax.axis_index("fsdp").astype(jnp.int32)
    local_rows = tokens.shape[1]
    own_rows = w_query.shape[0]
    bf, f32 = jnp.bfloat16, jnp.float32
    x, cot = tokens[0], cotangent[0]
    width = w_ffn_out.shape[0]
    high = rel_table.shape[0]
    spread = jnp.zeros((16, 4 * D), bf)
    spread = lax.dynamic_update_slice(spread, gain_attn[None], (0, shard * own_rows))
    spread = lax.dynamic_update_slice(spread, gain_ffn[None], (1, shard * own_rows))
    spread = lax.dynamic_update_slice(spread, rel_table.T, (0, D + shard * high))
    weights = jnp.concatenate([jnp.concatenate([w_query, w_key, w_value, w_out], axis=1), spread], axis=0)[None]
    (weights,) = lax.optimization_barrier((weights,))

    if fast:
        ids = jnp.stack([place, place, shard, shard, shard])
        order = [shard ^ r for r in range(4)]
        tokens_got = swap(x, "ctx", 1)
        w2 = swap(weights, "fsdp", 2)
        w1 = swap(after(weights, tokens_got), "fsdp", 1)
        columns = [block(w_in, order[r], 4, 1) for r in range(4)]
        columns = [columns[0], columns[2], jnp.stack([columns[1], columns[3]])]
        gathered, fifth = line_gather(x, tokens_got, w1, columns)
        xs = [p[None] for p in gathered]
        w3 = swap(after(w2, gathered[7]), "fsdp", 1)
        ws = [weights, w1, w2, w3]
        cot_late = after(cot, *fifth)
        side = swap(after(columns[2], *fifth), "fsdp", 1)
        win2 = swap(after(jnp.stack([columns[1], side[1]]), w2), "fsdp", 2)
        wins = [columns[0][None], side[:1], win2]
        cot1 = swap(after(cot, *fifth), "fsdp", 1)
        cot2 = swap(after(cot_late, w2), "fsdp", 2)
        cots = [p[None] for p in (cot, cot1, cot2, swap(cot2, "fsdp", 1))]
    else:
        ids = jnp.stack([place, jnp.int32(0), jnp.int32(0), jnp.int32(0), shard])
        xs = [lax.all_gather(x, "ctx", axis=0)]
        ws = [lax.all_gather(weights[0], "fsdp", axis=0)]
        parts = jnp.stack([w_in[:, i * width : (i + 1) * width] for i in range(n_fsdp)])
        wins = [lax.all_to_all(parts, "fsdp", 0, 0)]
        cots = [lax.all_gather(cot, "fsdp", axis=0)]

    nf, res, o, ot, lse, q, table, gains, k, v = forward(ids, span_order, lengths, xs, ws, local_rows)

    if fast:
        nfs = [nf[None], swap(nf, "fsdp", 1)[None], swap(nf, "fsdp", 2)[None]]
        halves = [ffn(ids, nfs[:2], cots[:2], wins, w_ffn_out)]
        nfs.append(swap(after(nfs[2], halves[0][0]), "fsdp", 1))
        halves.append(ffn(ids, nfs[2:], cots[2:], wins, w_ffn_out))
    else:
        nfs = [lax.all_gather(nf, "fsdp", axis=0)]
        halves = [ffn(ids, nfs, cots, wins, w_ffn_out)]
    acts, dups = [h[0] for h in halves], [h[1] for h in halves]
    dns, outs = [d for h in halves for d in h[2]], [d for h in halves for d in h[3]]
    if fast:
        first, third = swap(dns[1][0], "fsdp", 1), swap(dns[3][0], "fsdp", 1)
        far = add(dns[2][0], third)
        c = swap(far, "fsdp", 2)
        dnf = [dns[0][0], first, c]
        ffn_parts = ffn_grads(ids, nfs, cots, after(acts, far), dups, n_fsdp, 8)
        dnf = after(dnf, *ffn_parts)
        ffn_got = lax.all_to_all(after(ffn_parts[0], c), "ctx", 0, 0)
    else:
        dnf = [lax.psum_scatter(dns[0], "fsdp", scatter_dimension=0)]
        grad_ffn_out, grad_in = ffn_grads(ids, nfs, cots, acts, dups, n_fsdp, 1)
        grad_in = jnp.transpose(lax.all_to_all(grad_in, "fsdp", 0, 0), (1, 0, 2)).reshape(own_rows, n_fsdp * width)
        grad_ffn_out, grad_in = (lax.psum(g, "ctx").astype(f32) for g in (grad_ffn_out, grad_in))
    if fast:
        *out_terms, out_far = scatter_four([p[0] for p in outs])
        dnf = after(dnf, out_terms[1], out_far)
    else:
        out_terms = [lax.psum_scatter(outs[0], "fsdp", scatter_dimension=0)]

    *got, dres, dn_own = backward(
        ids, span_order, lengths, table, gains, dnf, res, cot, o, ot, lse, q, k, v, xs, ws,
        8 if fast else 1, n_fsdp,
    )
    if fast:
        got = after(got, ffn_got, *out_terms)
        dn, mine, shared = got[:8], got[8:10], got[10:12]
        ffn_own = jnp.sum(ffn_got.astype(f32), axis=0).astype(bf)
        terms, ffn_all, grads = tail(dn, mine, shared, ffn_own, place >= 4)
        d_normed = dn_own
        for term in terms:
            d_normed = d_normed + term.astype(f32)
        grad_ffn_out, grad_in = finish_ffn(ids, ffn_all, TURNS)
    else:
        d_normed = dn_own + lax.psum_scatter(got[0].reshape(n_ctx, local_rows, D), "ctx", scatter_dimension=0).astype(f32)
        grads = [lax.psum(lax.psum_scatter(g, "fsdp", scatter_dimension=0), "ctx") for g in got[1:]]
    g_query, g_out, g_key, g_value, g_attn, g_ffn, g_table = finish(
        ids, grads, TURNS if fast else ((0,), (1,)), rel_table.shape[0]
    )

    output = res
    for term in out_terms:
        output = output + term.astype(f32)
    output = output.astype(bf)
    xf = x.astype(f32)
    inv_rms = lax.rsqrt(jnp.mean(xf * xf, axis=1, keepdims=True) + EPS)
    scaled = d_normed * gains[0:1]
    inner = jnp.mean(scaled * xf, axis=1, keepdims=True)
    grad_tokens = (dres + inv_rms * scaled - xf * (inv_rms * inv_rms * inv_rms * inner)).astype(bf)
    return (
        output[None],
        grad_tokens[None],
        g_query,
        g_key,
        g_value,
        g_out,
        grad_in,
        grad_ffn_out,
        g_attn[0],
        g_ffn[0],
        g_table,
    )


def solution(mesh):
    rows, vector, whole = P("fsdp", None), P("fsdp"), P("fsdp", "ctx", None)
    return jax.shard_map(
        on_device,
        mesh=mesh,
        in_specs=(whole,) + (rows,) * 8 + (vector, vector, rows, whole),
        out_specs=(whole, whole) + (rows,) * 6 + (vector, vector, rows),
        check_vma=False,
    )
```
